32 devices in a mesh: group: 2 (over x), ctx: 16 (over z, y, core).
Axes of the slice: x: 2, y: 2, z: 4, core: 2. Of those that a mesh axis runs over, the one named last changes fastest.
Arguments:
- query_rows: bfloat16 [4096, 4096], P(('group', 'ctx')), parts along dimension 0, may hold values from -6 to 6
- key_rows: bfloat16 [4096, 4096], P(('group', 'ctx')), parts along dimension 0, may hold values from -6 to 6
- value_rows: bfloat16 [4096, 4096], P(('group', 'ctx')), parts along dimension 0, may hold values from -6 to 6
- conv_taps: float32 [3, 3, 4096], replicated, may hold values from -3.5 to 3.5
- decay_rate: float32 [4096], replicated, may hold values from 0.0007324219 to 0.034
- lag_profile: float32 [2048], replicated, may hold values from -3.6681164 to 3.6681164
- skip_gain: float32 [4096], replicated, may hold values from 0.5 to 1.5
- pair_lists: int32 [32, 9, 2], P('group'), parts along dimension 0, may hold values from -1 to 15, as said below
Outputs:
- layer_out: bfloat16 [4096, 4096], P(('group', 'ctx')), parts along dimension 0
The draws below stay inside these ranges and needn't reach their ends.
There are 2 independent parts, one for each index of `group`. The reference program is written for one: setup_inputs(seed, part) draws one part's arguments, and reference() takes and returns one part's arrays. A program takes and returns all parts, laid end to end along the dimension named above; an argument that names none is the same for every part. Nothing has to cross between parts.
Inputs may be any that keep to these rules, and one draw needn't show every extreme that they name: `pair_lists`: row r lists the pairs that reader r handles. Every live pair (source span <= target span, both in the same document) appears exactly once over all rows, and no other pair appears. A reader's sources are r or 15 - r, its targets are distinct, and unused entries are (-1, -1) after the used ones; some reader's row is full. The sequence holds two documents, the second beginning at a span between 4 and 12.
All inputs are finite; a program needn't handle non-finite values.
Results may differ from the reference program's by a relative error of at most 0.0051.
Values may be sent and summed in bfloat16 or wider, within the bound.
A program may use at most 128 MiB of HBM per device.

```python
import jax
import jax.numpy as jnp
from jax import lax

D = 4096
TOK_DEV = 128
SEQ = 2048
SLOTS = 9
N_CTX = 16


def document_of(span_ids, border):
    return (span_ids >= border).astype(jnp.int32)


def draw_pair_lists(key, part):
    border = jax.random.randint(jax.random.fold_in(key, 7), (), N_CTX // 4, 3 * N_CTX // 4 + 1)
    half_count = N_CTX // 2
    readers = jnp.arange(N_CTX, dtype=jnp.int32)[:, None]
    targets = jnp.arange(N_CTX, dtype=jnp.int32)[None, :]
    lower = jnp.where(readers < half_count, readers, N_CTX - 1 - readers)
    upper = N_CTX - 1 - lower
    source = jnp.where((readers < half_count) & (targets >= half_count), upper, lower)
    reach_from = jnp.where(readers < half_count, jnp.where(targets < half_count, lower, upper), half_count)
    valid = (targets >= reach_from) & (document_of(source, border) == document_of(targets, border))
    scores = jnp.where(valid, targets, N_CTX + targets) + jnp.zeros((N_CTX, N_CTX), jnp.int32)
    order = jnp.argsort(scores, axis=1)
    chosen = order[:, :SLOTS].astype(jnp.int32)
    keep = jnp.take_along_axis(valid + jnp.zeros((N_CTX, N_CTX), bool), chosen, axis=1)
    source_full = source + jnp.zeros((N_CTX, N_CTX), jnp.int32)
    source_list = jnp.where(keep, jnp.take_along_axis(source_full, chosen, axis=1), -1)
    target_list = jnp.where(keep, chosen, -1)
    return jnp.stack([source_list, target_list], axis=-1).astype(jnp.int32)


def loguniform_between(key, lowest, highest):
    spread = jax.random.uniform(key, (D,), jnp.float32)
    return jnp.exp(jnp.log(lowest) + spread * (jnp.log(highest) - jnp.log(lowest)))


def draw_decay_rate(key, part):
    slow_share = 0.5
    band_share = 0.85
    slow_floor = 1.8
    picker = jax.random.uniform(jax.random.fold_in(key, 11), (D,), jnp.float32)
    slow_rates = loguniform_between(jax.random.fold_in(key, 12), slow_floor / SEQ, 2.3 / SEQ)
    band_rates = loguniform_between(jax.random.fold_in(key, 13), 2.7 / SEQ, 6.0 / SEQ)
    fast_rates = loguniform_between(jax.random.fold_in(key, 14), 0.02, 0.033)
    return jnp.where(picker < slow_share, slow_rates, jnp.where(picker < band_share, band_rates, fast_rates)).astype(jnp.float32)


def draw_lag_profile(key, part):
    fraction = jnp.arange(SEQ, dtype=jnp.float32) / SEQ
    values = jnp.clip(jax.random.normal(jax.random.fold_in(key, 21), (SEQ,), jnp.float32), -4.0, 4.0)
    envelope = 1.0 + 0.1 * jnp.exp(6.0 * fraction)
    return (values * envelope / jnp.sqrt(jnp.float32(SEQ))).astype(jnp.float32)


def levels(key, shape, shards, smallest, top_value):
    factor_of, own = 1.0, jax.random.fold_in(key, 6)
    for axis_at, blocks in shards:
        heights = jnp.exp(jax.random.uniform(jax.random.fold_in(own, axis_at), (blocks,), jnp.float32, smallest / len(shards), top_value / len(shards)))
        factor_of = factor_of * jnp.repeat(heights, shape[axis_at] // blocks).reshape([-1 if axis == axis_at else 1 for axis in range(len(shape))])
    return factor_of


def scatter_about(own_key, shape, scale, limit, cuts=(), kind=jnp.bfloat16):
    drawn = jax.random.normal(own_key, shape, jnp.float32) * scale
    if len(cuts) > 0:
        drawn = levels(own_key, shape, cuts, -0.22, 0.18) * drawn
    return jnp.clip(drawn, min=-limit, max=limit).astype(kind)


def setup_inputs(seed: int = 0, part: int = 0) -> dict:
    arg_keys = jax.random.split(jax.random.key(seed), 9)
    part_keys = jax.random.split(jax.random.fold_in(arg_keys[8], part), 9)
    query_rows = scatter_about(part_keys[0], (SEQ, D), 1.0, 6.0, ((0, 16),))
    key_rows = scatter_about(part_keys[1], (SEQ, D), 1.0, 6.0, ((0, 16),))
    value_rows = scatter_about(part_keys[2], (SEQ, D), 1.0, 6.0, ((0, 16),))
    conv_taps = scatter_about(arg_keys[3], (3, 3, D), 3 ** -0.5, 3.5, (), jnp.float32)
    decay_rate = draw_decay_rate(jax.random.fold_in(arg_keys[8], 71), part)
    lag_profile = draw_lag_profile(jax.random.fold_in(arg_keys[8], 71), part)
    skip_gain = jnp.clip(jax.random.uniform(arg_keys[6], (D,), jnp.float32, 0.5, 1.5), 0.5, 1.5)
    pair_lists = draw_pair_lists(jax.random.fold_in(jax.random.fold_in(arg_keys[8], part), 71), part)
    return {"query_rows": query_rows, "key_rows": key_rows, "value_rows": value_rows, "conv_taps": conv_taps, "decay_rate": decay_rate, "lag_profile": lag_profile, "skip_gain": skip_gain, "pair_lists": pair_lists}


def short_conv(rows_in, conv_taps):
    values = rows_in.astype(jnp.float32)
    length = values.shape[0]
    padded = jnp.concatenate([jnp.zeros((2, values.shape[1]), jnp.float32), values], axis=0)
    return conv_taps[0] * padded[2:] + conv_taps[1] * padded[1:length + 1] + conv_taps[2] * padded[:length]


def toeplitz_of(window, span_rows):
    reverse_win = window[::-1]
    extended = jnp.concatenate([reverse_win, jnp.zeros((1,), reverse_win.dtype)])
    tiled = jnp.tile(extended, span_rows + 1)
    start = span_rows - 1
    flat_part = tiled[start:start + span_rows * (2 * span_rows - 1)]
    return flat_part.reshape(span_rows, 2 * span_rows - 1)[:, :span_rows]


def block_term(source, span_gap, decay_rate, padded_lag, span_rows):
    gap_rows = (span_gap * span_rows).astype(jnp.int32)
    window = lax.dynamic_slice_in_dim(padded_lag, gap_rows + 1, 2 * span_rows - 1)
    toeplitz = toeplitz_of(window, span_rows)
    positions = jnp.arange(span_rows, dtype=jnp.float32)
    scaled = source.astype(jnp.float32) * jnp.exp(decay_rate[None, :] * positions[:, None])
    mixed = jnp.dot(toeplitz, scaled, precision=lax.Precision.HIGHEST, preferred_element_type=jnp.float32)
    distance = positions[:, None] + gap_rows.astype(jnp.float32)
    return (mixed * jnp.exp(-decay_rate[None, :] * distance)).astype(jnp.bfloat16)


def reference(query_rows, key_rows, value_rows, conv_taps, decay_rate, lag_profile, skip_gain, pair_lists):
    query_feat = short_conv(query_rows, conv_taps[0])
    key_feat = short_conv(key_rows, conv_taps[1])
    value_feat = short_conv(value_rows, conv_taps[2])
    gated = (key_feat * value_feat).astype(jnp.bfloat16)
    spans = gated.reshape(N_CTX, TOK_DEV, D)
    sources = pair_lists[:, :, 0].reshape(-1)
    targets = pair_lists[:, :, 1].reshape(-1)
    span_ids = jnp.arange(N_CTX, dtype=jnp.int32)
    live = jnp.any((sources[:, None, None] == span_ids[None, :, None]) & (targets[:, None, None] == span_ids[None, None, :]), axis=0)
    padded_lag = jnp.concatenate([jnp.zeros((TOK_DEV,), jnp.float32), lag_profile])

    def per_target(target):
        def add_source(anchor, running):
            def compute_block():
                return block_term(spans[anchor], target - anchor, decay_rate, padded_lag, TOK_DEV).astype(jnp.float32)

            def zero_block():
                return jnp.zeros((TOK_DEV, D), jnp.float32)

            return running + lax.cond(live[anchor, target], compute_block, zero_block)

        return lax.fori_loop(0, N_CTX, add_source, jnp.zeros((TOK_DEV, D), jnp.float32))

    long_conv = lax.map(per_target, span_ids).reshape(SEQ, D)
    return (query_feat * (long_conv + skip_gain[None, :] * gated.astype(jnp.float32))).astype(jnp.bfloat16)
```

```python
import functools

import jax
import jax.numpy as jnp
from jax import lax
from jax.experimental import pallas as pl
from jax.experimental.pallas import tpu as pltpu
from jax.sharding import PartitionSpec as P

MESH = pl.DeviceIdType.MESH
WIDTH = 128
STRIPS = 8


def kernel(
    n, rows, chunks, width,
    q_hbm, k_hbm, v_hbm, taps_hbm, decay_hbm, lag_hbm, skip_hbm, pairs_hbm,
    out_hbm,
    out_ref, q_ref, k_ref, v_ref, taps_ref, decay_ref, lag_ref, skip_ref, pairs_ref,
    edge, rim_out, rim_in, rim, gated, qfeat, spans, inbox, outbox, toep, mix_here, mix_next,
    scaled, grow, fade, result, landed,
    load_sem, store_sem, rim_send, rim_recv, send1, recv1, send_z, recv_z, send2, recv2, ready,
):
    me = lax.axis_index("ctx")
    members = n // 4
    quarter = me // members
    base = quarter * members
    mine = me - base
    pair = 2 * (mine // 2)
    long = members * rows
    share = chunks * width
    f32, bf16 = jnp.float32, jnp.bfloat16

    loads = [
        pltpu.make_async_copy(src, dst, load_sem.at[index])
        for index, (src, dst) in enumerate(
            (
                (k_hbm, k_ref), (v_hbm, v_ref), (q_hbm, q_ref), (taps_hbm, taps_ref),
                (lag_hbm, lag_ref), (decay_hbm, decay_ref), (skip_hbm, skip_ref),
                (pairs_hbm, pairs_ref),
            )
        )
    ]
    for load in loads:
        load.start()

    barrier = pltpu.get_barrier_semaphore()
    inner = quarter < 3
    first_of_later = (quarter > 0) & (mine == 0)
    last_of_earlier = (quarter < 3) & (mine == members - 1)

    def tell(sem, to):
        pl.semaphore_signal(sem, inc=1, device_id={"ctx": to}, device_id_type=MESH)

    def greet(k, c):
        tell(barrier, base + lax.rem(mine + k, members))
        return c

    lax.fori_loop(1, members, greet, 0)

    @pl.when(inner)
    def _():
        tell(barrier, me + members)

    @pl.when(last_of_earlier)
    def _():
        tell(barrier, me + 1)

    def build_toep():
        def build(e, c):
            upper = lag_ref[:, pl.ds(pl.multiple_of(e * rows, rows), rows)]
            below = jnp.maximum(e - 1, 0)
            lower = lag_ref[:, pl.ds(pl.multiple_of(below * rows, rows), rows)]
            lower = jnp.where(e > 0, lower, 0.0)
            window = jnp.broadcast_to(jnp.concatenate([upper, lower], axis=1), (rows, 2 * rows))
            turned = pltpu.roll(window, 0, 1, stride=1, stride_axis=0)[:, :rows]
            toep[e] = turned.T
            return c

        lax.fori_loop(0, 3 * members, build, 0)

    def border_of():
        listed = jnp.where(pairs_ref[:, 0, :] == 0, pairs_ref[:, 1, :], -1)
        return 1 + jnp.max(jnp.max(listed, axis=1, keepdims=True), axis=0, keepdims=True)

    def build_mix():
        border = border_of()
        early = jnp.where(border <= n // 2, 1.0, 0.0)
        raw = jnp.where(quarter == 1, 1.0, jnp.where(quarter == 2, early, 0.0))
        eye = jnp.where(
            lax.broadcasted_iota(jnp.int32, (rows, rows), 0)
            == lax.broadcasted_iota(jnp.int32, (rows, rows), 1),
            1.0, 0.0,
        )

        def live(source, target):
            a = jnp.where(border > source, 1.0, 0.0)
            b = jnp.where(border > target, 1.0, 0.0)
            return 1.0 - jnp.abs(a - b)

        def at(index):
            return pl.ds(pl.multiple_of(index * rows, rows), rows)

        def fill(i, carry):
            def one(j, carry):
                src, dst = base + j, base + i
                causal = jnp.where(j <= i, 1.0, 0.0)
                mix_here[at(i), at(members + j)] = (
                    toep[jnp.maximum(i - j, 0)] * (live(src, dst) * causal)
                ).astype(bf16)

                @pl.when(quarter > 0)
                def _():
                    passed = (1.0 - raw) * jnp.where(i == j, 1.0, 0.0)
                    mix_here[at(i), at(j)] = (
                        toep[members + i - j] * (raw * live(src - members, dst)) + eye * passed
                    ).astype(bf16)

                @pl.when((quarter > 0) & (quarter < 3))
                def _():
                    mix_next[at(i), at(members + j)] = (
                        toep[members + i - j] * live(src, dst + members)
                    ).astype(bf16)
                    mix_next[at(i), at(j)] = (
                        toep[2 * members + i - j] * (raw * live(src - members, dst + members))
                    ).astype(bf16)

                return carry

            return lax.fori_loop(0, members, one, carry)

        lax.fori_loop(0, members, fill, 0)

    for load in loads:
        load.wait()

    edge[...] = jnp.zeros_like(edge)
    for index, ref in enumerate((k_ref, v_ref, q_ref)):
        tail = ref[rows - 16 :, :].astype(f32)
        for p in range(members):
            for side in range(2):
                at = (2 * index + side) * members + p
                edge[at : at + 1, :] = tail[14 + side : 15 + side, p * share : (p + 1) * share]
    rim_out[...] = edge[...].astype(bf16)

    @pl.when(quarter > 0)
    def _():
        build_toep()

    def awaited():
        total = members - 1 + jnp.where(quarter > 0, 1, 0)
        return total + jnp.where(first_of_later, 1, 0)

    pl.semaphore_wait(barrier, awaited())

    @pl.when(quarter > 0)
    def _():
        tell(ready.at[0], me - members)

    @pl.when(first_of_later)
    def _():
        tell(ready.at[1], me - 1)

    def rim_copy(to, part):
        size = 4 * members if part == 0 else rim_out.shape[0] - 4 * members
        at = pl.ds(4 * members * part, size)
        return pltpu.make_async_remote_copy(
            src_ref=rim_out.at[at], dst_ref=rim_in.at[at], send_sem=rim_send.at[part],
            recv_sem=rim_recv.at[part], device_id={"ctx": to}, device_id_type=MESH,
        )

    @pl.when(mine < members - 1)
    def _():
        for part in range(2):
            rim_copy(me + 1, part).start()

    @pl.when(quarter > 0)
    def _():
        build_mix()

    @pl.when(me == 0)
    def _():
        rim[...] = jnp.zeros_like(rim)

    @pl.when(me > 0)
    def _():
        for part in range(2):
            rim_copy(me - 1, part).wait_recv()
        edge[...] = rim_in[...].astype(f32)
        for at in range(6):
            for p in range(members):
                from_row = at * members + p
                rim[at : at + 1, p * share : (p + 1) * share] = edge[from_row : from_row + 1, :]

    row = lax.broadcasted_iota(jnp.int32, (rows, width), 0)

    def columns(c, p):
        return pl.ds(pl.multiple_of((p * chunks + c) * width, width), width)

    def feature(ref, index, c, p):
        cols = columns(c, p)
        tap = (index + 1) % 3
        x = ref[:, cols].astype(f32)
        two = rim[2 * index : 2 * index + 1, cols]
        one = rim[2 * index + 1 : 2 * index + 2, cols]
        x1 = jnp.where(row == 0, one, pltpu.roll(x, 1, 0))
        x2 = jnp.where(row == 0, two, jnp.where(row == 1, one, pltpu.roll(x, 2, 0)))
        return (
            taps_ref[tap, 0:1, cols] * x
            + taps_ref[tap, 1:2, cols] * x1
            + taps_ref[tap, 2:3, cols] * x2
        )

    def forward(c, p, sender):
        return pltpu.make_async_remote_copy(
            src_ref=gated.at[c, p], dst_ref=spans.at[c, sender],
            send_sem=send1.at[c, p], recv_sem=recv1.at[c, sender],
            device_id={"ctx": base + p}, device_id_type=MESH,
        )

    def backward(c, p, sender):
        return pltpu.make_async_remote_copy(
            src_ref=result.at[c, p], dst_ref=landed.at[c, sender],
            send_sem=send2.at[c, p], recv_sem=recv2.at[c, sender],
            device_id={"ctx": base + p}, device_id_type=MESH,
        )

    def raw_copy(c, j):
        return pltpu.make_async_remote_copy(
            src_ref=spans.at[c, j], dst_ref=inbox.at[c, j],
            send_sem=send_z.at[c], recv_sem=recv_z.at[c],
            device_id={"ctx": lax.rem(me + members, n)}, device_id_type=MESH,
        )

    def box_copy(c):
        return pltpu.make_async_remote_copy(
            src_ref=outbox.at[c], dst_ref=inbox.at[c],
            send_sem=send_z.at[c], recv_sem=recv_z.at[c],
            device_id={"ctx": lax.rem(me + members, n)}, device_id_type=MESH,
        )

    def gate_chunk(c):
        def gate(k, carry):
            p = lax.rem(pair + 2 + k, members)
            value = (feature(k_ref, 0, c, p) * feature(v_ref, 1, c, p)).astype(bf16)
            gated[c, p] = value

            @pl.when(p != mine)
            def _():
                forward(c, p, mine).start()

            @pl.when(p == mine)
            def _():
                spans[c, mine] = value

            return carry

        lax.fori_loop(0, members, gate, 0)

    def relay_chunk(c):
        def relay(k, carry):
            j = lax.rem(pair + k, members)

            @pl.when(j != mine)
            def _():
                forward(c, mine, j).wait_recv()

            raw_copy(c, j).start()
            return carry

        lax.fori_loop(0, members, relay, 0)

    gate_chunk(0)

    @pl.when(inner)
    def _():
        pl.semaphore_wait(ready.at[0], 1)

    @pl.when(last_of_earlier)
    def _():
        pl.semaphore_wait(ready.at[1], 1)
        for part in range(2):
            rim_copy(me + 1, part).start()

    def lead(c, carry):
        gate_chunk(c)

        @pl.when(quarter == 0)
        def _():
            relay_chunk(c - 1)

        return carry

    lax.fori_loop(1, chunks, lead, 0)

    @pl.when(quarter == 0)
    def _():
        relay_chunk(chunks - 1)
        build_toep()
        build_mix()

    border = border_of()
    early_all = border <= n // 2
    take_raw = early_all & (quarter == 1)
    is_raw = (quarter == 1) | (early_all & (quarter == 2))
    place = lax.broadcasted_iota(jnp.int32, (rows, width), 0).astype(f32)
    tile = 2 * rows

    def finish_chunk(c):
        def finish(k, carry):
            p = lax.rem(mine + k, members)

            @pl.when(p != mine)
            def _():
                backward(c, mine, p).wait_recv()

            cols = columns(c, p)
            direct = skip_ref[:, cols] * gated[c, p].astype(f32)
            out_ref[:, cols] = (
                qfeat[c, p] * (landed[c, p].astype(f32) + direct)
            ).astype(bf16)
            store(c, p).start()
            return carry

        lax.fori_loop(0, members, finish, 0)

    def store(c, p):
        cols = columns(c, p)
        return pltpu.make_async_copy(out_ref.at[:, cols], out_hbm.at[:, cols], store_sem.at[c, p])

    def at(index, size):
        return pl.ds(pl.multiple_of(index * size, size), size)

    def step(c, carry):
        rate = decay_ref[:, columns(c, mine)]
        far = jnp.exp(-rate * long)

        def query(p, carry):
            qfeat[c, p] = feature(q_ref, 2, c, p)
            return carry

        lax.fori_loop(0, members, query, 0)

        def prepare(j, carry):
            @pl.when((j != mine) & (quarter > 0))
            def _():
                forward(c, mine, j).wait_recv()

            spot = place + (j * rows).astype(f32)
            rise = jnp.exp(rate * spot)
            grow[j] = rise
            fade[j] = jnp.exp(-rate * spot)
            scaled[at(members + j, rows), :] = (spans[c, j].astype(f32) * rise).astype(bf16)
            return carry

        lax.fori_loop(0, members, prepare, 0)

        @pl.when(c >= 2)
        def _():
            finish_chunk(c - 2)

        @pl.when(quarter > 0)
        def _():
            box_copy(c).wait_recv()
            drop = jnp.where(is_raw, far, 1.0)

            def receive(j, carry):
                scaled[at(j, rows), :] = (
                    inbox[c, j].astype(f32) * (grow[j] * drop)
                ).astype(bf16)
                return carry

            lax.fori_loop(0, members, receive, 0)

        @pl.when((quarter > 0) & (quarter < 3))
        def _():
            def send(i, carry):
                acc = jnp.dot(mix_next[at(i, tile), :], scaled[...], preferred_element_type=f32)
                for side in range(2):
                    j = 2 * i + side
                    value = acc[side * rows : (side + 1) * rows] * (fade[j] * far)
                    raw = spans[c, j].astype(f32)
                    outbox[c, j] = jnp.where(take_raw, raw, value).astype(bf16)
                return carry

            lax.fori_loop(0, members // 2, send, 0)
            box_copy(c).start()

        def publish(i, acc):
            for side in range(2):
                reader = 2 * i + side
                value = (acc[side * rows : (side + 1) * rows] * fade[reader]).astype(bf16)
                result[c, reader] = value

                @pl.when(reader != mine)
                def _():
                    backward(c, reader, mine).start()

                @pl.when(reader == mine)
                def _():
                    landed[c, mine] = value

        @pl.when(quarter == 0)
        def _():
            def target(i, carry):
                publish(i, jnp.dot(
                    mix_here[at(i, tile), long:], scaled[long:, :], preferred_element_type=f32
                ))
                return carry

            lax.fori_loop(0, members // 2, target, 0)

        @pl.when(quarter > 0)
        def _():
            def target(i, carry):
                publish(i, jnp.dot(
                    mix_here[at(i, tile), :], scaled[...], preferred_element_type=f32
                ))
                return carry

            lax.fori_loop(0, members // 2, target, 0)

        return carry

    lax.fori_loop(0, chunks, step, 0)
    for c in range(chunks - 2, chunks):
        finish_chunk(c)

    def drain(c, carry):
        def one(k, carry):
            p = lax.rem(mine + k, members)
            forward(c, p, mine).wait_send()
            backward(c, p, mine).wait_send()
            return carry

        lax.fori_loop(1, members, one, 0)

        def stored(p, carry):
            store(c, p).wait()
            return carry

        lax.fori_loop(0, members, stored, 0)

        @pl.when(inner)
        def _():
            box_copy(c).wait_send()

        return carry

    lax.fori_loop(0, chunks, drain, 0)

    @pl.when(me < n - 1)
    def _():
        for part in range(2):
            rim_copy(me + 1, part).wait_send()


def hand_over(strip, src_ref, dst_ref, held, in_sem, out_sem):
    def load(i):
        part = pl.ds(i * strip, strip)
        return pltpu.make_async_copy(src_ref.at[part], held.at[part], in_sem.at[i])

    def store(i):
        part = pl.ds(i * strip, strip)
        return pltpu.make_async_copy(held.at[part], dst_ref.at[part], out_sem.at[i])

    for i in range(STRIPS):
        load(i).start()
    for i in range(STRIPS):
        load(i).wait()
        store(i).start()
    for i in range(STRIPS):
        store(i).wait()


def on_device(
    query_rows, key_rows, value_rows, conv_taps, decay_rate, lag_profile, skip_gain, pair_lists
):
    rows, channels = query_rows.shape
    n = lax.axis_size("ctx")
    members = n // 4
    share = channels // members
    width = WIDTH
    chunks = share // width
    long = members * rows
    pairs = pair_lists.transpose(1, 2, 0)
    hbm = pl.BlockSpec(memory_space=pltpu.HBM)
    bf16, f32 = jnp.bfloat16, jnp.float32
    piece = (chunks, members, rows, width)
    edges = 4 * members + max(16, 2 * members)
    dma = pltpu.SemaphoreType.DMA
    held = pl.pallas_call(
        functools.partial(kernel, n, rows, chunks, width),
        out_shape=jax.ShapeDtypeStruct((rows, channels), bf16),
        in_specs=[hbm] * 8,
        out_specs=hbm,
        scratch_shapes=[
            pltpu.VMEM((rows, channels), bf16),
            pltpu.VMEM((rows, channels), bf16),
            pltpu.VMEM((rows, channels), bf16),
            pltpu.VMEM((rows, channels), bf16),
            pltpu.VMEM(conv_taps.shape, f32),
            pltpu.VMEM((1, channels), f32),
            pltpu.VMEM((1, lag_profile.shape[0]), f32),
            pltpu.VMEM((1, channels), f32),
            pltpu.VMEM(pairs.shape, jnp.int32),
            pltpu.VMEM((edges, share), f32),
            pltpu.VMEM((edges, share), bf16),
            pltpu.VMEM((edges, share), bf16),
            pltpu.VMEM((8, channels), f32),
            pltpu.VMEM(piece, bf16),
            pltpu.VMEM(piece, f32),
            pltpu.VMEM(piece, bf16),
            pltpu.VMEM(piece, bf16),
            pltpu.VMEM(piece, bf16),
            pltpu.VMEM((3 * members, rows, rows), f32),
            pltpu.VMEM((long, 2 * long), bf16),
            pltpu.VMEM((long, 2 * long), bf16),
            pltpu.VMEM((2 * long, width), bf16),
            pltpu.VMEM((members, rows, width), f32),
            pltpu.VMEM((members, rows, width), f32),
            pltpu.VMEM(piece, bf16),
            pltpu.VMEM(piece, bf16),
            dma((8,)),
            dma((chunks, members)),
            dma((2,)),
            dma((2,)),
            dma((chunks, members)),
            dma((chunks, members)),
            dma((chunks,)),
            dma((chunks,)),
            dma((chunks, members)),
            dma((chunks, members)),
            pltpu.SemaphoreType.REGULAR((2,)),
        ],
        compiler_params=pltpu.CompilerParams(
            collective_id=0, has_side_effects=True, vmem_limit_bytes=60 * 1024 * 1024
        ),
    )(
        query_rows, key_rows, value_rows, conv_taps, decay_rate.reshape(1, -1),
        lag_profile.reshape(1, -1), skip_gain.reshape(1, -1), pairs,
    )
    return pl.pallas_call(
        functools.partial(hand_over, rows // STRIPS),
        out_shape=jax.ShapeDtypeStruct((rows, channels), bf16),
        in_specs=[hbm],
        out_specs=hbm,
        scratch_shapes=[pltpu.VMEM((rows, channels), bf16), dma((STRIPS,)), dma((STRIPS,))],
        compiler_params=pltpu.CompilerParams(vmem_limit_bytes=60 * 1024 * 1024),
    )(held)


def solution(mesh):
    rows = P(("group", "ctx"), None)
    return jax.shard_map(
        on_device,
        mesh=mesh,
        in_specs=(rows, rows, rows, P(), P(), P(), P(), P("group", None, None)),
        out_specs=rows,
        check_vma=False,
    )
```

```python
import functools

import jax
import jax.numpy as jnp
from jax import lax
from jax.experimental import pallas as pl
from jax.experimental.pallas import tpu as pltpu
from jax.sharding import PartitionSpec as P

MESH = pl.DeviceIdType.MESH
WIDTH = 128
STRIPS = 8


def kernel(
    n, rows, chunks, width,
    q_hbm, k_hbm, v_hbm, taps_hbm, decay_hbm, lag_hbm, skip_hbm, pairs_hbm,
    out_hbm,
    out_ref, q_ref, k_ref, v_ref, taps_ref, decay_ref, lag_ref, skip_ref, pairs_ref,
    edge, rim_out, rim_in, rim, gated, qfeat, spans, inbox, outbox, toep, mix_here, mix_next,
    scaled, grow, fade, result, landed,
    load_sem, store_sem, rim_send, rim_recv, send1, recv1, send_z, recv_z, send2, recv2, ready,
):
    me = lax.axis_index("ctx")
    members = n // 4
    quarter = me // members
    base = quarter * members
    mine = me - base
    pair = 2 * (mine // 2)
    long = members * rows
    share = chunks * width
    f32, bf16 = jnp.float32, jnp.bfloat16

    loads = [
        pltpu.make_async_copy(src, dst, load_sem.at[index])
        for index, (src, dst) in enumerate(
            (
                (k_hbm, k_ref), (v_hbm, v_ref), (taps_hbm, taps_ref), (q_hbm, q_ref),
                (lag_hbm, lag_ref), (pairs_hbm, pairs_ref), (decay_hbm, decay_ref),
                (skip_hbm, skip_ref),
            )
        )
    ]
    for load in loads:
        load.start()

    barrier = pltpu.get_barrier_semaphore()
    inner = quarter < 3
    linked = (quarter > 0) & (quarter < 3)
    first_of_later = (quarter > 0) & (mine == 0)
    last_of_earlier = (quarter < 3) & (mine == members - 1)

    def tell(sem, to):
        pl.semaphore_signal(sem, inc=1, device_id={"ctx": to}, device_id_type=MESH)

    def greet(k, c):
        tell(barrier, base + lax.rem(mine + k, members))
        return c

    lax.fori_loop(1, members, greet, 0)

    @pl.when(inner)
    def _():
        tell(barrier, me + members)

    @pl.when(last_of_earlier)
    def _():
        tell(barrier, me + 1)

    def build_toep(groups):
        wide = 4 * rows

        def build(g, c):
            upper = lag_ref[:, pl.ds(pl.multiple_of(g * wide, wide), wide)]
            below = jnp.maximum(4 * g - 1, 0)
            lower = lag_ref[:, pl.ds(pl.multiple_of(below * rows, rows), rows)]
            lower = jnp.where(g > 0, lower, 0.0)
            window = jnp.broadcast_to(
                jnp.concatenate([upper, lower], axis=1), (rows, wide + rows)
            )
            turned = pltpu.roll(window, 0, 1, stride=1, stride_axis=0)
            for e in range(4):
                toep[4 * g + e] = turned[:, e * rows : (e + 1) * rows].T.astype(bf16)
            return c

        lax.fori_loop(0, groups, build, 0)

    def border_of():
        listed = jnp.where(pairs_ref[:, 0, :] == 0, pairs_ref[:, 1, :], -1)
        return 1 + jnp.max(jnp.max(listed, axis=1, keepdims=True), axis=0, keepdims=True)

    def build_mix():
        border = border_of()
        early = jnp.where(border <= n // 2, 1.0, 0.0)
        raw = jnp.where(quarter == 1, 1.0, early)
        eye = jnp.where(
            lax.broadcasted_iota(jnp.int32, (rows, rows), 0)
            == lax.broadcasted_iota(jnp.int32, (rows, rows), 1),
            1.0, 0.0,
        ).astype(bf16)

        def live(source, target):
            a = jnp.where(border > source, 1.0, 0.0)
            b = jnp.where(border > target, 1.0, 0.0)
            return 1.0 - jnp.abs(a - b)

        def at(index):
            return pl.ds(pl.multiple_of(index * rows, rows), rows)

        def fill(i, carry):
            def one(j, carry):
                src, dst = base + j, base + i
                causal = jnp.where(j <= i, 1.0, 0.0)
                mix_here[at(i), at(members + j)] = (
                    toep[jnp.maximum(i - j, 0)] * (live(src, dst) * causal).astype(bf16)
                )

                @pl.when(linked)
                def _():
                    passed = (1.0 - raw) * jnp.where(i == j, 1.0, 0.0)
                    near = toep[members + i - j]
                    mix_here[at(i), at(j)] = (
                        near * (raw * live(src - members, dst)).astype(bf16)
                        + eye * passed.astype(bf16)
                    )
                    mix_next[at(i), at(members + j)] = (
                        near * live(src, dst + members).astype(bf16)
                    )
                    mix_next[at(i), at(j)] = (
                        toep[2 * members + i - j]
                        * (raw * live(src - members, dst + members)).astype(bf16)
                    )

                return carry

            return lax.fori_loop(0, members, one, carry)

        lax.fori_loop(0, members, fill, 0)

    def build_all():
        loads[4].wait()
        loads[5].wait()

        @pl.when(linked)
        def _():
            build_toep(3 * members // 4)

        @pl.when(~linked)
        def _():
            build_toep(members // 4)

        build_mix()

    def awaited():
        total = members - 1 + jnp.where(quarter > 0, 1, 0)
        return total + jnp.where(first_of_later, 1, 0)

    pl.semaphore_wait(barrier, awaited())

    @pl.when(quarter > 0)
    def _():
        tell(ready.at[0], me - members)

    @pl.when(first_of_later)
    def _():
        tell(ready.at[1], me - 1)

    def rim_copy(to, part):
        size = 4 * members if part == 0 else rim_out.shape[0] - 4 * members
        at = pl.ds(4 * members * part, size)
        return pltpu.make_async_remote_copy(
            src_ref=rim_out.at[at], dst_ref=rim_in.at[at], send_sem=rim_send.at[part],
            recv_sem=rim_recv.at[part], device_id={"ctx": to}, device_id_type=MESH,
        )

    def edges(index, ref):
        tail = ref[rows - 16 :, :].astype(f32)
        for p in range(members):
            for side in range(2):
                at = (2 * index + side) * members + p
                edge[at : at + 1, :] = tail[14 + side : 15 + side, p * share : (p + 1) * share]

    edge[...] = jnp.zeros_like(edge)
    loads[0].wait()
    edges(0, k_ref)
    loads[1].wait()
    edges(1, v_ref)
    rim_out[: 4 * members, :] = edge[: 4 * members, :].astype(bf16)

    @pl.when(mine < members - 1)
    def _():
        rim_copy(me + 1, 0).start()

    loads[2].wait()
    loads[3].wait()
    edges(2, q_ref)
    rim_out[4 * members :, :] = edge[4 * members :, :].astype(bf16)

    @pl.when(mine < members - 1)
    def _():
        rim_copy(me + 1, 1).start()

    def spread(first, last):
        size = max(16, (last - first) * members)
        held = rim_in[first * members : first * members + size, :].astype(f32)
        for at in range(first, last):
            for p in range(members):
                from_row = (at - first) * members + p
                rim[at : at + 1, p * share : (p + 1) * share] = held[from_row : from_row + 1, :]

    @pl.when(me == 0)
    def _():
        rim[...] = jnp.zeros_like(rim)

    @pl.when(me > 0)
    def _():
        rim_copy(me - 1, 0).wait_recv()
        spread(0, 4)

    def late_rim():
        @pl.when(me > 0)
        def _():
            rim_copy(me - 1, 1).wait_recv()
            spread(4, 6)

    row = lax.broadcasted_iota(jnp.int32, (rows, width), 0)

    def columns(c, p):
        return pl.ds(pl.multiple_of((p * chunks + c) * width, width), width)

    def feature(ref, index, c, p):
        cols = columns(c, p)
        tap = (index + 1) % 3
        x = ref[:, cols].astype(f32)
        two = rim[2 * index : 2 * index + 1, cols]
        one = rim[2 * index + 1 : 2 * index + 2, cols]
        x1 = jnp.where(row == 0, one, pltpu.roll(x, 1, 0))
        x2 = jnp.where(row == 0, two, jnp.where(row == 1, one, pltpu.roll(x, 2, 0)))
        return (
            taps_ref[tap, 0:1, cols] * x
            + taps_ref[tap, 1:2, cols] * x1
            + taps_ref[tap, 2:3, cols] * x2
        )

    def forward(c, p, sender):
        return pltpu.make_async_remote_copy(
            src_ref=gated.at[c, p], dst_ref=spans.at[c, sender],
            send_sem=send1.at[c, p], recv_sem=recv1.at[c, sender],
            device_id={"ctx": base + p}, device_id_type=MESH,
        )

    def backward(c, p, sender):
        return pltpu.make_async_remote_copy(
            src_ref=result.at[c, p], dst_ref=landed.at[c, sender],
            send_sem=send2.at[c, p], recv_sem=recv2.at[c, sender],
            device_id={"ctx": base + p}, device_id_type=MESH,
        )

    def raw_copy(c, j):
        return pltpu.make_async_remote_copy(
            src_ref=spans.at[c, j], dst_ref=inbox.at[c, j],
            send_sem=send_z.at[c], recv_sem=recv_z.at[c],
            device_id={"ctx": lax.rem(me + members, n)}, device_id_type=MESH,
        )

    def box_copy(c):
        return pltpu.make_async_remote_copy(
            src_ref=outbox.at[c], dst_ref=inbox.at[c],
            send_sem=send_z.at[c], recv_sem=recv_z.at[c],
            device_id={"ctx": lax.rem(me + members, n)}, device_id_type=MESH,
        )

    def gate_chunk(c):
        def gate(k, carry):
            p = lax.rem(pair + 2 + k, members)
            value = (feature(k_ref, 0, c, p) * feature(v_ref, 1, c, p)).astype(bf16)
            gated[c, p] = value

            @pl.when(p != mine)
            def _():
                forward(c, p, mine).start()

            @pl.when(p == mine)
            def _():
                spans[c, mine] = value

            return carry

        lax.fori_loop(0, members, gate, 0)

    def relay_chunk(c):
        def relay(k, carry):
            j = lax.rem(pair + k, members)

            @pl.when(j != mine)
            def _():
                forward(c, mine, j).wait_recv()

            raw_copy(c, j).start()
            return carry

        lax.fori_loop(0, members, relay, 0)

    gate_chunk(0)

    @pl.when(inner)
    def _():
        pl.semaphore_wait(ready.at[0], 1)

    @pl.when(last_of_earlier)
    def _():
        pl.semaphore_wait(ready.at[1], 1)
        for part in range(2):
            rim_copy(me + 1, part).start()

    gate_chunk(1)

    @pl.when(quarter == 0)
    def _():
        relay_chunk(0)

    build_all()

    def lead(c, carry):
        gate_chunk(c)
        return carry

    @pl.when(quarter > 0)
    def _():
        lax.fori_loop(2, chunks, lead, 0)

    late_rim()
    loads[6].wait()
    loads[7].wait()
    border = border_of()
    early_all = border <= n // 2
    take_raw = early_all & (quarter == 1)
    is_raw = (quarter == 1) | (early_all & (quarter == 2))
    place = lax.broadcasted_iota(jnp.int32, (rows, width), 0).astype(f32)
    tile = 2 * rows

    def finish_chunk(c):
        def finish(k, carry):
            p = lax.rem(mine + k, members)

            @pl.when(p != mine)
            def _():
                backward(c, mine, p).wait_recv()

            cols = columns(c, p)
            direct = skip_ref[:, cols] * gated[c, p].astype(f32)
            out_ref[:, cols] = (
                qfeat[c, p] * (landed[c, p].astype(f32) + direct)
            ).astype(bf16)
            store(c, p).start()
            return carry

        lax.fori_loop(0, members, finish, 0)

    def store(c, p):
        cols = columns(c, p)
        return pltpu.make_async_copy(out_ref.at[:, cols], out_hbm.at[:, cols], store_sem.at[c, p])

    def at(index, size):
        return pl.ds(pl.multiple_of(index * size, size), size)

    lag = jnp.where(quarter == 3, 1, jnp.where(quarter == 0, 3, 4))

    def step(c, carry):
        @pl.when((quarter == 0) & (c + 2 < chunks))
        def _():
            gate_chunk(c + 2)

        @pl.when((quarter == 0) & (c + 1 < chunks))
        def _():
            relay_chunk(c + 1)

        rate = decay_ref[:, columns(c, mine)]
        far = jnp.exp(-rate * long)

        def query(p, carry):
            qfeat[c, p] = feature(q_ref, 2, c, p)
            return carry

        lax.fori_loop(0, members, query, 0)

        def prepare(j, carry):
            @pl.when((j != mine) & (quarter > 0))
            def _():
                forward(c, mine, j).wait_recv()

            spot = place + (j * rows).astype(f32)
            rise = jnp.exp(rate * spot)
            grow[j] = rise
            fade[j] = jnp.exp(-rate * spot)
            scaled[at(members + j, rows), :] = (spans[c, j].astype(f32) * rise).astype(bf16)
            return carry

        lax.fori_loop(0, members, prepare, 0)

        @pl.when(c >= lag)
        def _():
            finish_chunk(c - lag)

        def own_part(i):
            return jnp.dot(
                mix_here[at(i, tile), long:], scaled[long:, :], preferred_element_type=f32
            )

        @pl.when(quarter == 3)
        def _():
            def target(i, carry):
                acc = own_part(i)
                for side in range(2):
                    j = 2 * i + side
                    grow[j] = acc[side * rows : (side + 1) * rows] * fade[j]
                return carry

            lax.fori_loop(0, members // 2, target, 0)
            box_copy(c).wait_recv()

        @pl.when(linked)
        def _():
            box_copy(c).wait_recv()
            drop = jnp.where(is_raw, far, 1.0)

            def receive(j, carry):
                scaled[at(j, rows), :] = (
                    inbox[c, j].astype(f32) * (grow[j] * drop)
                ).astype(bf16)
                return carry

            lax.fori_loop(0, members, receive, 0)

        @pl.when(linked)
        def _():
            def send(i, carry):
                acc = jnp.dot(mix_next[at(i, tile), :], scaled[...], preferred_element_type=f32)
                for side in range(2):
                    j = 2 * i + side
                    value = acc[side * rows : (side + 1) * rows] * (fade[j] * far)
                    raw = spans[c, j].astype(f32)
                    outbox[c, j] = jnp.where(take_raw, raw, value).astype(bf16)
                return carry

            lax.fori_loop(0, members // 2, send, 0)
            box_copy(c).start()

        def publish(reader, value):
            value = value.astype(bf16)
            result[c, reader] = value

            @pl.when(reader != mine)
            def _():
                backward(c, reader, mine).start()

            @pl.when(reader == mine)
            def _():
                landed[c, mine] = value

        def publish_both(i, acc):
            for side in range(2):
                reader = 2 * i + side
                publish(reader, acc[side * rows : (side + 1) * rows] * fade[reader])

        @pl.when(quarter == 0)
        def _():
            def target(i, carry):
                publish_both(i, own_part(i))
                return carry

            lax.fori_loop(0, members // 2, target, 0)

        @pl.when(linked)
        def _():
            def target(i, carry):
                publish_both(i, jnp.dot(
                    mix_here[at(i, tile), :], scaled[...], preferred_element_type=f32
                ))
                return carry

            lax.fori_loop(0, members // 2, target, 0)

        @pl.when(quarter == 3)
        def _():
            def target(k, carry):
                reader = lax.rem(pair + 2 + k, members)
                publish(reader, grow[reader] + inbox[c, reader].astype(f32))
                return carry

            lax.fori_loop(0, members, target, 0)

        return carry

    lax.fori_loop(0, chunks, step, 0)

    def tail(c, carry):
        finish_chunk(c)
        return carry

    lax.fori_loop(chunks - lag, chunks, tail, 0)

    def drain(c, carry):
        def one(k, carry):
            p = lax.rem(mine + k, members)
            forward(c, p, mine).wait_send()
            backward(c, p, mine).wait_send()
            return carry

        lax.fori_loop(1, members, one, 0)

        def stored(p, carry):
            store(c, p).wait()
            return carry

        lax.fori_loop(0, members, stored, 0)

        @pl.when(inner)
        def _():
            box_copy(c).wait_send()

        return carry

    lax.fori_loop(0, chunks, drain, 0)

    @pl.when(me < n - 1)
    def _():
        for part in range(2):
            rim_copy(me + 1, part).wait_send()


def hand_over(strip, src_ref, dst_ref, held, in_sem, out_sem):
    def load(i):
        part = pl.ds(i * strip, strip)
        return pltpu.make_async_copy(src_ref.at[part], held.at[part], in_sem.at[i])

    def store(i):
        part = pl.ds(i * strip, strip)
        return pltpu.make_async_copy(held.at[part], dst_ref.at[part], out_sem.at[i])

    for i in range(STRIPS):
        load(i).start()
    for i in range(STRIPS):
        load(i).wait()
        store(i).start()
    for i in range(STRIPS):
        store(i).wait()


def on_device(
    query_rows, key_rows, value_rows, conv_taps, decay_rate, lag_profile, skip_gain, pair_lists
):
    rows, channels = query_rows.shape
    n = lax.axis_size("ctx")
    members = n // 4
    share = channels // members
    width = WIDTH
    chunks = share // width
    long = members * rows
    pairs = pair_lists.transpose(1, 2, 0)
    hbm = pl.BlockSpec(memory_space=pltpu.HBM)
    bf16, f32 = jnp.bfloat16, jnp.float32
    piece = (chunks, members, rows, width)
    edges = 4 * members + max(16, 2 * members)
    dma = pltpu.SemaphoreType.DMA
    held = pl.pallas_call(
        functools.partial(kernel, n, rows, chunks, width),
        out_shape=jax.ShapeDtypeStruct((rows, channels), bf16),
        in_specs=[hbm] * 8,
        out_specs=hbm,
        scratch_shapes=[
            pltpu.VMEM((rows, channels), bf16),
            pltpu.VMEM((rows, channels), bf16),
            pltpu.VMEM((rows, channels), bf16),
            pltpu.VMEM((rows, channels), bf16),
            pltpu.VMEM(conv_taps.shape, f32),
            pltpu.VMEM((1, channels), f32),
            pltpu.VMEM((1, lag_profile.shape[0]), f32),
            pltpu.VMEM((1, channels), f32),
            pltpu.VMEM(pairs.shape, jnp.int32),
            pltpu.VMEM((edges, share), f32),
            pltpu.VMEM((edges, share), bf16),
            pltpu.VMEM((edges, share), bf16),
            pltpu.VMEM((8, channels), f32),
            pltpu.VMEM(piece, bf16),
            pltpu.VMEM(piece, f32),
            pltpu.VMEM(piece, bf16),
            pltpu.VMEM(piece, bf16),
            pltpu.VMEM(piece, bf16),
            pltpu.VMEM((3 * members, rows, rows), bf16),
            pltpu.VMEM((long, 2 * long), bf16),
            pltpu.VMEM((long, 2 * long), bf16),
            pltpu.VMEM((2 * long, width), bf16),
            pltpu.VMEM((members, rows, width), f32),
            pltpu.VMEM((members, rows, width), f32),
            pltpu.VMEM(piece, bf16),
            pltpu.VMEM(piece, bf16),
            dma((8,)),
            dma((chunks, members)),
            dma((2,)),
            dma((2,)),
            dma((chunks, members)),
            dma((chunks, members)),
            dma((chunks,)),
            dma((chunks,)),
            dma((chunks, members)),
            dma((chunks, members)),
            pltpu.SemaphoreType.REGULAR((2,)),
        ],
        compiler_params=pltpu.CompilerParams(
            collective_id=0, has_side_effects=True, vmem_limit_bytes=60 * 1024 * 1024
        ),
    )(
        query_rows, key_rows, value_rows, conv_taps, decay_rate.reshape(1, -1),
        lag_profile.reshape(1, -1), skip_gain.reshape(1, -1), pairs,
    )
    return pl.pallas_call(
        functools.partial(hand_over, rows // STRIPS),
        out_shape=jax.ShapeDtypeStruct((rows, channels), bf16),
        in_specs=[hbm],
        out_specs=hbm,
        scratch_shapes=[pltpu.VMEM((rows, channels), bf16), dma((STRIPS,)), dma((STRIPS,))],
        compiler_params=pltpu.CompilerParams(vmem_limit_bytes=60 * 1024 * 1024),
    )(held)


def solution(mesh):
    rows = P(("group", "ctx"), None)
    return jax.shard_map(
        on_device,
        mesh=mesh,
        in_specs=(rows, rows, rows, P(), P(), P(), P(), P("group", None, None)),
        out_specs=rows,
        check_vma=False,
    )
```

```python
import functools

import jax
import jax.numpy as jnp
from jax import lax
from jax.experimental import pallas as pl
from jax.experimental.pallas import tpu as pltpu
from jax.sharding import PartitionSpec as P

MESH = pl.DeviceIdType.MESH
WIDTH = 128
STRIPS = 8


def kernel(
    n, rows, chunks, width,
    q_hbm, k_hbm, v_hbm, taps_hbm, decay_hbm, lag_hbm, skip_hbm, pairs_hbm,
    out_hbm,
    out_ref, q_ref, k_ref, v_ref, taps_ref, decay_ref, lag_ref, skip_ref, pairs_ref,
    edge, rim_out, rim_in, rim, gated, qfeat, spans, inbox, outbox, toep, mix_here, mix_next,
    scaled, grow, fade, ahead, result, landed,
    load_sem, rim_sem, sent, recv1, recv_z, recv2, ready,
):
    me = lax.axis_index("ctx")
    members = n // 4
    quarter = me // members
    base = quarter * members
    mine = me - base
    pair = 2 * (mine // 2)
    long = members * rows
    share = chunks * width
    f32, bf16 = jnp.float32, jnp.bfloat16

    loads = [
        pltpu.make_async_copy(src, dst, load_sem.at[index])
        for index, (src, dst) in enumerate(
            (
                (k_hbm, k_ref), (v_hbm, v_ref), (taps_hbm, taps_ref), (q_hbm, q_ref),
                (lag_hbm, lag_ref), (pairs_hbm, pairs_ref), (decay_hbm, decay_ref),
                (skip_hbm, skip_ref),
            )
        )
    ]
    for load in loads:
        load.start()

    barrier = pltpu.get_barrier_semaphore()
    inner = quarter < 3
    linked = (quarter > 0) & (quarter < 3)
    first_of_later = (quarter > 0) & (mine == 0)
    last_of_earlier = (quarter < 3) & (mine == members - 1)

    def tell(sem, to):
        pl.semaphore_signal(sem, inc=1, device_id={"ctx": to}, device_id_type=MESH)

    def greet(k, c):
        tell(barrier, base + lax.rem(mine + k, members))
        return c

    lax.fori_loop(1, members, greet, 0)

    @pl.when(inner)
    def _():
        tell(barrier, me + members)

    @pl.when(last_of_earlier)
    def _():
        tell(barrier, me + 1)

    def build_toep(groups):
        wide = 4 * rows

        def build(g, c):
            upper = lag_ref[:, pl.ds(pl.multiple_of(g * wide, wide), wide)]
            below = jnp.maximum(4 * g - 1, 0)
            lower = lag_ref[:, pl.ds(pl.multiple_of(below * rows, rows), rows)]
            lower = jnp.where(g > 0, lower, 0.0)
            window = jnp.broadcast_to(
                jnp.concatenate([upper, lower], axis=1), (rows, wide + rows)
            )
            turned = pltpu.roll(window, 0, 1, stride=1, stride_axis=0)
            for e in range(4):
                toep[4 * g + e] = turned[:, e * rows : (e + 1) * rows].T.astype(bf16)
            return c

        lax.fori_loop(0, groups, build, 0)

    def border_of():
        listed = jnp.where(pairs_ref[:, 0, :] == 0, pairs_ref[:, 1, :], -1)
        return 1 + jnp.max(jnp.max(listed, axis=1, keepdims=True), axis=0, keepdims=True)

    def build_mix():
        border = border_of()
        early = jnp.where(border <= n // 2, 1.0, 0.0)
        raw = jnp.where(quarter == 1, 1.0, early)
        eye = jnp.where(
            lax.broadcasted_iota(jnp.int32, (rows, rows), 0)
            == lax.broadcasted_iota(jnp.int32, (rows, rows), 1),
            1.0, 0.0,
        ).astype(bf16)

        def live(source, target):
            a = jnp.where(border > source, 1.0, 0.0)
            b = jnp.where(border > target, 1.0, 0.0)
            return 1.0 - jnp.abs(a - b)

        def at(index):
            return pl.ds(pl.multiple_of(index * rows, rows), rows)

        def fill(i, carry):
            def one(j, carry):
                src, dst = base + j, base + i
                causal = jnp.where(j <= i, 1.0, 0.0)
                mix_here[at(i), at(members + j)] = (
                    toep[jnp.maximum(i - j, 0)] * (live(src, dst) * causal).astype(bf16)
                )

                @pl.when(linked)
                def _():
                    passed = (1.0 - raw) * jnp.where(i == j, 1.0, 0.0)
                    near = toep[members + i - j]
                    mix_here[at(i), at(j)] = (
                        near * (raw * live(src - members, dst)).astype(bf16)
                        + eye * passed.astype(bf16)
                    )
                    mix_next[at(i), at(members + j)] = (
                        near * live(src, dst + members).astype(bf16)
                    )
                    mix_next[at(i), at(j)] = (
                        toep[2 * members + i - j]
                        * (raw * live(src - members, dst + members)).astype(bf16)
                    )

                return carry

            return lax.fori_loop(0, members, one, carry)

        lax.fori_loop(0, members, fill, 0)

    def build_all():
        loads[4].wait()
        loads[5].wait()

        @pl.when(linked)
        def _():
            build_toep(3 * members // 4)

        @pl.when(~linked)
        def _():
            build_toep(members // 4)

        build_mix()

    def awaited():
        total = members - 1 + jnp.where(quarter > 0, 1, 0)
        return total + jnp.where(first_of_later, 1, 0)

    pl.semaphore_wait(barrier, awaited())

    @pl.when(quarter > 0)
    def _():
        tell(ready.at[0], me - members)

    @pl.when(first_of_later)
    def _():
        tell(ready.at[1], me - 1)

    def rim_copy(to, part):
        size = 4 * members if part == 0 else rim_out.shape[0] - 4 * members
        at = pl.ds(4 * members * part, size)
        return pltpu.make_async_remote_copy(
            src_ref=rim_out.at[at], dst_ref=rim_in.at[at], send_sem=rim_sem.at[part],
            recv_sem=rim_sem.at[2 + part], device_id={"ctx": to}, device_id_type=MESH,
        )

    def edges(index, ref):
        tail = ref[rows - 16 :, :].astype(f32)
        for p in range(members):
            for side in range(2):
                at = (2 * index + side) * members + p
                edge[at : at + 1, :] = tail[14 + side : 15 + side, p * share : (p + 1) * share]

    edge[...] = jnp.zeros_like(edge)
    loads[0].wait()
    edges(0, k_ref)
    loads[1].wait()
    edges(1, v_ref)
    rim_out[: 4 * members, :] = edge[: 4 * members, :].astype(bf16)

    @pl.when(mine < members - 1)
    def _():
        rim_copy(me + 1, 0).start()

    loads[2].wait()
    loads[3].wait()
    edges(2, q_ref)
    rim_out[4 * members :, :] = edge[4 * members :, :].astype(bf16)

    @pl.when(mine < members - 1)
    def _():
        rim_copy(me + 1, 1).start()

    def spread(first, last):
        size = max(16, (last - first) * members)
        held = rim_in[first * members : first * members + size, :].astype(f32)
        for at in range(first, last):
            for p in range(members):
                from_row = (at - first) * members + p
                rim[at : at + 1, p * share : (p + 1) * share] = held[from_row : from_row + 1, :]

    @pl.when(me == 0)
    def _():
        rim[...] = jnp.zeros_like(rim)

    @pl.when(me > 0)
    def _():
        rim_copy(me - 1, 0).wait_recv()
        spread(0, 4)

    def late_rim():
        @pl.when(me > 0)
        def _():
            rim_copy(me - 1, 1).wait_recv()
            spread(4, 6)

    row = lax.broadcasted_iota(jnp.int32, (rows, width), 0)

    def columns(c, p):
        return pl.ds(pl.multiple_of((p * chunks + c) * width, width), width)

    def feature(ref, index, c, p):
        cols = columns(c, p)
        tap = (index + 1) % 3
        x = ref[:, cols].astype(f32)
        two = rim[2 * index : 2 * index + 1, cols]
        one = rim[2 * index + 1 : 2 * index + 2, cols]
        x1 = jnp.where(row == 0, one, pltpu.roll(x, 1, 0))
        x2 = jnp.where(row == 0, two, jnp.where(row == 1, one, pltpu.roll(x, 2, 0)))
        return (
            taps_ref[tap, 0:1, cols] * x
            + taps_ref[tap, 1:2, cols] * x1
            + taps_ref[tap, 2:3, cols] * x2
        )

    def forward(c, p, sender):
        return pltpu.make_async_remote_copy(
            src_ref=gated.at[c, p], dst_ref=spans.at[c, sender],
            send_sem=sent.at[0], recv_sem=recv1.at[c],
            device_id={"ctx": base + p}, device_id_type=MESH,
        )

    def backward(c, p, sender):
        return pltpu.make_async_remote_copy(
            src_ref=result.at[c, p], dst_ref=landed.at[c, sender],
            send_sem=sent.at[1], recv_sem=recv2.at[c],
            device_id={"ctx": base + p}, device_id_type=MESH,
        )

    others = pl.ds(0, members - 1)

    def all_forward(c):
        return pltpu.make_async_remote_copy(
            src_ref=gated.at[c, others], dst_ref=spans.at[c, others],
            send_sem=sent.at[0], recv_sem=recv1.at[c],
            device_id={"ctx": base + lax.rem(mine + 1, members)}, device_id_type=MESH,
        )

    def all_backward(c):
        return pltpu.make_async_remote_copy(
            src_ref=result.at[c, others], dst_ref=landed.at[c, others],
            send_sem=sent.at[1], recv_sem=recv2.at[c],
            device_id={"ctx": base + lax.rem(mine + 1, members)}, device_id_type=MESH,
        )

    def raw_copy(c, j):
        return pltpu.make_async_remote_copy(
            src_ref=spans.at[c, j], dst_ref=inbox.at[c, j],
            send_sem=sent.at[2], recv_sem=recv_z.at[c],
            device_id={"ctx": lax.rem(me + members, n)}, device_id_type=MESH,
        )

    def box_copy(c):
        return pltpu.make_async_remote_copy(
            src_ref=outbox.at[c], dst_ref=inbox.at[c],
            send_sem=sent.at[2], recv_sem=recv_z.at[c],
            device_id={"ctx": lax.rem(me + members, n)}, device_id_type=MESH,
        )

    def half_box(c, i):
        both = pl.ds(2 * i, 2)
        return pltpu.make_async_remote_copy(
            src_ref=outbox.at[c, both], dst_ref=inbox.at[c, both],
            send_sem=sent.at[2], recv_sem=recv_z.at[c],
            device_id={"ctx": lax.rem(me + members, n)}, device_id_type=MESH,
        )

    def gate_chunk(c):
        def gate(k, carry):
            p = lax.rem(pair + 2 + k, members)
            value = (feature(k_ref, 0, c, p) * feature(v_ref, 1, c, p)).astype(bf16)
            gated[c, p] = value

            @pl.when(p != mine)
            def _():
                forward(c, p, mine).start()

            @pl.when(p == mine)
            def _():
                spans[c, mine] = value

            return carry

        lax.fori_loop(0, members, gate, 0)

    def relay_chunk(c):
        raw_copy(c, mine).start()
        all_forward(c).wait_recv()

        def relay(k, carry):
            raw_copy(c, lax.rem(mine + k, members)).start()
            return carry

        lax.fori_loop(1, members, relay, 0)

    gate_chunk(0)

    @pl.when(inner)
    def _():
        pl.semaphore_wait(ready.at[0], 1)

    @pl.when(last_of_earlier)
    def _():
        pl.semaphore_wait(ready.at[1], 1)
        for part in range(2):
            rim_copy(me + 1, part).start()

    gate_chunk(1)

    @pl.when(quarter == 0)
    def _():
        relay_chunk(0)

    build_all()

    def lead(c, carry):
        gate_chunk(c)
        return carry

    @pl.when(quarter > 0)
    def _():
        lax.fori_loop(2, chunks, lead, 0)

    late_rim()
    loads[6].wait()
    loads[7].wait()
    border = border_of()
    early_all = border <= n // 2
    take_raw = early_all & (quarter == 1)
    is_raw = (quarter == 1) | (early_all & (quarter == 2))
    place = lax.broadcasted_iota(jnp.int32, (rows, width), 0).astype(f32)
    tile = 2 * rows

    def finish_chunk(c):
        all_backward(c).wait_recv()

        def finish(p, carry):
            cols = columns(c, p)
            direct = skip_ref[:, cols] * gated[c, p].astype(f32)
            out_ref[:, cols] = (
                qfeat[c, p] * (landed[c, p].astype(f32) + direct)
            ).astype(bf16)
            pltpu.make_async_copy(
                out_ref.at[:, cols], out_hbm.at[:, cols], load_sem.at[8]
            ).start()
            return carry

        lax.fori_loop(0, members, finish, 0)

    def at(index, size):
        return pl.ds(pl.multiple_of(index * size, size), size)

    lag = jnp.where(quarter == 3, 2, jnp.where(quarter == 0, 3, 4))

    def step(c, carry):
        @pl.when((quarter == 0) & (c + 2 < chunks))
        def _():
            gate_chunk(c + 2)

        @pl.when((quarter == 0) & (c + 1 < chunks))
        def _():
            relay_chunk(c + 1)

        rate = decay_ref[:, columns(c, mine)]
        far = jnp.exp(-rate * long)

        def query(p, carry):
            qfeat[c, p] = feature(q_ref, 2, c, p)
            return carry

        lax.fori_loop(0, members, query, 0)

        @pl.when(quarter > 0)
        def _():
            all_forward(c).wait_recv()

        def prepare(j, carry):
            spot = place + (j * rows).astype(f32)
            rise = jnp.exp(rate * spot)
            grow[j] = rise
            fade[j] = jnp.exp(-rate * spot)
            scaled[at(members + j, rows), :] = (spans[c, j].astype(f32) * rise).astype(bf16)
            return carry

        lax.fori_loop(0, members, prepare, 0)

        @pl.when(c >= lag)
        def _():
            finish_chunk(c - lag)

        def own_part(i):
            return jnp.dot(
                mix_here[at(i, tile), long:], scaled[long:, :], preferred_element_type=f32
            )

        @pl.when(quarter == 3)
        def _():
            def target(i, carry):
                acc = own_part(i)
                for side in range(2):
                    j = 2 * i + side
                    grow[j] = acc[side * rows : (side + 1) * rows] * fade[j]
                return carry

            lax.fori_loop(0, members // 2, target, 0)
            box_copy(c).wait_recv()

        @pl.when(linked)
        def _():
            def before(i, carry):
                acc = jnp.dot(
                    mix_next[at(i, tile), long:], scaled[long:, :], preferred_element_type=f32
                )
                for side in range(2):
                    ahead[2 * i + side] = acc[side * rows : (side + 1) * rows]
                return carry

            lax.fori_loop(0, members // 2, before, 0)
            box_copy(c).wait_recv()
            drop = jnp.where(is_raw, far, 1.0)

            def receive(j, carry):
                scaled[at(j, rows), :] = (
                    inbox[c, j].astype(f32) * (grow[j] * drop)
                ).astype(bf16)
                return carry

            lax.fori_loop(0, members, receive, 0)

        @pl.when(linked)
        def _():
            def send(i, carry):
                acc = jnp.dot(
                    mix_next[at(i, tile), :long], scaled[:long, :], preferred_element_type=f32
                )
                for side in range(2):
                    j = 2 * i + side
                    value = (ahead[j] + acc[side * rows : (side + 1) * rows]) * (fade[j] * far)
                    raw = spans[c, j].astype(f32)
                    outbox[c, j] = jnp.where(take_raw, raw, value).astype(bf16)
                half_box(c, i).start()
                return carry

            lax.fori_loop(0, members // 2, send, 0)

        def publish(reader, value):
            value = value.astype(bf16)
            result[c, reader] = value

            @pl.when(reader != mine)
            def _():
                backward(c, reader, mine).start()

            @pl.when(reader == mine)
            def _():
                landed[c, mine] = value

        def publish_both(i, acc):
            for side in range(2):
                reader = 2 * i + side
                publish(reader, acc[side * rows : (side + 1) * rows] * fade[reader])

        @pl.when(quarter == 0)
        def _():
            def target(i, carry):
                publish_both(i, own_part(i))
                return carry

            lax.fori_loop(0, members // 2, target, 0)

        @pl.when(linked)
        def _():
            def target(i, carry):
                publish_both(i, jnp.dot(
                    mix_here[at(i, tile), :], scaled[...], preferred_element_type=f32
                ))
                return carry

            lax.fori_loop(0, members // 2, target, 0)

        @pl.when(quarter == 3)
        def _():
            def target(k, carry):
                reader = lax.rem(pair + 2 + k, members)
                publish(reader, grow[reader] + inbox[c, reader].astype(f32))
                return carry

            lax.fori_loop(0, members, target, 0)

        return carry

    lax.fori_loop(0, chunks, step, 0)

    def tail(c, carry):
        finish_chunk(c)
        return carry

    lax.fori_loop(chunks - lag, chunks, tail, 0)

    def everything(src, dst, index, count):
        part = pl.ds(0, count)
        return pltpu.make_async_remote_copy(
            src_ref=src.at[:, part], dst_ref=dst.at[:, part],
            send_sem=sent.at[index], recv_sem=recv1.at[0],
            device_id={"ctx": base + lax.rem(mine + 1, members)}, device_id_type=MESH,
        )

    everything(gated, spans, 0, members - 1).wait_send()
    everything(result, landed, 1, members - 1).wait_send()
    pltpu.make_async_copy(out_ref, out_hbm, load_sem.at[8]).wait()

    @pl.when(inner)
    def _():
        everything(spans, inbox, 2, members).wait_send()

    @pl.when(me < n - 1)
    def _():
        for part in range(2):
            rim_copy(me + 1, part).wait_send()


def hand_over(strip, src_ref, dst_ref, held, in_sem, out_sem):
    def load(i):
        part = pl.ds(i * strip, strip)
        return pltpu.make_async_copy(src_ref.at[part], held.at[part], in_sem.at[i])

    def store(i):
        part = pl.ds(i * strip, strip)
        return pltpu.make_async_copy(held.at[part], dst_ref.at[part], out_sem.at[i])

    for i in range(STRIPS):
        load(i).start()
    for i in range(STRIPS):
        load(i).wait()
        store(i).start()
    for i in range(STRIPS):
        store(i).wait()


def on_device(
    query_rows, key_rows, value_rows, conv_taps, decay_rate, lag_profile, skip_gain, pair_lists
):
    rows, channels = query_rows.shape
    n = lax.axis_size("ctx")
    members = n // 4
    share = channels // members
    width = WIDTH
    chunks = share // width
    long = members * rows
    pairs = pair_lists.transpose(1, 2, 0)
    hbm = pl.BlockSpec(memory_space=pltpu.HBM)
    bf16, f32 = jnp.bfloat16, jnp.float32
    piece = (chunks, members, rows, width)
    edges = 4 * members + max(16, 2 * members)
    dma = pltpu.SemaphoreType.DMA
    held = pl.pallas_call(
        functools.partial(kernel, n, rows, chunks, width),
        out_shape=jax.ShapeDtypeStruct((rows, channels), bf16),
        in_specs=[hbm] * 8,
        out_specs=hbm,
        scratch_shapes=[
            pltpu.VMEM((rows, channels), bf16),
            pltpu.VMEM((rows, channels), bf16),
            pltpu.VMEM((rows, channels), bf16),
            pltpu.VMEM((rows, channels), bf16),
            pltpu.VMEM(conv_taps.shape, f32),
            pltpu.VMEM((1, channels), f32),
            pltpu.VMEM((1, lag_profile.shape[0]), f32),
            pltpu.VMEM((1, channels), f32),
            pltpu.VMEM(pairs.shape, jnp.int32),
            pltpu.VMEM((edges, share), f32),
            pltpu.VMEM((edges, share), bf16),
            pltpu.VMEM((edges, share), bf16),
            pltpu.VMEM((8, channels), f32),
            pltpu.VMEM(piece, bf16),
            pltpu.VMEM(piece, f32),
            pltpu.VMEM(piece, bf16),
            pltpu.VMEM(piece, bf16),
            pltpu.VMEM(piece, bf16),
            pltpu.VMEM((3 * members, rows, rows), bf16),
            pltpu.VMEM((long, 2 * long), bf16),
            pltpu.VMEM((long, 2 * long), bf16),
            pltpu.VMEM((2 * long, width), bf16),
            pltpu.VMEM((members, rows, width), f32),
            pltpu.VMEM((members, rows, width), f32),
            pltpu.VMEM((members, rows, width), f32),
            pltpu.VMEM(piece, bf16),
            pltpu.VMEM(piece, bf16),
            dma((9,)),
            dma((4,)),
            dma((3,)),
            dma((chunks,)),
            dma((chunks,)),
            dma((chunks,)),
            pltpu.SemaphoreType.REGULAR((2,)),
        ],
        compiler_params=pltpu.CompilerParams(
            collective_id=0, has_side_effects=True, vmem_limit_bytes=60 * 1024 * 1024
        ),
    )(
        query_rows, key_rows, value_rows, conv_taps, decay_rate.reshape(1, -1),
        lag_profile.reshape(1, -1), skip_gain.reshape(1, -1), pairs,
    )
    return pl.pallas_call(
        functools.partial(hand_over, rows // STRIPS),
        out_shape=jax.ShapeDtypeStruct((rows, channels), bf16),
        in_specs=[hbm],
        out_specs=hbm,
        scratch_shapes=[pltpu.VMEM((rows, channels), bf16), dma((STRIPS,)), dma((STRIPS,))],
        compiler_params=pltpu.CompilerParams(vmem_limit_bytes=60 * 1024 * 1024),
    )(held)


def solution(mesh):
    rows = P(("group", "ctx"), None)
    return jax.shard_map(
        on_device,
        mesh=mesh,
        in_specs=(rows, rows, rows, P(), P(), P(), P(), P("group", None, None)),
        out_specs=rows,
        check_vma=False,
    )
```

```python
import functools

import jax
import jax.numpy as jnp
from jax import lax
from jax.experimental import pallas as pl
from jax.experimental.pallas import tpu as pltpu
from jax.sharding import PartitionSpec as P

MESH = pl.DeviceIdType.MESH
WIDTH = 128
STRIPS = 8


def kernel(
    n, rows, chunks, width,
    q_hbm, k_hbm, v_hbm, taps_hbm, decay_hbm, lag_hbm, skip_hbm, pairs_hbm,
    out_ref, q_ref, k_ref, v_ref, taps_ref, decay_ref, lag_ref, skip_ref, pairs_ref,
    tail_ref, edge, rim_out, rim_in, rim, gated, qfeat, spans, inbox, outbox, toep, mix_here, mix_next,
    scaled, grow, fade, ahead, result, landed,
    load_sem, rim_sem, sent, recv1, recv_z, recv2, ready,
):
    me = lax.axis_index("ctx")
    members = n // 4
    quarter = me // members
    base = quarter * members
    mine = me - base
    pair = 2 * (mine // 2)
    long = members * rows
    share = chunks * width
    f32, bf16 = jnp.float32, jnp.bfloat16

    loads = [
        pltpu.make_async_copy(src, dst, load_sem.at[index])
        for index, (src, dst) in enumerate(
            (
                (k_hbm, k_ref), (v_hbm, v_ref), (taps_hbm, taps_ref), (q_hbm, q_ref),
                (lag_hbm, lag_ref), (pairs_hbm, pairs_ref), (decay_hbm, decay_ref),
                (skip_hbm, skip_ref),
            )
        )
    ]
    tails = [
        pltpu.make_async_copy(
            src.at[pl.ds(rows - 16, 16)], tail_ref.at[index], load_sem.at[9 + index]
        )
        for index, src in enumerate((k_hbm, v_hbm, q_hbm))
    ]
    for load in tails + loads:
        load.start()

    barrier = pltpu.get_barrier_semaphore()
    inner = quarter < 3
    linked = (quarter > 0) & (quarter < 3)
    first_of_later = (quarter > 0) & (mine == 0)
    last_of_earlier = (quarter < 3) & (mine == members - 1)

    def tell(sem, to):
        pl.semaphore_signal(sem, inc=1, device_id={"ctx": to}, device_id_type=MESH)

    def greet(k, c):
        tell(barrier, base + lax.rem(mine + k, members))
        return c

    lax.fori_loop(1, members, greet, 0)

    @pl.when(inner)
    def _():
        tell(barrier, me + members)

    @pl.when(last_of_earlier)
    def _():
        tell(barrier, me + 1)

    def build_toep(groups):
        wide = 4 * rows

        def build(g, c):
            upper = lag_ref[:, pl.ds(pl.multiple_of(g * wide, wide), wide)]
            below = jnp.maximum(4 * g - 1, 0)
            lower = lag_ref[:, pl.ds(pl.multiple_of(below * rows, rows), rows)]
            lower = jnp.where(g > 0, lower, 0.0)
            window = jnp.broadcast_to(
                jnp.concatenate([upper, lower], axis=1), (rows, wide + rows)
            )
            turned = pltpu.roll(window, 0, 1, stride=1, stride_axis=0)
            for e in range(4):
                toep[4 * g + e] = turned[:, e * rows : (e + 1) * rows].T.astype(bf16)
            return c

        lax.fori_loop(0, groups, build, 0)

    def border_of():
        listed = jnp.where(pairs_ref[:, 0, :] == 0, pairs_ref[:, 1, :], -1)
        return 1 + jnp.max(jnp.max(listed, axis=1, keepdims=True), axis=0, keepdims=True)

    def build_mix():
        border = border_of()
        early = jnp.where(border <= n // 2, 1.0, 0.0)
        raw = jnp.where(quarter == 1, 1.0, early)
        eye = jnp.where(
            lax.broadcasted_iota(jnp.int32, (rows, rows), 0)
            == lax.broadcasted_iota(jnp.int32, (rows, rows), 1),
            1.0, 0.0,
        ).astype(bf16)

        def live(source, target):
            a = jnp.where(border > source, 1.0, 0.0)
            b = jnp.where(border > target, 1.0, 0.0)
            return 1.0 - jnp.abs(a - b)

        def at(index):
            return pl.ds(pl.multiple_of(index * rows, rows), rows)

        def fill(i, carry):
            def one(j, carry):
                src, dst = base + j, base + i
                causal = jnp.where(j <= i, 1.0, 0.0)
                mix_here[at(i), at(members + j)] = (
                    toep[jnp.maximum(i - j, 0)] * (live(src, dst) * causal).astype(bf16)
                )

                @pl.when(linked)
                def _():
                    passed = (1.0 - raw) * jnp.where(i == j, 1.0, 0.0)
                    near = toep[members + i - j]
                    mix_here[at(i), at(j)] = (
                        near * (raw * live(src - members, dst)).astype(bf16)
                        + eye * passed.astype(bf16)
                    )
                    mix_next[at(i), at(members + j)] = (
                        near * live(src, dst + members).astype(bf16)
                    )
                    mix_next[at(i), at(j)] = (
                        toep[2 * members + i - j]
                        * (raw * live(src - members, dst + members)).astype(bf16)
                    )

                return carry

            return lax.fori_loop(0, members, one, carry)

        lax.fori_loop(0, members, fill, 0)

    def build_all():
        loads[4].wait()
        loads[5].wait()

        @pl.when(linked)
        def _():
            build_toep(3 * members // 4)

        @pl.when(~linked)
        def _():
            build_toep(members // 4)

        build_mix()

    def awaited():
        total = members - 1 + jnp.where(quarter > 0, 1, 0)
        return total + jnp.where(first_of_later, 1, 0)

    pl.semaphore_wait(barrier, awaited())

    @pl.when(quarter > 0)
    def _():
        tell(ready.at[0], me - members)

    @pl.when(first_of_later)
    def _():
        tell(ready.at[1], me - 1)

    def rim_copy(to, part):
        size = 4 * members if part == 0 else rim_out.shape[0] - 4 * members
        at = pl.ds(4 * members * part, size)
        return pltpu.make_async_remote_copy(
            src_ref=rim_out.at[at], dst_ref=rim_in.at[at], send_sem=rim_sem.at[part],
            recv_sem=rim_sem.at[2 + part], device_id={"ctx": to}, device_id_type=MESH,
        )

    def edges(index):
        tail = tail_ref[index].astype(f32)
        for p in range(members):
            for side in range(2):
                at = (2 * index + side) * members + p
                edge[at : at + 1, :] = tail[14 + side : 15 + side, p * share : (p + 1) * share]

    edge[4 * members :, :] = jnp.zeros((edge.shape[0] - 4 * members, share), f32)
    for index in range(2):
        tails[index].wait()
        edges(index)
    rim_out[: 4 * members, :] = edge[: 4 * members, :].astype(bf16)

    @pl.when(mine < members - 1)
    def _():
        rim_copy(me + 1, 0).start()

    tails[2].wait()
    edges(2)
    rim_out[4 * members :, :] = edge[4 * members :, :].astype(bf16)

    @pl.when(mine < members - 1)
    def _():
        rim_copy(me + 1, 1).start()

    @pl.when(last_of_earlier)
    def _():
        pl.semaphore_wait(ready.at[1], 1)
        for part in range(2):
            rim_copy(me + 1, part).start()

    for index in range(3):
        loads[index].wait()

    def spread(first, last):
        size = max(16, (last - first) * members)
        held = rim_in[first * members : first * members + size, :].astype(f32)
        for at in range(first, last):
            for p in range(members):
                from_row = (at - first) * members + p
                rim[at : at + 1, p * share : (p + 1) * share] = held[from_row : from_row + 1, :]

    @pl.when(me == 0)
    def _():
        rim[...] = jnp.zeros_like(rim)

    @pl.when(me > 0)
    def _():
        rim_copy(me - 1, 0).wait_recv()
        spread(0, 4)

    def late_rim():
        @pl.when(me > 0)
        def _():
            rim_copy(me - 1, 1).wait_recv()
            spread(4, 6)

    row = lax.broadcasted_iota(jnp.int32, (rows, width), 0)

    def columns(c, p):
        return pl.ds(pl.multiple_of((p * chunks + c) * width, width), width)

    def feature(ref, index, c, p):
        cols = columns(c, p)
        tap = (index + 1) % 3
        x = ref[:, cols].astype(f32)
        two = rim[2 * index : 2 * index + 1, cols]
        one = rim[2 * index + 1 : 2 * index + 2, cols]
        x1 = jnp.where(row == 0, one, pltpu.roll(x, 1, 0))
        x2 = jnp.where(row == 0, two, jnp.where(row == 1, one, pltpu.roll(x, 2, 0)))
        return (
            taps_ref[tap, 0:1, cols] * x
            + taps_ref[tap, 1:2, cols] * x1
            + taps_ref[tap, 2:3, cols] * x2
        )

    def forward(c, p, sender):
        return pltpu.make_async_remote_copy(
            src_ref=gated.at[c, p], dst_ref=spans.at[c, sender],
            send_sem=sent.at[0], recv_sem=recv1.at[c, jnp.where(sender // 2 == p // 2, 1, 0)],
            device_id={"ctx": base + p}, device_id_type=MESH,
        )

    def backward(c, p, sender):
        return pltpu.make_async_remote_copy(
            src_ref=result.at[c, p], dst_ref=landed.at[c, sender],
            send_sem=sent.at[1], recv_sem=recv2.at[c],
            device_id={"ctx": base + p}, device_id_type=MESH,
        )

    others = pl.ds(0, members - 1)

    def arrived(c, count, mate):
        part = pl.ds(0, count)
        return pltpu.make_async_remote_copy(
            src_ref=gated.at[c, part], dst_ref=spans.at[c, part],
            send_sem=sent.at[0], recv_sem=recv1.at[c, mate],
            device_id={"ctx": base + lax.rem(mine + 1, members)}, device_id_type=MESH,
        )

    def all_backward(c):
        return pltpu.make_async_remote_copy(
            src_ref=result.at[c, others], dst_ref=landed.at[c, others],
            send_sem=sent.at[1], recv_sem=recv2.at[c],
            device_id={"ctx": base + lax.rem(mine + 1, members)}, device_id_type=MESH,
        )

    def raw_copy(c, j):
        return pltpu.make_async_remote_copy(
            src_ref=spans.at[c, j], dst_ref=inbox.at[c, j],
            send_sem=sent.at[2], recv_sem=recv_z.at[c],
            device_id={"ctx": lax.rem(me + members, n)}, device_id_type=MESH,
        )

    def box_copy(c):
        return pltpu.make_async_remote_copy(
            src_ref=outbox.at[c], dst_ref=inbox.at[c],
            send_sem=sent.at[2], recv_sem=recv_z.at[c],
            device_id={"ctx": lax.rem(me + members, n)}, device_id_type=MESH,
        )

    def half_box(c, i):
        both = pl.ds(2 * i, 2)
        return pltpu.make_async_remote_copy(
            src_ref=outbox.at[c, both], dst_ref=inbox.at[c, both],
            send_sem=sent.at[2], recv_sem=recv_z.at[c],
            device_id={"ctx": lax.rem(me + members, n)}, device_id_type=MESH,
        )

    def gate_chunk(c):
        def gate(k, carry):
            p = lax.rem(pair + 2 + k, members)
            value = (feature(k_ref, 0, c, p) * feature(v_ref, 1, c, p)).astype(bf16)
            gated[c, p] = value

            @pl.when(p != mine)
            def _():
                forward(c, p, mine).start()

            @pl.when(p == mine)
            def _():
                spans[c, mine] = value

            return carry

        lax.fori_loop(0, members, gate, 0)

    def relay_chunk(c, whole):
        if whole:
            raw_copy(c, mine).start()
        arrived(c, 1, 1).wait_recv()
        raw_copy(c, 2 * pair + 1 - mine).start()
        arrived(c, members - 2, 0).wait_recv()

        def relay(k, carry):
            raw_copy(c, lax.rem(pair + k, members)).start()
            return carry

        lax.fori_loop(2, members, relay, 0)

    gate_chunk(0)

    @pl.when(inner)
    def _():
        pl.semaphore_wait(ready.at[0], 1)

    @pl.when(quarter == 0)
    def _():
        raw_copy(0, mine).start()

    gate_chunk(1)

    @pl.when(quarter == 0)
    def _():
        relay_chunk(0, False)

    def lead(c, carry):
        gate_chunk(c)
        return carry

    @pl.when(quarter == 0)
    def _():
        lax.fori_loop(2, chunks, lead, 0)

    build_all()

    @pl.when(quarter > 0)
    def _():
        lax.fori_loop(2, chunks, lead, 0)

    late_rim()
    loads[3].wait()
    loads[6].wait()
    loads[7].wait()
    border = border_of()
    early_all = border <= n // 2
    take_raw = early_all & (quarter == 1)
    is_raw = (quarter == 1) | (early_all & (quarter == 2))
    place = lax.broadcasted_iota(jnp.int32, (rows, width), 0).astype(f32)
    tile = 2 * rows

    def finish_chunk(c):
        all_backward(c).wait_recv()

        def finish(p, carry):
            cols = columns(c, p)
            direct = skip_ref[:, cols] * gated[c, p].astype(f32)
            out_ref[:, cols] = (
                qfeat[c, p] * (landed[c, p].astype(f32) + direct)
            ).astype(bf16)
            return carry

        lax.fori_loop(0, members, finish, 0)

    def at(index, size):
        return pl.ds(pl.multiple_of(index * size, size), size)

    lag = jnp.where(quarter == 3, 2, jnp.where(quarter == 0, chunks, 4))

    def step(c, carry):
        @pl.when((quarter == 0) & (c + 1 < chunks))
        def _():
            relay_chunk(c + 1, True)

        rate = decay_ref[:, columns(c, mine)]
        far = jnp.exp(-rate * long)

        def query(p, carry):
            qfeat[c, p] = feature(q_ref, 2, c, p)
            return carry

        lax.fori_loop(0, members, query, 0)

        @pl.when(quarter > 0)
        def _():
            arrived(c, 1, 1).wait_recv()
            arrived(c, members - 2, 0).wait_recv()

        def prepare(j, carry):
            spot = place + (j * rows).astype(f32)
            rise = jnp.exp(rate * spot)
            grow[j] = rise
            fade[j] = jnp.exp(-rate * spot)
            scaled[at(members + j, rows), :] = (spans[c, j].astype(f32) * rise).astype(bf16)
            return carry

        lax.fori_loop(0, members, prepare, 0)

        @pl.when(c >= lag)
        def _():
            finish_chunk(c - lag)

        def own_part(i):
            return jnp.dot(
                mix_here[at(i, tile), long:], scaled[long:, :], preferred_element_type=f32
            )

        @pl.when(quarter == 3)
        def _():
            def target(i, carry):
                acc = own_part(i)
                for side in range(2):
                    j = 2 * i + side
                    grow[j] = acc[side * rows : (side + 1) * rows] * fade[j]
                return carry

            for i in range(members // 2):
                target(i, 0)
            box_copy(c).wait_recv()

        @pl.when(linked)
        def _():
            def before(i, carry):
                acc = jnp.dot(
                    mix_next[at(i, tile), long:], scaled[long:, :], preferred_element_type=f32
                )
                for side in range(2):
                    ahead[2 * i + side] = acc[side * rows : (side + 1) * rows]
                return carry

            for i in range(members // 2):
                before(i, 0)
            box_copy(c).wait_recv()
            drop = jnp.where(is_raw, far, 1.0)

            def receive(j, carry):
                scaled[at(j, rows), :] = (
                    inbox[c, j].astype(f32) * (grow[j] * drop)
                ).astype(bf16)
                return carry

            lax.fori_loop(0, members, receive, 0)

        @pl.when(linked)
        def _():
            def send(i, carry):
                acc = jnp.dot(
                    mix_next[at(i, tile), :long], scaled[:long, :], preferred_element_type=f32
                )
                for side in range(2):
                    j = 2 * i + side
                    value = (ahead[j] + acc[side * rows : (side + 1) * rows]) * (fade[j] * far)
                    raw = spans[c, j].astype(f32)
                    outbox[c, j] = jnp.where(take_raw, raw, value).astype(bf16)
                half_box(c, i).start()
                return carry

            for i in range(members // 2):
                send(i, 0)

        def publish(reader, value):
            value = value.astype(bf16)
            result[c, reader] = value

            @pl.when(reader != mine)
            def _():
                backward(c, reader, mine).start()

            @pl.when(reader == mine)
            def _():
                landed[c, mine] = value

        def publish_both(i, acc):
            for side in range(2):
                reader = 2 * i + side
                publish(reader, acc[side * rows : (side + 1) * rows] * fade[reader])

        @pl.when(quarter == 0)
        def _():
            def target(i, carry):
                publish_both(i, own_part(i))
                return carry

            for i in range(members // 2):
                target(i, 0)

        @pl.when(linked)
        def _():
            def target(i, carry):
                publish_both(i, jnp.dot(
                    mix_here[at(i, tile), :], scaled[...], preferred_element_type=f32
                ))
                return carry

            for i in range(members // 2):
                target(i, 0)

        @pl.when(quarter == 3)
        def _():
            def target(k, carry):
                reader = lax.rem(pair + 2 + k, members)
                publish(reader, grow[reader] + inbox[c, reader].astype(f32))
                return carry

            lax.fori_loop(0, members, target, 0)

        return carry

    lax.fori_loop(0, chunks, step, 0)

    def tail(c, carry):
        finish_chunk(c)
        return carry

    lax.fori_loop(chunks - lag, chunks, tail, 0)

    def everything(src, dst, index, count):
        part = pl.ds(0, count)
        return pltpu.make_async_remote_copy(
            src_ref=src.at[:, part], dst_ref=dst.at[:, part],
            send_sem=sent.at[index], recv_sem=recv1.at[0, 0],
            device_id={"ctx": base + lax.rem(mine + 1, members)}, device_id_type=MESH,
        )

    everything(gated, spans, 0, members - 1).wait_send()
    everything(result, landed, 1, members - 1).wait_send()

    @pl.when(inner)
    def _():
        everything(spans, inbox, 2, members).wait_send()

    @pl.when(me < n - 1)
    def _():
        for part in range(2):
            rim_copy(me + 1, part).wait_send()


def hand_over(src_ref, dst_ref, sem):
    copy = pltpu.make_async_copy(src_ref, dst_ref, sem.at[0])
    copy.start()
    copy.wait()


def on_device(
    query_rows, key_rows, value_rows, conv_taps, decay_rate, lag_profile, skip_gain, pair_lists
):
    rows, channels = query_rows.shape
    n = lax.axis_size("ctx")
    members = n // 4
    share = channels // members
    width = WIDTH
    chunks = share // width
    long = members * rows
    pairs = pair_lists.transpose(1, 2, 0)
    hbm = pl.BlockSpec(memory_space=pltpu.HBM)
    bf16, f32 = jnp.bfloat16, jnp.float32
    piece = (chunks, members, rows, width)
    edges = 4 * members + max(16, 2 * members)
    dma = pltpu.SemaphoreType.DMA
    held = pl.pallas_call(
        functools.partial(kernel, n, rows, chunks, width),
        out_shape=pltpu.VMEM((rows, channels), bf16),
        in_specs=[hbm] * 8,
        out_specs=pl.BlockSpec(memory_space=pltpu.VMEM),
        scratch_shapes=[
            pltpu.VMEM((rows, channels), bf16),
            pltpu.VMEM((rows, channels), bf16),
            pltpu.VMEM((rows, channels), bf16),
            pltpu.VMEM(conv_taps.shape, f32),
            pltpu.VMEM((1, channels), f32),
            pltpu.VMEM((1, lag_profile.shape[0]), f32),
            pltpu.VMEM((1, channels), f32),
            pltpu.VMEM(pairs.shape, jnp.int32),
            pltpu.VMEM((3, 16, channels), bf16),
            pltpu.VMEM((edges, share), f32),
            pltpu.VMEM((edges, share), bf16),
            pltpu.VMEM((edges, share), bf16),
            pltpu.VMEM((8, channels), f32),
            pltpu.VMEM(piece, bf16),
            pltpu.VMEM(piece, f32),
            pltpu.VMEM(piece, bf16),
            pltpu.VMEM(piece, bf16),
            pltpu.VMEM(piece, bf16),
            pltpu.VMEM((3 * members, rows, rows), bf16),
            pltpu.VMEM((long, 2 * long), bf16),
            pltpu.VMEM((long, 2 * long), bf16),
            pltpu.VMEM((2 * long, width), bf16),
            pltpu.VMEM((members, rows, width), f32),
            pltpu.VMEM((members, rows, width), f32),
            pltpu.VMEM((members, rows, width), f32),
            pltpu.VMEM(piece, bf16),
            pltpu.VMEM(piece, bf16),
            dma((12,)),
            dma((4,)),
            dma((3,)),
            dma((chunks, 2)),
            dma((chunks,)),
            dma((chunks,)),
            pltpu.SemaphoreType.REGULAR((2,)),
        ],
        compiler_params=pltpu.CompilerParams(
            collective_id=0, has_side_effects=True, vmem_limit_bytes=62 * 1024 * 1024
        ),
    )(
        query_rows, key_rows, value_rows, conv_taps, decay_rate.reshape(1, -1),
        lag_profile.reshape(1, -1), skip_gain.reshape(1, -1), pairs,
    )
    return pl.pallas_call(
        hand_over,
        out_shape=jax.ShapeDtypeStruct((rows, channels), bf16),
        in_specs=[pl.BlockSpec(memory_space=pltpu.VMEM)],
        out_specs=hbm,
        scratch_shapes=[dma((1,))],
        compiler_params=pltpu.CompilerParams(vmem_limit_bytes=1024 * 1024),
    )(held)


def solution(mesh):
    rows = P(("group", "ctx"), None)
    return jax.shard_map(
        on_device,
        mesh=mesh,
        in_specs=(rows, rows, rows, P(), P(), P(), P(), P("group", None, None)),
        out_specs=rows,
        check_vma=False,
    )
```

```python
import functools

import jax
import jax.numpy as jnp
from jax import lax
from jax.experimental import pallas as pl
from jax.experimental.pallas import tpu as pltpu
from jax.sharding import PartitionSpec as P

MESH = pl.DeviceIdType.MESH
WIDTH = 128
STRIPS = 8


def kernel(
    n, rows, chunks, width,
    q_hbm, k_hbm, v_hbm, taps_hbm, decay_hbm, lag_hbm, skip_hbm, pairs_hbm,
    out_ref, q_ref, k_ref, v_ref, taps_ref, decay_ref, lag_ref, skip_ref, pairs_ref,
    tail_ref, edge, rim_out, rim_in, rim, gated, qfeat, spans, inbox, outbox, toep, mix_here, mix_next,
    scaled, grow, fade, ahead, result, landed,
    load_sem, rim_sem, sent, recv1, recv_z, recv2, ready,
):
    me = lax.axis_index("ctx")
    members = n // 4
    quarter = me // members
    base = quarter * members
    mine = me - base
    pair = 2 * (mine // 2)
    long = members * rows
    share = chunks * width
    f32, bf16 = jnp.float32, jnp.bfloat16

    loads = [
        pltpu.make_async_copy(src, dst, load_sem.at[index])
        for index, (src, dst) in enumerate(
            (
                (k_hbm, k_ref), (v_hbm, v_ref), (taps_hbm, taps_ref), (q_hbm, q_ref),
                (lag_hbm, lag_ref), (pairs_hbm, pairs_ref), (decay_hbm, decay_ref),
                (skip_hbm, skip_ref),
            )
        )
    ]
    tails = [
        pltpu.make_async_copy(
            src.at[pl.ds(rows - 16, 16)], tail_ref.at[index], load_sem.at[9 + index]
        )
        for index, src in enumerate((k_hbm, v_hbm, q_hbm))
    ]
    for load in tails + loads:
        load.start()

    barrier = pltpu.get_barrier_semaphore()
    inner = quarter < 3
    linked = (quarter > 0) & (quarter < 3)
    first_of_later = (quarter > 0) & (mine == 0)
    last_of_earlier = (quarter < 3) & (mine == members - 1)

    def tell(sem, to):
        pl.semaphore_signal(sem, inc=1, device_id={"ctx": to}, device_id_type=MESH)

    def greet(k, c):
        tell(barrier, base + lax.rem(mine + k, members))
        return c

    lax.fori_loop(1, members, greet, 0)

    @pl.when(inner)
    def _():
        tell(barrier, me + members)

    @pl.when(first_of_later)
    def _():
        tell(barrier, me - 1)

    def build_toep(groups):
        wide = 4 * rows

        def build(g, c):
            upper = lag_ref[:, pl.ds(pl.multiple_of(g * wide, wide), wide)]
            below = jnp.maximum(4 * g - 1, 0)
            lower = lag_ref[:, pl.ds(pl.multiple_of(below * rows, rows), rows)]
            lower = jnp.where(g > 0, lower, 0.0)
            window = jnp.broadcast_to(
                jnp.concatenate([upper, lower], axis=1), (rows, wide + rows)
            )
            turned = pltpu.roll(window, 0, 1, stride=1, stride_axis=0)
            for e in range(4):
                toep[4 * g + e] = turned[:, e * rows : (e + 1) * rows].T.astype(bf16)
            return c

        lax.fori_loop(0, groups, build, 0)

    def border_of():
        listed = jnp.where(pairs_ref[:, 0, :] == 0, pairs_ref[:, 1, :], -1)
        return 1 + jnp.max(jnp.max(listed, axis=1, keepdims=True), axis=0, keepdims=True)

    def build_mix():
        border = border_of()
        early = jnp.where(border <= n // 2, 1.0, 0.0)
        raw = jnp.where(quarter == 1, 1.0, early)
        eye = jnp.where(
            lax.broadcasted_iota(jnp.int32, (rows, rows), 0)
            == lax.broadcasted_iota(jnp.int32, (rows, rows), 1),
            1.0, 0.0,
        ).astype(bf16)

        def live(source, target):
            a = jnp.where(border > source, 1.0, 0.0)
            b = jnp.where(border > target, 1.0, 0.0)
            return 1.0 - jnp.abs(a - b)

        def at(index):
            return pl.ds(pl.multiple_of(index * rows, rows), rows)

        def fill(i, carry):
            def one(j, carry):
                src, dst = base + j, base + i
                causal = jnp.where(j <= i, 1.0, 0.0)
                mix_here[at(i), at(members + j)] = (
                    toep[jnp.maximum(i - j, 0)] * (live(src, dst) * causal).astype(bf16)
                )

                @pl.when(linked)
                def _():
                    passed = (1.0 - raw) * jnp.where(i == j, 1.0, 0.0)
                    near = toep[members + i - j]
                    mix_here[at(i), at(j)] = (
                        near * (raw * live(src - members, dst)).astype(bf16)
                        + eye * passed.astype(bf16)
                    )
                    mix_next[at(i), at(members + j)] = (
                        near * live(src, dst + members).astype(bf16)
                    )
                    mix_next[at(i), at(j)] = (
                        toep[2 * members + i - j]
                        * (raw * live(src - members, dst + members)).astype(bf16)
                    )

                return carry

            return lax.fori_loop(0, members, one, carry)

        lax.fori_loop(0, members, fill, 0)

    def build_all():
        loads[4].wait()
        loads[5].wait()

        @pl.when(linked)
        def _():
            build_toep(3 * members // 4)

        @pl.when(~linked)
        def _():
            build_toep(members // 4)

        build_mix()

    def awaited():
        total = members - 1 + jnp.where(quarter > 0, 1, 0)
        return total + jnp.where(last_of_earlier, 1, 0)

    pl.semaphore_wait(barrier, awaited())

    @pl.when(quarter > 0)
    def _():
        tell(ready.at[0], me - members)

    def rim_copy(to, part):
        size = 4 * members if part == 0 else rim_out.shape[0] - 4 * members
        at = pl.ds(4 * members * part, size)
        return pltpu.make_async_remote_copy(
            src_ref=rim_out.at[at], dst_ref=rim_in.at[at], send_sem=rim_sem.at[part],
            recv_sem=rim_sem.at[2 + part], device_id={"ctx": to}, device_id_type=MESH,
        )

    def edges(index):
        tail = tail_ref[index].astype(f32)
        for p in range(members):
            for side in range(2):
                at = (2 * index + side) * members + p
                edge[at : at + 1, :] = tail[14 + side : 15 + side, p * share : (p + 1) * share]

    edge[4 * members :, :] = jnp.zeros((edge.shape[0] - 4 * members, share), f32)
    for index in range(2):
        tails[index].wait()
        edges(index)
    rim_out[: 4 * members, :] = edge[: 4 * members, :].astype(bf16)

    @pl.when(mine < members - 1)
    def _():
        rim_copy(me + 1, 0).start()

    tails[2].wait()
    edges(2)
    rim_out[4 * members :, :] = edge[4 * members :, :].astype(bf16)

    @pl.when(mine < members - 1)
    def _():
        rim_copy(me + 1, 1).start()

    @pl.when(last_of_earlier)
    def _():
        for part in range(2):
            rim_copy(me + 1, part).start()

    for index in range(3):
        loads[index].wait()

    def spread(first, last):
        size = max(16, (last - first) * members)
        held = rim_in[first * members : first * members + size, :].astype(f32)
        for at in range(first, last):
            for p in range(members):
                from_row = (at - first) * members + p
                rim[at : at + 1, p * share : (p + 1) * share] = held[from_row : from_row + 1, :]

    @pl.when(me == 0)
    def _():
        rim[...] = jnp.zeros_like(rim)

    @pl.when(me > 0)
    def _():
        rim_copy(me - 1, 0).wait_recv()
        spread(0, 4)

    def late_rim():
        @pl.when(me > 0)
        def _():
            rim_copy(me - 1, 1).wait_recv()
            spread(4, 6)

    row = lax.broadcasted_iota(jnp.int32, (rows, width), 0)

    def columns(c, p):
        return pl.ds(pl.multiple_of((p * chunks + c) * width, width), width)

    def feature(ref, index, c, p):
        cols = columns(c, p)
        tap = (index + 1) % 3
        x = ref[:, cols].astype(f32)
        two = rim[2 * index : 2 * index + 1, cols]
        one = rim[2 * index + 1 : 2 * index + 2, cols]
        x1 = jnp.where(row == 0, one, pltpu.roll(x, 1, 0))
        x2 = jnp.where(row == 0, two, jnp.where(row == 1, one, pltpu.roll(x, 2, 0)))
        return (
            taps_ref[tap, 0:1, cols] * x
            + taps_ref[tap, 1:2, cols] * x1
            + taps_ref[tap, 2:3, cols] * x2
        )

    def forward(c, p, sender):
        return pltpu.make_async_remote_copy(
            src_ref=gated.at[c, p], dst_ref=spans.at[c, sender],
            send_sem=sent.at[0], recv_sem=recv1.at[c, jnp.where(sender // 2 == p // 2, 1, 0)],
            device_id={"ctx": base + p}, device_id_type=MESH,
        )

    def backward(c, p, sender):
        return pltpu.make_async_remote_copy(
            src_ref=result.at[c, p], dst_ref=landed.at[c, sender],
            send_sem=sent.at[1], recv_sem=recv2.at[c],
            device_id={"ctx": base + p}, device_id_type=MESH,
        )

    others = pl.ds(0, members - 1)

    def arrived(c, count, mate):
        part = pl.ds(0, count)
        return pltpu.make_async_remote_copy(
            src_ref=gated.at[c, part], dst_ref=spans.at[c, part],
            send_sem=sent.at[0], recv_sem=recv1.at[c, mate],
            device_id={"ctx": base + lax.rem(mine + 1, members)}, device_id_type=MESH,
        )

    def all_backward(c):
        return pltpu.make_async_remote_copy(
            src_ref=result.at[c, others], dst_ref=landed.at[c, others],
            send_sem=sent.at[1], recv_sem=recv2.at[c],
            device_id={"ctx": base + lax.rem(mine + 1, members)}, device_id_type=MESH,
        )

    def raw_copy(c, j):
        return pltpu.make_async_remote_copy(
            src_ref=spans.at[c, j], dst_ref=inbox.at[c, j],
            send_sem=sent.at[2], recv_sem=recv_z.at[c],
            device_id={"ctx": lax.rem(me + members, n)}, device_id_type=MESH,
        )

    def box_copy(c):
        return pltpu.make_async_remote_copy(
            src_ref=outbox.at[c], dst_ref=inbox.at[c],
            send_sem=sent.at[2], recv_sem=recv_z.at[c],
            device_id={"ctx": lax.rem(me + members, n)}, device_id_type=MESH,
        )

    def half_box(c, i):
        both = pl.ds(2 * i, 2)
        return pltpu.make_async_remote_copy(
            src_ref=outbox.at[c, both], dst_ref=inbox.at[c, both],
            send_sem=sent.at[2], recv_sem=recv_z.at[c],
            device_id={"ctx": lax.rem(me + members, n)}, device_id_type=MESH,
        )

    def gate_chunk(c):
        def gate(k, carry):
            p = lax.rem(pair + 2 + k, members)
            value = (feature(k_ref, 0, c, p) * feature(v_ref, 1, c, p)).astype(bf16)
            gated[c, p] = value

            @pl.when(p != mine)
            def _():
                forward(c, p, mine).start()

            @pl.when(p == mine)
            def _():
                spans[c, mine] = value

            return carry

        lax.fori_loop(0, members, gate, 0)

    def relay_chunk(c, whole):
        if whole:
            raw_copy(c, mine).start()
        arrived(c, 1, 1).wait_recv()
        raw_copy(c, 2 * pair + 1 - mine).start()
        arrived(c, members - 2, 0).wait_recv()

        def relay(k, carry):
            raw_copy(c, lax.rem(pair + k, members)).start()
            return carry

        lax.fori_loop(2, members, relay, 0)

    gate_chunk(0)

    @pl.when(inner)
    def _():
        pl.semaphore_wait(ready.at[0], 1)

    @pl.when(quarter == 0)
    def _():
        raw_copy(0, mine).start()

    gate_chunk(1)

    @pl.when(quarter == 0)
    def _():
        relay_chunk(0, False)

    def lead(c, carry):
        gate_chunk(c)
        return carry

    front = jnp.where(quarter == 0, 2, jnp.where(quarter == 1, 2, jnp.where(quarter == 2, 3, 8)))
    front = jnp.minimum(front, chunks)

    @pl.when(quarter == 0)
    def _():
        lax.fori_loop(2, front, lead, 0)

    build_all()

    @pl.when(quarter > 0)
    def _():
        lax.fori_loop(2, front, lead, 0)

    late_rim()
    loads[3].wait()
    loads[6].wait()
    loads[7].wait()
    border = border_of()
    early_all = border <= n // 2
    take_raw = early_all & (quarter == 1)
    is_raw = (quarter == 1) | (early_all & (quarter == 2))
    place = lax.broadcasted_iota(jnp.int32, (rows, width), 0).astype(f32)
    tile = 2 * rows

    def finish_chunk(c):
        all_backward(c).wait_recv()

        def finish(p, carry):
            cols = columns(c, p)
            direct = skip_ref[:, cols] * gated[c, p].astype(f32)
            out_ref[:, cols] = (
                qfeat[c, p] * (landed[c, p].astype(f32) + direct)
            ).astype(bf16)
            return carry

        lax.fori_loop(0, members, finish, 0)

    def at(index, size):
        return pl.ds(pl.multiple_of(index * size, size), size)

    lag = jnp.where(quarter == 3, 2, jnp.where(quarter == 0, chunks, 4))

    def step(c, carry):
        @pl.when(c + front < chunks)
        def _():
            gate_chunk(c + front)

        @pl.when((quarter == 0) & (c + 1 < chunks))
        def _():
            relay_chunk(c + 1, True)

        rate = decay_ref[:, columns(c, mine)]
        far = jnp.exp(-rate * long)

        def query(p, carry):
            qfeat[c, p] = feature(q_ref, 2, c, p)
            return carry

        lax.fori_loop(0, members, query, 0)

        @pl.when(quarter > 0)
        def _():
            arrived(c, 1, 1).wait_recv()
            arrived(c, members - 2, 0).wait_recv()

        def prepare(j, carry):
            spot = place + (j * rows).astype(f32)
            rise = jnp.exp(rate * spot)
            grow[j] = rise
            fade[j] = jnp.exp(-rate * spot)
            scaled[at(members + j, rows), :] = (spans[c, j].astype(f32) * rise).astype(bf16)
            return carry

        lax.fori_loop(0, members, prepare, 0)

        @pl.when(c >= lag)
        def _():
            finish_chunk(c - lag)

        def own_part(i):
            return jnp.dot(
                mix_here[at(i, tile), long:], scaled[long:, :], preferred_element_type=f32
            )

        @pl.when(quarter == 3)
        def _():
            def target(i, carry):
                acc = own_part(i)
                for side in range(2):
                    j = 2 * i + side
                    grow[j] = acc[side * rows : (side + 1) * rows] * fade[j]
                return carry

            for i in range(members // 2):
                target(i, 0)
            box_copy(c).wait_recv()

        @pl.when(linked)
        def _():
            def before(i, carry):
                acc = jnp.dot(
                    mix_next[at(i, tile), long:], scaled[long:, :], preferred_element_type=f32
                )
                for side in range(2):
                    ahead[2 * i + side] = acc[side * rows : (side + 1) * rows]
                return carry

            for i in range(members // 2):
                before(i, 0)
            box_copy(c).wait_recv()
            drop = jnp.where(is_raw, far, 1.0)

            def receive(j, carry):
                scaled[at(j, rows), :] = (
                    inbox[c, j].astype(f32) * (grow[j] * drop)
                ).astype(bf16)
                return carry

            lax.fori_loop(0, members, receive, 0)

        @pl.when(linked)
        def _():
            def send(i, carry):
                acc = jnp.dot(
                    mix_next[at(i, tile), :long], scaled[:long, :], preferred_element_type=f32
                )
                for side in range(2):
                    j = 2 * i + side
                    value = (ahead[j] + acc[side * rows : (side + 1) * rows]) * (fade[j] * far)
                    raw = spans[c, j].astype(f32)
                    outbox[c, j] = jnp.where(take_raw, raw, value).astype(bf16)
                half_box(c, i).start()
                return carry

            for i in range(members // 2):
                send(i, 0)

        def publish(reader, value):
            value = value.astype(bf16)
            result[c, reader] = value

            @pl.when(reader != mine)
            def _():
                backward(c, reader, mine).start()

            @pl.when(reader == mine)
            def _():
                landed[c, mine] = value

        def publish_both(i, acc):
            for side in range(2):
                reader = 2 * i + side
                publish(reader, acc[side * rows : (side + 1) * rows] * fade[reader])

        @pl.when(quarter == 0)
        def _():
            def target(i, carry):
                publish_both(i, own_part(i))
                return carry

            for i in range(members // 2):
                target(i, 0)

        @pl.when(linked)
        def _():
            def target(i, carry):
                publish_both(i, jnp.dot(
                    mix_here[at(i, tile), :], scaled[...], preferred_element_type=f32
                ))
                return carry

            for i in range(members // 2):
                target(i, 0)

        @pl.when(quarter == 3)
        def _():
            def target(k, carry):
                reader = lax.rem(pair + 2 + k, members)
                publish(reader, grow[reader] + inbox[c, reader].astype(f32))
                return carry

            lax.fori_loop(0, members, target, 0)

        return carry

    lax.fori_loop(0, chunks, step, 0)

    def tail(c, carry):
        finish_chunk(c)
        return carry

    lax.fori_loop(chunks - lag, chunks, tail, 0)

    def everything(src, dst, index, count):
        part = pl.ds(0, count)
        return pltpu.make_async_remote_copy(
            src_ref=src.at[:, part], dst_ref=dst.at[:, part],
            send_sem=sent.at[index], recv_sem=recv1.at[0, 0],
            device_id={"ctx": base + lax.rem(mine + 1, members)}, device_id_type=MESH,
        )

    everything(gated, spans, 0, members - 1).wait_send()
    everything(result, landed, 1, members - 1).wait_send()

    @pl.when(inner)
    def _():
        everything(spans, inbox, 2, members).wait_send()

    @pl.when(me < n - 1)
    def _():
        for part in range(2):
            rim_copy(me + 1, part).wait_send()


def hand_over(src_ref, dst_ref, sem):
    copy = pltpu.make_async_copy(src_ref, dst_ref, sem.at[0])
    copy.start()
    copy.wait()


def on_device(
    query_rows, key_rows, value_rows, conv_taps, decay_rate, lag_profile, skip_gain, pair_lists
):
    rows, channels = query_rows.shape
    n = lax.axis_size("ctx")
    members = n // 4
    share = channels // members
    width = WIDTH
    chunks = share // width
    long = members * rows
    pairs = pair_lists.transpose(1, 2, 0)
    hbm = pl.BlockSpec(memory_space=pltpu.HBM)
    bf16, f32 = jnp.bfloat16, jnp.float32
    piece = (chunks, members, rows, width)
    edges = 4 * members + max(16, 2 * members)
    dma = pltpu.SemaphoreType.DMA
    held = pl.pallas_call(
        functools.partial(kernel, n, rows, chunks, width),
        out_shape=pltpu.VMEM((rows, channels), bf16),
        in_specs=[hbm] * 8,
        out_specs=pl.BlockSpec(memory_space=pltpu.VMEM),
        scratch_shapes=[
            pltpu.VMEM((rows, channels), bf16),
            pltpu.VMEM((rows, channels), bf16),
            pltpu.VMEM((rows, channels), bf16),
            pltpu.VMEM(conv_taps.shape, f32),
            pltpu.VMEM((1, channels), f32),
            pltpu.VMEM((1, lag_profile.shape[0]), f32),
            pltpu.VMEM((1, channels), f32),
            pltpu.VMEM(pairs.shape, jnp.int32),
            pltpu.VMEM((3, 16, channels), bf16),
            pltpu.VMEM((edges, share), f32),
            pltpu.VMEM((edges, share), bf16),
            pltpu.VMEM((edges, share), bf16),
            pltpu.VMEM((8, channels), f32),
            pltpu.VMEM(piece, bf16),
            pltpu.VMEM(piece, f32),
            pltpu.VMEM(piece, bf16),
            pltpu.VMEM(piece, bf16),
            pltpu.VMEM(piece, bf16),
            pltpu.VMEM((3 * members, rows, rows), bf16),
            pltpu.VMEM((long, 2 * long), bf16),
            pltpu.VMEM((long, 2 * long), bf16),
            pltpu.VMEM((2 * long, width), bf16),
            pltpu.VMEM((members, rows, width), f32),
            pltpu.VMEM((members, rows, width), f32),
            pltpu.VMEM((members, rows, width), f32),
            pltpu.VMEM(piece, bf16),
            pltpu.VMEM(piece, bf16),
            dma((12,)),
            dma((4,)),
            dma((3,)),
            dma((chunks, 2)),
            dma((chunks,)),
            dma((chunks,)),
            pltpu.SemaphoreType.REGULAR((1,)),
        ],
        compiler_params=pltpu.CompilerParams(
            collective_id=0, has_side_effects=True, vmem_limit_bytes=62 * 1024 * 1024
        ),
    )(
        query_rows, key_rows, value_rows, conv_taps, decay_rate.reshape(1, -1),
        lag_profile.reshape(1, -1), skip_gain.reshape(1, -1), pairs,
    )
    return pl.pallas_call(
        hand_over,
        out_shape=jax.ShapeDtypeStruct((rows, channels), bf16),
        in_specs=[pl.BlockSpec(memory_space=pltpu.VMEM)],
        out_specs=hbm,
        scratch_shapes=[dma((1,))],
        compiler_params=pltpu.CompilerParams(vmem_limit_bytes=1024 * 1024),
    )(held)


def solution(mesh):
    rows = P(("group", "ctx"), None)
    return jax.shard_map(
        on_device,
        mesh=mesh,
        in_specs=(rows, rows, rows, P(), P(), P(), P(), P("group", None, None)),
        out_specs=rows,
        check_vma=False,
    )
```

```python
import functools

import jax
import jax.numpy as jnp
from jax import lax
from jax.experimental import pallas as pl
from jax.experimental.pallas import tpu as pltpu
from jax.sharding import PartitionSpec as P

MESH = pl.DeviceIdType.MESH
WIDTH = 128
STRIPS = 8


def kernel(
    n, rows, chunks, width,
    q_hbm, k_hbm, v_hbm, taps_hbm, decay_hbm, lag_hbm, skip_hbm, pairs_hbm,
    out_ref, q_ref, k_ref, v_ref, taps_ref, decay_ref, lag_ref, skip_ref, pairs_ref,
    tail_ref, edge, rim_out, rim_in, rim, gated, qfeat, spans, inbox, outbox, toep, mix_here, mix_next,
    scaled, grow, fade, ahead, result, landed,
    load_sem, rim_sem, sent, recv1, recv_z, recv2, ready,
):
    me = lax.axis_index("ctx")
    members = n // 4
    quarter = me // members
    base = quarter * members
    mine = me - base
    pair = 2 * (mine // 2)
    long = members * rows
    share = chunks * width
    f32, bf16 = jnp.float32, jnp.bfloat16

    loads = [
        pltpu.make_async_copy(src, dst, load_sem.at[index])
        for index, (src, dst) in enumerate(
            (
                (k_hbm, k_ref), (v_hbm, v_ref), (taps_hbm, taps_ref), (q_hbm, q_ref),
                (lag_hbm, lag_ref), (pairs_hbm, pairs_ref), (decay_hbm, decay_ref),
                (skip_hbm, skip_ref),
            )
        )
    ]
    tails = [
        pltpu.make_async_copy(
            src.at[pl.ds(rows - 16, 16)], tail_ref.at[index], load_sem.at[9 + index]
        )
        for index, src in enumerate((k_hbm, v_hbm, q_hbm))
    ]
    for load in tails + loads:
        load.start()

    barrier = pltpu.get_barrier_semaphore()
    inner = quarter < 3
    linked = (quarter > 0) & (quarter < 3)
    first_of_later = (quarter > 0) & (mine == 0)
    last_of_earlier = (quarter < 3) & (mine == members - 1)

    def tell(sem, to):
        pl.semaphore_signal(sem, inc=1, device_id={"ctx": to}, device_id_type=MESH)

    def greet(k, c):
        tell(barrier, base + lax.rem(mine + k, members))
        return c

    lax.fori_loop(1, members, greet, 0)

    @pl.when(inner)
    def _():
        tell(barrier, me + members)

    @pl.when(first_of_later)
    def _():
        tell(barrier, me - 1)

    def build_toep(groups):
        wide = 4 * rows

        def build(g, c):
            upper = lag_ref[:, pl.ds(pl.multiple_of(g * wide, wide), wide)]
            below = jnp.maximum(4 * g - 1, 0)
            lower = lag_ref[:, pl.ds(pl.multiple_of(below * rows, rows), rows)]
            lower = jnp.where(g > 0, lower, 0.0)
            window = jnp.broadcast_to(
                jnp.concatenate([upper, lower], axis=1), (rows, wide + rows)
            )
            turned = pltpu.roll(window, 0, 1, stride=1, stride_axis=0)
            for e in range(4):
                toep[4 * g + e] = turned[:, e * rows : (e + 1) * rows].T.astype(bf16)
            return c

        lax.fori_loop(0, groups, build, 0)

    def border_of():
        listed = jnp.where(pairs_ref[:, 0, :] == 0, pairs_ref[:, 1, :], -1)
        return 1 + jnp.max(jnp.max(listed, axis=1, keepdims=True), axis=0, keepdims=True)

    def build_mix():
        border = border_of()
        early = jnp.where(border <= n // 2, 1.0, 0.0)
        raw = jnp.where(quarter == 1, 1.0, early)
        eye = jnp.where(
            lax.broadcasted_iota(jnp.int32, (rows, rows), 0)
            == lax.broadcasted_iota(jnp.int32, (rows, rows), 1),
            1.0, 0.0,
        ).astype(bf16)

        def live(source, target):
            a = jnp.where(border > source, 1.0, 0.0)
            b = jnp.where(border > target, 1.0, 0.0)
            return 1.0 - jnp.abs(a - b)

        def at(index):
            return pl.ds(pl.multiple_of(index * rows, rows), rows)

        def fill(i, carry):
            def one(j, carry):
                src, dst = base + j, base + i
                causal = jnp.where(j <= i, 1.0, 0.0)
                mix_here[at(i), at(members + j)] = (
                    toep[jnp.maximum(i - j, 0)] * (live(src, dst) * causal).astype(bf16)
                )

                @pl.when(linked)
                def _():
                    passed = (1.0 - raw) * jnp.where(i == j, 1.0, 0.0)
                    near = toep[members + i - j]
                    mix_here[at(i), at(j)] = (
                        near * (raw * live(src - members, dst)).astype(bf16)
                        + eye * passed.astype(bf16)
                    )
                    mix_next[at(i), at(members + j)] = (
                        near * live(src, dst + members).astype(bf16)
                    )
                    mix_next[at(i), at(j)] = (
                        toep[2 * members + i - j]
                        * (raw * live(src - members, dst + members)).astype(bf16)
                    )

                return carry

            return lax.fori_loop(0, members, one, carry)

        lax.fori_loop(0, members, fill, 0)

    def build_all():
        loads[4].wait()
        loads[5].wait()

        @pl.when(linked)
        def _():
            build_toep(3 * members // 4)

        @pl.when(~linked)
        def _():
            build_toep(members // 4)

        build_mix()

    def awaited():
        total = members - 1 + jnp.where(quarter > 0, 1, 0)
        return total + jnp.where(last_of_earlier, 1, 0)

    pl.semaphore_wait(barrier, awaited())

    @pl.when(quarter > 0)
    def _():
        tell(ready.at[0], me - members)

    def rim_copy(to, part):
        size = 4 * members if part == 0 else rim_out.shape[0] - 4 * members
        at = pl.ds(4 * members * part, size)
        return pltpu.make_async_remote_copy(
            src_ref=rim_out.at[at], dst_ref=rim_in.at[at], send_sem=rim_sem.at[part],
            recv_sem=rim_sem.at[2 + part], device_id={"ctx": to}, device_id_type=MESH,
        )

    def edges(index):
        tail = tail_ref[index].astype(f32)
        for p in range(members):
            for side in range(2):
                at = (2 * index + side) * members + p
                edge[at : at + 1, :] = tail[14 + side : 15 + side, p * share : (p + 1) * share]

    edge[4 * members :, :] = jnp.zeros((edge.shape[0] - 4 * members, share), f32)
    for index in range(2):
        tails[index].wait()
        edges(index)
    rim_out[: 4 * members, :] = edge[: 4 * members, :].astype(bf16)

    @pl.when(mine < members - 1)
    def _():
        rim_copy(me + 1, 0).start()

    tails[2].wait()
    edges(2)
    rim_out[4 * members :, :] = edge[4 * members :, :].astype(bf16)

    @pl.when(mine < members - 1)
    def _():
        rim_copy(me + 1, 1).start()

    @pl.when(last_of_earlier)
    def _():
        for part in range(2):
            rim_copy(me + 1, part).start()

    for index in range(3):
        loads[index].wait()

    def spread(first, last):
        size = max(16, (last - first) * members)
        held = rim_in[first * members : first * members + size, :].astype(f32)
        for at in range(first, last):
            for p in range(members):
                from_row = (at - first) * members + p
                rim[at : at + 1, p * share : (p + 1) * share] = held[from_row : from_row + 1, :]

    @pl.when(me == 0)
    def _():
        rim[...] = jnp.zeros_like(rim)

    @pl.when(me > 0)
    def _():
        rim_copy(me - 1, 0).wait_recv()
        spread(0, 4)

    def late_rim():
        @pl.when(me > 0)
        def _():
            rim_copy(me - 1, 1).wait_recv()
            spread(4, 6)

    row = lax.broadcasted_iota(jnp.int32, (rows, width), 0)

    def columns(c, p):
        return pl.ds(pl.multiple_of((p * chunks + c) * width, width), width)

    def feature(ref, index, c, p):
        cols = columns(c, p)
        tap = (index + 1) % 3
        x = ref[:, cols].astype(f32)
        two = rim[2 * index : 2 * index + 1, cols]
        one = rim[2 * index + 1 : 2 * index + 2, cols]
        x1 = jnp.where(row == 0, one, pltpu.roll(x, 1, 0))
        x2 = jnp.where(row == 0, two, jnp.where(row == 1, one, pltpu.roll(x, 2, 0)))
        return (
            taps_ref[tap, 0:1, cols] * x
            + taps_ref[tap, 1:2, cols] * x1
            + taps_ref[tap, 2:3, cols] * x2
        )

    def forward(c, p, sender):
        return pltpu.make_async_remote_copy(
            src_ref=gated.at[c, p], dst_ref=spans.at[c, sender],
            send_sem=sent.at[0], recv_sem=recv1.at[c, jnp.where(sender // 2 == p // 2, 1, 0)],
            device_id={"ctx": base + p}, device_id_type=MESH,
        )

    def backward(c, p, sender):
        return pltpu.make_async_remote_copy(
            src_ref=result.at[c, p], dst_ref=landed.at[c, sender],
            send_sem=sent.at[1], recv_sem=recv2.at[c],
            device_id={"ctx": base + p}, device_id_type=MESH,
        )

    others = pl.ds(0, members - 1)

    def arrived(c, count, mate):
        part = pl.ds(0, count)
        return pltpu.make_async_remote_copy(
            src_ref=gated.at[c, part], dst_ref=spans.at[c, part],
            send_sem=sent.at[0], recv_sem=recv1.at[c, mate],
            device_id={"ctx": base + lax.rem(mine + 1, members)}, device_id_type=MESH,
        )

    def all_backward(c):
        return pltpu.make_async_remote_copy(
            src_ref=result.at[c, others], dst_ref=landed.at[c, others],
            send_sem=sent.at[1], recv_sem=recv2.at[c],
            device_id={"ctx": base + lax.rem(mine + 1, members)}, device_id_type=MESH,
        )

    def raw_copy(c, j):
        return pltpu.make_async_remote_copy(
            src_ref=spans.at[c, j], dst_ref=inbox.at[c, j],
            send_sem=sent.at[2], recv_sem=recv_z.at[c],
            device_id={"ctx": lax.rem(me + members, n)}, device_id_type=MESH,
        )

    def box_copy(c):
        return pltpu.make_async_remote_copy(
            src_ref=outbox.at[c], dst_ref=inbox.at[c],
            send_sem=sent.at[2], recv_sem=recv_z.at[c],
            device_id={"ctx": lax.rem(me + members, n)}, device_id_type=MESH,
        )

    def part_copy(c, j):
        return pltpu.make_async_remote_copy(
            src_ref=outbox.at[c, j], dst_ref=inbox.at[c, mine],
            send_sem=sent.at[2], recv_sem=recv_z.at[c],
            device_id={"ctx": lax.rem(base + members + j, n)}, device_id_type=MESH,
        )

    def half_box(c, i):
        both = pl.ds(2 * i, 2)
        return pltpu.make_async_remote_copy(
            src_ref=outbox.at[c, both], dst_ref=inbox.at[c, both],
            send_sem=sent.at[2], recv_sem=recv_z.at[c],
            device_id={"ctx": lax.rem(me + members, n)}, device_id_type=MESH,
        )

    def gate_chunk(c):
        def gate(k, carry):
            p = lax.rem(pair + 2 + k, members)
            value = (feature(k_ref, 0, c, p) * feature(v_ref, 1, c, p)).astype(bf16)
            gated[c, p] = value

            @pl.when(p != mine)
            def _():
                forward(c, p, mine).start()

            @pl.when(p == mine)
            def _():
                spans[c, mine] = value

            return carry

        lax.fori_loop(0, members, gate, 0)

    def relay_chunk(c, whole):
        if whole:
            raw_copy(c, mine).start()
        arrived(c, 1, 1).wait_recv()
        raw_copy(c, 2 * pair + 1 - mine).start()
        arrived(c, members - 2, 0).wait_recv()

        def relay(k, carry):
            raw_copy(c, lax.rem(pair + k, members)).start()
            return carry

        lax.fori_loop(2, members, relay, 0)

    gate_chunk(0)

    @pl.when(quarter == 0)
    def _():
        pl.semaphore_wait(ready.at[0], 1)

    @pl.when(quarter == 0)
    def _():
        raw_copy(0, mine).start()

    gate_chunk(1)

    @pl.when(quarter == 0)
    def _():
        relay_chunk(0, False)

    def lead(c, carry):
        gate_chunk(c)
        return carry

    front = jnp.where(quarter == 0, 4, jnp.where(quarter == 1, 3, jnp.where(quarter == 2, 8, chunks)))
    front = jnp.minimum(front, chunks)

    @pl.when(quarter == 0)
    def _():
        lax.fori_loop(2, front, lead, 0)

    build_all()

    @pl.when(quarter > 0)
    def _():
        lax.fori_loop(2, front, lead, 0)

    @pl.when(linked)
    def _():
        pl.semaphore_wait(ready.at[0], 1)

    late_rim()
    loads[3].wait()
    loads[6].wait()
    loads[7].wait()
    border = border_of()
    early_all = border <= n // 2
    take_raw = early_all & (quarter == 1)
    is_raw = (quarter == 1) | (early_all & (quarter == 2))
    place = lax.broadcasted_iota(jnp.int32, (rows, width), 0).astype(f32)
    tile = 2 * rows

    def finish_chunk(c):
        all_backward(c).wait_recv()

        def finish(p, carry, last=False):
            cols = columns(c, p)
            total = landed[c, p].astype(f32) + skip_ref[:, cols] * gated[c, p].astype(f32)
            if last:
                total = total + inbox[c, p].astype(f32)
            out_ref[:, cols] = (qfeat[c, p] * total).astype(bf16)
            return carry

        @pl.when(quarter < 3)
        def _():
            lax.fori_loop(0, members, finish, 0)

        @pl.when(quarter == 3)
        def _():
            box_copy(c).wait_recv()
            lax.fori_loop(0, members, functools.partial(finish, last=True), 0)

    def at(index, size):
        return pl.ds(pl.multiple_of(index * size, size), size)

    lag = jnp.where(linked, 4, chunks)

    def step(c, carry):
        @pl.when((quarter == 0) & (c + 1 < chunks))
        def _():
            relay_chunk(c + 1, True)

        @pl.when(c + front < chunks)
        def _():
            gate_chunk(c + front)

        rate = decay_ref[:, columns(c, mine)]
        far = jnp.exp(-rate * long)

        def query(p, carry):
            qfeat[c, p] = feature(q_ref, 2, c, p)
            return carry

        lax.fori_loop(0, members, query, 0)

        @pl.when(quarter > 0)
        def _():
            arrived(c, 1, 1).wait_recv()
            arrived(c, members - 2, 0).wait_recv()

        def prepare(j, carry):
            spot = place + (j * rows).astype(f32)
            rise = jnp.exp(rate * spot)
            grow[j] = rise
            fade[j] = jnp.exp(-rate * spot)
            scaled[at(members + j, rows), :] = (spans[c, j].astype(f32) * rise).astype(bf16)
            return carry

        lax.fori_loop(0, members, prepare, 0)

        @pl.when(c >= lag)
        def _():
            finish_chunk(c - lag)

        def own_part(i):
            return jnp.dot(
                mix_here[at(i, tile), long:], scaled[long:, :], preferred_element_type=f32
            )

        @pl.when(linked)
        def _():
            def before(i, carry):
                acc = jnp.dot(
                    mix_next[at(i, tile), long:], scaled[long:, :], preferred_element_type=f32
                )
                for side in range(2):
                    ahead[2 * i + side] = acc[side * rows : (side + 1) * rows]
                return carry

            for i in range(members // 2):
                before(i, 0)
            box_copy(c).wait_recv()
            drop = jnp.where(is_raw, far, 1.0)

            def receive(j, carry):
                scaled[at(j, rows), :] = (
                    inbox[c, j].astype(f32) * (grow[j] * drop)
                ).astype(bf16)
                return carry

            lax.fori_loop(0, members, receive, 0)

        @pl.when(linked)
        def _():
            def send(i, carry):
                acc = jnp.dot(
                    mix_next[at(i, tile), :long], scaled[:long, :], preferred_element_type=f32
                )
                for side in range(2):
                    j = 2 * i + side
                    value = (ahead[j] + acc[side * rows : (side + 1) * rows]) * (fade[j] * far)
                    raw = spans[c, j].astype(f32)
                    outbox[c, j] = jnp.where(take_raw, raw, value).astype(bf16)

                @pl.when(quarter == 1)
                def _():
                    half_box(c, i).start()

                @pl.when(quarter == 2)
                def _():
                    for side in range(2):
                        part_copy(c, 2 * i + side).start()

                return carry

            for i in range(members // 2):
                send(i, 0)

        def publish(reader, value):
            value = value.astype(bf16)
            result[c, reader] = value

            @pl.when(reader != mine)
            def _():
                backward(c, reader, mine).start()

            @pl.when(reader == mine)
            def _():
                landed[c, mine] = value

        def publish_both(i, acc):
            for side in range(2):
                reader = 2 * i + side
                publish(reader, acc[side * rows : (side + 1) * rows] * fade[reader])

        @pl.when(~linked)
        def _():
            def target(i, carry):
                publish_both(i, own_part(i))
                return carry

            for i in range(members // 2):
                target(i, 0)

        @pl.when(linked)
        def _():
            def target(i, carry):
                publish_both(i, jnp.dot(
                    mix_here[at(i, tile), :], scaled[...], preferred_element_type=f32
                ))
                return carry

            for i in range(members // 2):
                target(i, 0)

        return carry

    lax.fori_loop(0, chunks, step, 0)

    def tail(c, carry):
        finish_chunk(c)
        return carry

    lax.fori_loop(chunks - lag, chunks, tail, 0)

    def everything(src, dst, index, count):
        part = pl.ds(0, count)
        return pltpu.make_async_remote_copy(
            src_ref=src.at[:, part], dst_ref=dst.at[:, part],
            send_sem=sent.at[index], recv_sem=recv1.at[0, 0],
            device_id={"ctx": base + lax.rem(mine + 1, members)}, device_id_type=MESH,
        )

    everything(gated, spans, 0, members - 1).wait_send()
    everything(result, landed, 1, members - 1).wait_send()

    @pl.when(inner)
    def _():
        everything(spans, inbox, 2, members).wait_send()

    @pl.when(me < n - 1)
    def _():
        for part in range(2):
            rim_copy(me + 1, part).wait_send()


def hand_over(src_ref, dst_ref, sem):
    copy = pltpu.make_async_copy(src_ref, dst_ref, sem.at[0])
    copy.start()
    copy.wait()


def on_device(
    query_rows, key_rows, value_rows, conv_taps, decay_rate, lag_profile, skip_gain, pair_lists
):
    rows, channels = query_rows.shape
    n = lax.axis_size("ctx")
    members = n // 4
    share = channels // members
    width = WIDTH
    chunks = share // width
    long = members * rows
    pairs = pair_lists.transpose(1, 2, 0)
    hbm = pl.BlockSpec(memory_space=pltpu.HBM)
    bf16, f32 = jnp.bfloat16, jnp.float32
    piece = (chunks, members, rows, width)
    edges = 4 * members + max(16, 2 * members)
    dma = pltpu.SemaphoreType.DMA
    held = pl.pallas_call(
        functools.partial(kernel, n, rows, chunks, width),
        out_shape=pltpu.VMEM((rows, channels), bf16),
        in_specs=[hbm] * 8,
        out_specs=pl.BlockSpec(memory_space=pltpu.VMEM),
        scratch_shapes=[
            pltpu.VMEM((rows, channels), bf16),
            pltpu.VMEM((rows, channels), bf16),
            pltpu.VMEM((rows, channels), bf16),
            pltpu.VMEM(conv_taps.shape, f32),
            pltpu.VMEM((1, channels), f32),
            pltpu.VMEM((1, lag_profile.shape[0]), f32),
            pltpu.VMEM((1, channels), f32),
            pltpu.VMEM(pairs.shape, jnp.int32),
            pltpu.VMEM((3, 16, channels), bf16),
            pltpu.VMEM((edges, share), f32),
            pltpu.VMEM((edges, share), bf16),
            pltpu.VMEM((edges, share), bf16),
            pltpu.VMEM((8, channels), f32),
            pltpu.VMEM(piece, bf16),
            pltpu.VMEM(piece, f32),
            pltpu.VMEM(piece, bf16),
            pltpu.VMEM(piece, bf16),
            pltpu.VMEM(piece, bf16),
            pltpu.VMEM((3 * members, rows, rows), bf16),
            pltpu.VMEM((long, 2 * long), bf16),
            pltpu.VMEM((long, 2 * long), bf16),
            pltpu.VMEM((2 * long, width), bf16),
            pltpu.VMEM((members, rows, width), f32),
            pltpu.VMEM((members, rows, width), f32),
            pltpu.VMEM((members, rows, width), f32),
            pltpu.VMEM(piece, bf16),
            pltpu.VMEM(piece, bf16),
            dma((12,)),
            dma((4,)),
            dma((3,)),
            dma((chunks, 2)),
            dma((chunks,)),
            dma((chunks,)),
            pltpu.SemaphoreType.REGULAR((1,)),
        ],
        compiler_params=pltpu.CompilerParams(
            collective_id=0, has_side_effects=True, vmem_limit_bytes=62 * 1024 * 1024
        ),
    )(
        query_rows, key_rows, value_rows, conv_taps, decay_rate.reshape(1, -1),
        lag_profile.reshape(1, -1), skip_gain.reshape(1, -1), pairs,
    )
    return pl.pallas_call(
        hand_over,
        out_shape=jax.ShapeDtypeStruct((rows, channels), bf16),
        in_specs=[pl.BlockSpec(memory_space=pltpu.VMEM)],
        out_specs=hbm,
        scratch_shapes=[dma((1,))],
        compiler_params=pltpu.CompilerParams(vmem_limit_bytes=1024 * 1024),
    )(held)


def solution(mesh):
    rows = P(("group", "ctx"), None)
    return jax.shard_map(
        on_device,
        mesh=mesh,
        in_specs=(rows, rows, rows, P(), P(), P(), P(), P("group", None, None)),
        out_specs=rows,
        check_vma=False,
    )
```

```python
import functools

import jax
import jax.numpy as jnp
from jax import lax
from jax.experimental import pallas as pl
from jax.experimental.pallas import tpu as pltpu
from jax.sharding import PartitionSpec as P

MESH = pl.DeviceIdType.MESH
WIDTH = 128
STRAIGHT = 2
STRIPS = 8


def kernel(
    n, rows, chunks, width,
    q_hbm, k_hbm, v_hbm, taps_hbm, decay_hbm, lag_hbm, skip_hbm, pairs_hbm,
    out_ref, q_ref, k_ref, v_ref, taps_ref, decay_ref, lag_ref, skip_ref, pairs_ref,
    tail_ref, edge, rim_out, rim_in, rim, gated, qfeat, spans, inbox, outbox, toep, mix_here, mix_next,
    scaled, grow, fade, ahead, result, landed,
    load_sem, rim_sem, sent, recv1, recv_z, recv2, ready,
):
    me = lax.axis_index("ctx")
    members = n // 4
    quarter = me // members
    base = quarter * members
    mine = me - base
    pair = 2 * (mine // 2)
    long = members * rows
    share = chunks * width
    f32, bf16 = jnp.float32, jnp.bfloat16

    loads = [
        pltpu.make_async_copy(src, dst, load_sem.at[index])
        for index, (src, dst) in enumerate(
            (
                (k_hbm, k_ref), (v_hbm, v_ref), (taps_hbm, taps_ref), (q_hbm, q_ref),
                (lag_hbm, lag_ref), (pairs_hbm, pairs_ref), (decay_hbm, decay_ref),
                (skip_hbm, skip_ref),
            )
        )
    ]
    tails = [
        pltpu.make_async_copy(
            src.at[pl.ds(rows - 16, 16)], tail_ref.at[index], load_sem.at[9 + index]
        )
        for index, src in enumerate((k_hbm, v_hbm, q_hbm))
    ]
    for load in tails + loads:
        load.start()

    barrier = pltpu.get_barrier_semaphore()
    inner = quarter < 3
    linked = (quarter > 0) & (quarter < 3)
    first_of_later = (quarter > 0) & (mine == 0)
    last_of_earlier = (quarter < 3) & (mine == members - 1)

    def tell(sem, to):
        pl.semaphore_signal(sem, inc=1, device_id={"ctx": to}, device_id_type=MESH)

    def greet(k, c):
        tell(barrier, base + lax.rem(mine + k, members))
        return c

    lax.fori_loop(1, members, greet, 0)

    @pl.when(inner)
    def _():
        tell(barrier, me + members)

    @pl.when(first_of_later)
    def _():
        tell(barrier, me - 1)

    def build_toep(groups):
        wide = 4 * rows

        def build(g, c):
            upper = lag_ref[:, pl.ds(pl.multiple_of(g * wide, wide), wide)]
            below = jnp.maximum(4 * g - 1, 0)
            lower = lag_ref[:, pl.ds(pl.multiple_of(below * rows, rows), rows)]
            lower = jnp.where(g > 0, lower, 0.0)
            window = jnp.broadcast_to(
                jnp.concatenate([upper, lower], axis=1), (rows, wide + rows)
            )
            turned = pltpu.roll(window, 0, 1, stride=1, stride_axis=0)
            for e in range(4):
                toep[4 * g + e] = turned[:, e * rows : (e + 1) * rows].T.astype(bf16)
            return c

        lax.fori_loop(0, groups, build, 0)

    def border_of():
        listed = jnp.where(pairs_ref[:, 0, :] == 0, pairs_ref[:, 1, :], -1)
        return 1 + jnp.max(jnp.max(listed, axis=1, keepdims=True), axis=0, keepdims=True)

    def build_mix():
        border = border_of()
        early = jnp.where(border <= n // 2, 1.0, 0.0)
        raw = jnp.where(quarter == 1, 1.0, early)
        eye = jnp.where(
            lax.broadcasted_iota(jnp.int32, (rows, rows), 0)
            == lax.broadcasted_iota(jnp.int32, (rows, rows), 1),
            1.0, 0.0,
        ).astype(bf16)

        def live(source, target):
            a = jnp.where(border > source, 1.0, 0.0)
            b = jnp.where(border > target, 1.0, 0.0)
            return 1.0 - jnp.abs(a - b)

        def at(index):
            return pl.ds(pl.multiple_of(index * rows, rows), rows)

        def fill(i, carry):
            def one(j, carry):
                src, dst = base + j, base + i
                causal = jnp.where(j <= i, 1.0, 0.0)
                mix_here[at(i), at(members + j)] = (
                    toep[jnp.maximum(i - j, 0)] * (live(src, dst) * causal).astype(bf16)
                )

                @pl.when(linked)
                def _():
                    passed = (1.0 - raw) * jnp.where(i == j, 1.0, 0.0)
                    near = toep[members + i - j]
                    mix_here[at(i), at(j)] = (
                        near * (raw * live(src - members, dst)).astype(bf16)
                        + eye * passed.astype(bf16)
                    )
                    mix_next[at(i), at(members + j)] = (
                        near * live(src, dst + members).astype(bf16)
                    )
                    mix_next[at(i), at(j)] = (
                        toep[2 * members + i - j]
                        * (raw * live(src - members, dst + members)).astype(bf16)
                    )

                return carry

            return lax.fori_loop(0, members, one, carry)

        lax.fori_loop(0, members, fill, 0)

    def build_all():
        loads[4].wait()
        loads[5].wait()

        @pl.when(linked)
        def _():
            build_toep(3 * members // 4)

        @pl.when(~linked)
        def _():
            build_toep(members // 4)

        build_mix()

    def awaited():
        total = members - 1 + jnp.where(quarter > 0, 1, 0)
        return total + jnp.where(last_of_earlier, 1, 0)

    pl.semaphore_wait(barrier, awaited())

    @pl.when(quarter > 0)
    def _():
        tell(ready.at[0], me - members)

    def rim_copy(to, part):
        size = 4 * members if part == 0 else rim_out.shape[0] - 4 * members
        at = pl.ds(4 * members * part, size)
        return pltpu.make_async_remote_copy(
            src_ref=rim_out.at[at], dst_ref=rim_in.at[at], send_sem=rim_sem.at[part],
            recv_sem=rim_sem.at[2 + part], device_id={"ctx": to}, device_id_type=MESH,
        )

    def edges(index):
        tail = tail_ref[index].astype(f32)
        for p in range(members):
            for side in range(2):
                at = (2 * index + side) * members + p
                edge[at : at + 1, :] = tail[14 + side : 15 + side, p * share : (p + 1) * share]

    edge[4 * members :, :] = jnp.zeros((edge.shape[0] - 4 * members, share), f32)
    for index in range(2):
        tails[index].wait()
        edges(index)
    rim_out[: 4 * members, :] = edge[: 4 * members, :].astype(bf16)

    @pl.when(mine < members - 1)
    def _():
        rim_copy(me + 1, 0).start()

    tails[2].wait()
    edges(2)
    rim_out[4 * members :, :] = edge[4 * members :, :].astype(bf16)

    @pl.when(mine < members - 1)
    def _():
        rim_copy(me + 1, 1).start()

    @pl.when(last_of_earlier)
    def _():
        for part in range(2):
            rim_copy(me + 1, part).start()

    for index in range(3):
        loads[index].wait()

    def spread(first, last):
        size = max(16, (last - first) * members)
        held = rim_in[first * members : first * members + size, :].astype(f32)
        for at in range(first, last):
            for p in range(members):
                from_row = (at - first) * members + p
                rim[at : at + 1, p * share : (p + 1) * share] = held[from_row : from_row + 1, :]

    @pl.when(me == 0)
    def _():
        rim[...] = jnp.zeros_like(rim)

    @pl.when(me > 0)
    def _():
        rim_copy(me - 1, 0).wait_recv()
        spread(0, 4)

    def late_rim():
        @pl.when(me > 0)
        def _():
            rim_copy(me - 1, 1).wait_recv()
            spread(4, 6)

    row = lax.broadcasted_iota(jnp.int32, (rows, width), 0)

    def columns(c, p):
        return pl.ds(pl.multiple_of((p * chunks + c) * width, width), width)

    def feature(ref, index, c, p):
        cols = columns(c, p)
        tap = (index + 1) % 3
        x = ref[:, cols].astype(f32)
        two = rim[2 * index : 2 * index + 1, cols]
        one = rim[2 * index + 1 : 2 * index + 2, cols]
        x1 = jnp.where(row == 0, one, pltpu.roll(x, 1, 0))
        x2 = jnp.where(row == 0, two, jnp.where(row == 1, one, pltpu.roll(x, 2, 0)))
        return (
            taps_ref[tap, 0:1, cols] * x
            + taps_ref[tap, 1:2, cols] * x1
            + taps_ref[tap, 2:3, cols] * x2
        )

    def forward(c, p, sender):
        return pltpu.make_async_remote_copy(
            src_ref=gated.at[c, p], dst_ref=spans.at[c, sender],
            send_sem=sent.at[0], recv_sem=recv1.at[c, jnp.where(sender // 2 == p // 2, 1, 0)],
            device_id={"ctx": base + p}, device_id_type=MESH,
        )

    def backward(c, p, sender):
        return pltpu.make_async_remote_copy(
            src_ref=result.at[c, p], dst_ref=landed.at[c, sender],
            send_sem=sent.at[1], recv_sem=recv2.at[c],
            device_id={"ctx": base + p}, device_id_type=MESH,
        )

    others = pl.ds(0, members - 1)

    def arrived(c, count, mate):
        part = pl.ds(0, count)
        return pltpu.make_async_remote_copy(
            src_ref=gated.at[c, part], dst_ref=spans.at[c, part],
            send_sem=sent.at[0], recv_sem=recv1.at[c, mate],
            device_id={"ctx": base + lax.rem(mine + 1, members)}, device_id_type=MESH,
        )

    def all_backward(c):
        return pltpu.make_async_remote_copy(
            src_ref=result.at[c, others], dst_ref=landed.at[c, others],
            send_sem=sent.at[1], recv_sem=recv2.at[c],
            device_id={"ctx": base + lax.rem(mine + 1, members)}, device_id_type=MESH,
        )

    def raw_copy(c, j):
        return pltpu.make_async_remote_copy(
            src_ref=spans.at[c, j], dst_ref=inbox.at[c, j],
            send_sem=sent.at[2], recv_sem=recv_z.at[c],
            device_id={"ctx": lax.rem(me + members, n)}, device_id_type=MESH,
        )

    def box_copy(c):
        return pltpu.make_async_remote_copy(
            src_ref=outbox.at[c], dst_ref=inbox.at[c],
            send_sem=sent.at[2], recv_sem=recv_z.at[c],
            device_id={"ctx": lax.rem(me + members, n)}, device_id_type=MESH,
        )

    def part_copy(c, j):
        return pltpu.make_async_remote_copy(
            src_ref=outbox.at[c, j], dst_ref=inbox.at[c, mine],
            send_sem=sent.at[2], recv_sem=recv_z.at[c],
            device_id={"ctx": lax.rem(base + members + j, n)}, device_id_type=MESH,
        )

    def half_box(c, i):
        both = pl.ds(2 * i, 2)
        return pltpu.make_async_remote_copy(
            src_ref=outbox.at[c, both], dst_ref=inbox.at[c, both],
            send_sem=sent.at[2], recv_sem=recv_z.at[c],
            device_id={"ctx": lax.rem(me + members, n)}, device_id_type=MESH,
        )

    def gate_chunk(c):
        def gate(k, carry):
            p = lax.rem(pair + 2 + k, members)
            value = (feature(k_ref, 0, c, p) * feature(v_ref, 1, c, p)).astype(bf16)
            gated[c, p] = value

            @pl.when(p != mine)
            def _():
                forward(c, p, mine).start()

            @pl.when(p == mine)
            def _():
                spans[c, mine] = value

            return carry

        lax.fori_loop(0, members, gate, 0)

    def relay_chunk(c, whole):
        if whole:
            raw_copy(c, mine).start()
        arrived(c, 1, 1).wait_recv()
        raw_copy(c, 2 * pair + 1 - mine).start()
        arrived(c, members - 2, 0).wait_recv()

        def relay(k, carry):
            raw_copy(c, lax.rem(pair + k, members)).start()
            return carry

        lax.fori_loop(2, members, relay, 0)

    gate_chunk(0)

    @pl.when(quarter == 0)
    def _():
        pl.semaphore_wait(ready.at[0], 1)

    @pl.when(quarter == 0)
    def _():
        raw_copy(0, mine).start()

    gate_chunk(1)

    @pl.when(quarter == 0)
    def _():
        relay_chunk(0, False)

    def lead(c, carry):
        gate_chunk(c)
        return carry

    front = jnp.where(quarter == 0, 4, jnp.where(quarter == 1, 3, jnp.where(quarter == 2, 5, chunks)))
    front = jnp.minimum(front, chunks)

    @pl.when(quarter == 0)
    def _():
        lax.fori_loop(2, front, lead, 0)

    build_all()

    @pl.when(quarter > 0)
    def _():
        lax.fori_loop(2, front, lead, 0)

    @pl.when(linked)
    def _():
        pl.semaphore_wait(ready.at[0], 1)

    late_rim()
    loads[3].wait()
    loads[6].wait()
    loads[7].wait()
    border = border_of()
    early_all = border <= n // 2
    take_raw = early_all & (quarter == 1)
    is_raw = (quarter == 1) | (early_all & (quarter == 2))
    place = lax.broadcasted_iota(jnp.int32, (rows, width), 0).astype(f32)
    tile = 2 * rows

    def finish_chunk(c):
        all_backward(c).wait_recv()

        def finish(p, carry, last=False):
            cols = columns(c, p)
            total = landed[c, p].astype(f32) + skip_ref[:, cols] * gated[c, p].astype(f32)
            if last:
                total = total + inbox[c, p].astype(f32)
            out_ref[:, cols] = (qfeat[c, p] * total).astype(bf16)
            return carry

        late = (quarter == 3) & (c >= chunks - STRAIGHT)

        @pl.when(~late)
        def _():
            lax.fori_loop(0, members, finish, 0)

        @pl.when(late)
        def _():
            box_copy(c).wait_recv()
            lax.fori_loop(0, members, functools.partial(finish, last=True), 0)

    def at(index, size):
        return pl.ds(pl.multiple_of(index * size, size), size)

    lag = jnp.where(quarter == 0, chunks, jnp.where(quarter == 1, 4, jnp.where(quarter == 2, 3, 2)))

    skip = jnp.where(quarter == 3, STRAIGHT, 0)

    def step(u, carry):
        c = jnp.where(quarter == 3, lax.rem(u + chunks - STRAIGHT, chunks), u)
        straight = c >= chunks - STRAIGHT
        @pl.when((quarter == 0) & (c + 1 < chunks))
        def _():
            relay_chunk(c + 1, True)

        @pl.when(c + front < chunks)
        def _():
            gate_chunk(c + front)

        rate = decay_ref[:, columns(c, mine)]
        far = jnp.exp(-rate * long)

        def query(p, carry):
            qfeat[c, p] = feature(q_ref, 2, c, p)
            return carry

        lax.fori_loop(0, members, query, 0)

        @pl.when(quarter > 0)
        def _():
            arrived(c, 1, 1).wait_recv()
            arrived(c, members - 2, 0).wait_recv()

        def prepare(j, carry):
            spot = place + (j * rows).astype(f32)
            rise = jnp.exp(rate * spot)
            grow[j] = rise
            fade[j] = jnp.exp(-rate * spot)
            scaled[at(members + j, rows), :] = (spans[c, j].astype(f32) * rise).astype(bf16)
            return carry

        lax.fori_loop(0, members, prepare, 0)

        @pl.when(u - lag >= skip)
        def _():
            finish_chunk(u - lag - skip)

        def own_part(i):
            return jnp.dot(
                mix_here[at(i, tile), long:], scaled[long:, :], preferred_element_type=f32
            )

        @pl.when(linked)
        def _():
            def before(i, carry):
                acc = jnp.dot(
                    mix_next[at(i, tile), long:], scaled[long:, :], preferred_element_type=f32
                )
                for side in range(2):
                    ahead[2 * i + side] = acc[side * rows : (side + 1) * rows]
                return carry

            for i in range(members // 2):
                before(i, 0)
            box_copy(c).wait_recv()
            drop = jnp.where(is_raw, far, 1.0)

            def receive(j, carry):
                scaled[at(j, rows), :] = (
                    inbox[c, j].astype(f32) * (grow[j] * drop)
                ).astype(bf16)
                return carry

            lax.fori_loop(0, members, receive, 0)

        @pl.when(linked)
        def _():
            def send(i, carry):
                acc = jnp.dot(
                    mix_next[at(i, tile), :long], scaled[:long, :], preferred_element_type=f32
                )
                for side in range(2):
                    j = 2 * i + side
                    value = (ahead[j] + acc[side * rows : (side + 1) * rows]) * (fade[j] * far)
                    raw = spans[c, j].astype(f32)
                    outbox[c, j] = jnp.where(take_raw, raw, value).astype(bf16)

                @pl.when((quarter == 1) | ~straight)
                def _():
                    half_box(c, i).start()

                @pl.when((quarter == 2) & straight)
                def _():
                    for side in range(2):
                        part_copy(c, 2 * i + side).start()

                return carry

            for k in range(members // 2):
                send(lax.rem(mine // 2 + 1 + k, members // 2), 0)

        def publish(reader, value):
            value = value.astype(bf16)
            result[c, reader] = value

            @pl.when(reader != mine)
            def _():
                backward(c, reader, mine).start()

            @pl.when(reader == mine)
            def _():
                landed[c, mine] = value

        def publish_both(i, acc):
            for side in range(2):
                reader = 2 * i + side
                publish(reader, acc[side * rows : (side + 1) * rows] * fade[reader])

        @pl.when((quarter == 3) & ~straight)
        def _():
            for i in range(members // 2):
                acc = own_part(i)
                for side in range(2):
                    j = 2 * i + side
                    grow[j] = acc[side * rows : (side + 1) * rows] * fade[j]
            box_copy(c).wait_recv()

            def target(k, carry):
                reader = lax.rem(pair + 2 + k, members)
                publish(reader, grow[reader] + inbox[c, reader].astype(f32))
                return carry

            lax.fori_loop(0, members, target, 0)

        @pl.when((quarter == 0) | ((quarter == 3) & straight))
        def _():
            def target(i, carry):
                publish_both(i, own_part(i))
                return carry

            for k in range(members // 2):
                target(lax.rem(mine // 2 + 1 + k, members // 2), 0)

        @pl.when(linked)
        def _():
            def target(i, carry):
                publish_both(i, jnp.dot(
                    mix_here[at(i, tile), :], scaled[...], preferred_element_type=f32
                ))
                return carry

            for k in range(members // 2):
                target(lax.rem(mine // 2 + 1 + k, members // 2), 0)

        return carry

    lax.fori_loop(0, chunks, step, 0)

    def tail(c, carry):
        finish_chunk(c)
        return carry

    lax.fori_loop(chunks - lag - skip, chunks - skip, tail, 0)

    @pl.when(quarter == 3)
    def _():
        lax.fori_loop(chunks - STRAIGHT, chunks, tail, 0)

    def everything(src, dst, index, count):
        part = pl.ds(0, count)
        return pltpu.make_async_remote_copy(
            src_ref=src.at[:, part], dst_ref=dst.at[:, part],
            send_sem=sent.at[index], recv_sem=recv1.at[0, 0],
            device_id={"ctx": base + lax.rem(mine + 1, members)}, device_id_type=MESH,
        )

    everything(gated, spans, 0, members - 1).wait_send()
    everything(result, landed, 1, members - 1).wait_send()

    @pl.when(inner)
    def _():
        everything(spans, inbox, 2, members).wait_send()

    @pl.when(me < n - 1)
    def _():
        for part in range(2):
            rim_copy(me + 1, part).wait_send()


def hand_over(src_ref, dst_ref, sem):
    copy = pltpu.make_async_copy(src_ref, dst_ref, sem.at[0])
    copy.start()
    copy.wait()


def on_device(
    query_rows, key_rows, value_rows, conv_taps, decay_rate, lag_profile, skip_gain, pair_lists
):
    rows, channels = query_rows.shape
    n = lax.axis_size("ctx")
    members = n // 4
    share = channels // members
    width = WIDTH
    chunks = share // width
    long = members * rows
    pairs = pair_lists.transpose(1, 2, 0)
    hbm = pl.BlockSpec(memory_space=pltpu.HBM)
    bf16, f32 = jnp.bfloat16, jnp.float32
    piece = (chunks, members, rows, width)
    edges = 4 * members + max(16, 2 * members)
    dma = pltpu.SemaphoreType.DMA
    held = pl.pallas_call(
        functools.partial(kernel, n, rows, chunks, width),
        out_shape=pltpu.VMEM((rows, channels), bf16),
        in_specs=[hbm] * 8,
        out_specs=pl.BlockSpec(memory_space=pltpu.VMEM),
        scratch_shapes=[
            pltpu.VMEM((rows, channels), bf16),
            pltpu.VMEM((rows, channels), bf16),
            pltpu.VMEM((rows, channels), bf16),
            pltpu.VMEM(conv_taps.shape, f32),
            pltpu.VMEM((1, channels), f32),
            pltpu.VMEM((1, lag_profile.shape[0]), f32),
            pltpu.VMEM((1, channels), f32),
            pltpu.VMEM(pairs.shape, jnp.int32),
            pltpu.VMEM((3, 16, channels), bf16),
            pltpu.VMEM((edges, share), f32),
            pltpu.VMEM((edges, share), bf16),
            pltpu.VMEM((edges, share), bf16),
            pltpu.VMEM((8, channels), f32),
            pltpu.VMEM(piece, bf16),
            pltpu.VMEM(piece, f32),
            pltpu.VMEM(piece, bf16),
            pltpu.VMEM(piece, bf16),
            pltpu.VMEM(piece, bf16),
            pltpu.VMEM((3 * members, rows, rows), bf16),
            pltpu.VMEM((long, 2 * long), bf16),
            pltpu.VMEM((long, 2 * long), bf16),
            pltpu.VMEM((2 * long, width), bf16),
            pltpu.VMEM((members, rows, width), f32),
            pltpu.VMEM((members, rows, width), f32),
            pltpu.VMEM((members, rows, width), f32),
            pltpu.VMEM(piece, bf16),
            pltpu.VMEM(piece, bf16),
            dma((12,)),
            dma((4,)),
            dma((3,)),
            dma((chunks, 2)),
            dma((chunks,)),
            dma((chunks,)),
            pltpu.SemaphoreType.REGULAR((1,)),
        ],
        compiler_params=pltpu.CompilerParams(
            collective_id=0, has_side_effects=True, vmem_limit_bytes=62 * 1024 * 1024
        ),
    )(
        query_rows, key_rows, value_rows, conv_taps, decay_rate.reshape(1, -1),
        lag_profile.reshape(1, -1), skip_gain.reshape(1, -1), pairs,
    )
    return pl.pallas_call(
        hand_over,
        out_shape=jax.ShapeDtypeStruct((rows, channels), bf16),
        in_specs=[pl.BlockSpec(memory_space=pltpu.VMEM)],
        out_specs=hbm,
        scratch_shapes=[dma((1,))],
        compiler_params=pltpu.CompilerParams(vmem_limit_bytes=1024 * 1024),
    )(held)


def solution(mesh):
    rows = P(("group", "ctx"), None)
    return jax.shard_map(
        on_device,
        mesh=mesh,
        in_specs=(rows, rows, rows, P(), P(), P(), P(), P("group", None, None)),
        out_specs=rows,
        check_vma=False,
    )
```

```python
import functools

import jax
import jax.numpy as jnp
from jax import lax
from jax.experimental import pallas as pl
from jax.experimental.pallas import tpu as pltpu
from jax.sharding import PartitionSpec as P

MESH = pl.DeviceIdType.MESH
WIDTH = 128
STRAIGHT = 2
STRIPS = 8


def kernel(
    n, rows, chunks, width,
    q_hbm, k_hbm, v_hbm, taps_hbm, decay_hbm, lag_hbm, skip_hbm, pairs_hbm,
    out_ref, q_ref, k_ref, v_ref, taps_ref, decay_ref, lag_ref, skip_ref, pairs_ref,
    tail_ref, edge, rim_out, rim_in, rim, gated, qfeat, spans, inbox, outbox, toep, mix_here, mix_next,
    scaled, grow, fade, ahead, result, landed,
    load_sem, rim_sem, sent, recv1, recv_z, recv2, ready,
):
    me = lax.axis_index("ctx")
    members = n // 4
    quarter = me // members
    base = quarter * members
    mine = me - base
    pair = 2 * (mine // 2)
    long = members * rows
    share = chunks * width
    f32, bf16 = jnp.float32, jnp.bfloat16

    loads = [
        pltpu.make_async_copy(src, dst, load_sem.at[index])
        for index, (src, dst) in enumerate(
            (
                (k_hbm, k_ref), (v_hbm, v_ref), (taps_hbm, taps_ref), (q_hbm, q_ref),
                (lag_hbm, lag_ref), (pairs_hbm, pairs_ref), (decay_hbm, decay_ref),
                (skip_hbm, skip_ref),
            )
        )
    ]
    tails = [
        pltpu.make_async_copy(
            src.at[pl.ds(rows - 16, 16)], tail_ref.at[index], load_sem.at[9 + index]
        )
        for index, src in enumerate((k_hbm, v_hbm, q_hbm))
    ]
    for load in tails + loads:
        load.start()

    barrier = pltpu.get_barrier_semaphore()
    inner = quarter < 3
    linked = (quarter > 0) & (quarter < 3)
    first_of_later = (quarter > 0) & (mine == 0)
    last_of_earlier = (quarter < 3) & (mine == members - 1)

    def tell(sem, to):
        pl.semaphore_signal(sem, inc=1, device_id={"ctx": to}, device_id_type=MESH)

    def greet(k, c):
        tell(barrier, base + lax.rem(mine + k, members))
        return c

    lax.fori_loop(1, members, greet, 0)

    @pl.when(inner)
    def _():
        tell(barrier, me + members)

    @pl.when(first_of_later)
    def _():
        tell(barrier, me - 1)

    def build_toep(groups):
        wide = 4 * rows

        def build(g, c):
            upper = lag_ref[:, pl.ds(pl.multiple_of(g * wide, wide), wide)]
            below = jnp.maximum(4 * g - 1, 0)
            lower = lag_ref[:, pl.ds(pl.multiple_of(below * rows, rows), rows)]
            lower = jnp.where(g > 0, lower, 0.0)
            window = jnp.broadcast_to(
                jnp.concatenate([upper, lower], axis=1), (rows, wide + rows)
            )
            turned = pltpu.roll(window, 0, 1, stride=1, stride_axis=0)
            for e in range(4):
                toep[4 * g + e] = turned[:, e * rows : (e + 1) * rows].T.astype(bf16)
            return c

        lax.fori_loop(0, groups, build, 0)

    def border_of():
        listed = jnp.where(pairs_ref[:, 0, :] == 0, pairs_ref[:, 1, :], -1)
        return 1 + jnp.max(jnp.max(listed, axis=1, keepdims=True), axis=0, keepdims=True)

    def build_mix():
        border = border_of()
        early = jnp.where(border <= n // 2, 1.0, 0.0)
        raw = jnp.where(quarter == 1, 1.0, early)
        eye = jnp.where(
            lax.broadcasted_iota(jnp.int32, (rows, rows), 0)
            == lax.broadcasted_iota(jnp.int32, (rows, rows), 1),
            1.0, 0.0,
        ).astype(bf16)

        def live(source, target):
            a = jnp.where(border > source, 1.0, 0.0)
            b = jnp.where(border > target, 1.0, 0.0)
            return 1.0 - jnp.abs(a - b)

        def at(index):
            return pl.ds(pl.multiple_of(index * rows, rows), rows)

        def fill(i, carry):
            def one(j, carry):
                src, dst = base + j, base + i
                causal = jnp.where(j <= i, 1.0, 0.0)
                mix_here[at(i), at(members + j)] = (
                    toep[jnp.maximum(i - j, 0)] * (live(src, dst) * causal).astype(bf16)
                )

                @pl.when(linked)
                def _():
                    passed = (1.0 - raw) * jnp.where(i == j, 1.0, 0.0)
                    near = toep[members + i - j]
                    mix_here[at(i), at(j)] = (
                        near * (raw * live(src - members, dst)).astype(bf16)
                        + eye * passed.astype(bf16)
                    )
                    mix_next[at(i), at(members + j)] = (
                        near * live(src, dst + members).astype(bf16)
                    )
                    mix_next[at(i), at(j)] = (
                        toep[2 * members + i - j]
                        * (raw * live(src - members, dst + members)).astype(bf16)
                    )

                return carry

            return lax.fori_loop(0, members, one, carry)

        lax.fori_loop(0, members, fill, 0)

    def build_all():
        loads[4].wait()
        loads[5].wait()

        @pl.when(linked)
        def _():
            build_toep(3 * members // 4)

        @pl.when(~linked)
        def _():
            build_toep(members // 4)

        build_mix()

    def awaited():
        total = members - 1 + jnp.where(quarter > 0, 1, 0)
        return total + jnp.where(last_of_earlier, 1, 0)

    pl.semaphore_wait(barrier, awaited())

    @pl.when(quarter > 0)
    def _():
        tell(ready.at[0], me - members)

    def rim_copy(to, part):
        size = 4 * members if part == 0 else rim_out.shape[0] - 4 * members
        at = pl.ds(4 * members * part, size)
        return pltpu.make_async_remote_copy(
            src_ref=rim_out.at[at], dst_ref=rim_in.at[at], send_sem=rim_sem.at[part],
            recv_sem=rim_sem.at[2 + part], device_id={"ctx": to}, device_id_type=MESH,
        )

    def edges(index):
        tail = tail_ref[index].astype(f32)
        for p in range(members):
            for side in range(2):
                at = (2 * index + side) * members + p
                edge[at : at + 1, :] = tail[14 + side : 15 + side, p * share : (p + 1) * share]

    edge[4 * members :, :] = jnp.zeros((edge.shape[0] - 4 * members, share), f32)
    for index in range(2):
        tails[index].wait()
        edges(index)
    rim_out[: 4 * members, :] = edge[: 4 * members, :].astype(bf16)

    @pl.when(mine < members - 1)
    def _():
        rim_copy(me + 1, 0).start()

    tails[2].wait()
    edges(2)
    rim_out[4 * members :, :] = edge[4 * members :, :].astype(bf16)

    @pl.when(mine < members - 1)
    def _():
        rim_copy(me + 1, 1).start()

    @pl.when(last_of_earlier)
    def _():
        for part in range(2):
            rim_copy(me + 1, part).start()

    for index in range(3):
        loads[index].wait()

    def spread(first, last):
        size = max(16, (last - first) * members)
        held = rim_in[first * members : first * members + size, :].astype(f32)
        for at in range(first, last):
            for p in range(members):
                from_row = (at - first) * members + p
                rim[at : at + 1, p * share : (p + 1) * share] = held[from_row : from_row + 1, :]

    rim[...] = jnp.zeros_like(rim)

    def late_rim():
        @pl.when(me > 0)
        def _():
            rim_copy(me - 1, 1).wait_recv()
            spread(4, 6)

    row = lax.broadcasted_iota(jnp.int32, (rows, width), 0)

    def columns(c, p):
        return pl.ds(pl.multiple_of((p * chunks + c) * width, width), width)

    def feature(ref, index, c, p):
        cols = columns(c, p)
        tap = (index + 1) % 3
        x = ref[:, cols].astype(f32)
        two = rim[2 * index : 2 * index + 1, cols]
        one = rim[2 * index + 1 : 2 * index + 2, cols]
        x1 = jnp.where(row == 0, one, pltpu.roll(x, 1, 0))
        x2 = jnp.where(row == 0, two, jnp.where(row == 1, one, pltpu.roll(x, 2, 0)))
        return (
            taps_ref[tap, 0:1, cols] * x
            + taps_ref[tap, 1:2, cols] * x1
            + taps_ref[tap, 2:3, cols] * x2
        )

    def forward(c, p, sender):
        return pltpu.make_async_remote_copy(
            src_ref=gated.at[c, p], dst_ref=spans.at[c, sender],
            send_sem=sent.at[0], recv_sem=recv1.at[c, jnp.where(sender // 2 == p // 2, 1, 0)],
            device_id={"ctx": base + p}, device_id_type=MESH,
        )

    def backward(c, p, sender):
        return pltpu.make_async_remote_copy(
            src_ref=result.at[c, p], dst_ref=landed.at[c, sender],
            send_sem=sent.at[1], recv_sem=recv2.at[c],
            device_id={"ctx": base + p}, device_id_type=MESH,
        )

    others = pl.ds(0, members - 1)

    def arrived(c, count, mate):
        part = pl.ds(0, count)
        return pltpu.make_async_remote_copy(
            src_ref=gated.at[c, part], dst_ref=spans.at[c, part],
            send_sem=sent.at[0], recv_sem=recv1.at[c, mate],
            device_id={"ctx": base + lax.rem(mine + 1, members)}, device_id_type=MESH,
        )

    def all_backward(c):
        return pltpu.make_async_remote_copy(
            src_ref=result.at[c, others], dst_ref=landed.at[c, others],
            send_sem=sent.at[1], recv_sem=recv2.at[c],
            device_id={"ctx": base + lax.rem(mine + 1, members)}, device_id_type=MESH,
        )

    def raw_copy(c, j):
        return pltpu.make_async_remote_copy(
            src_ref=spans.at[c, j], dst_ref=inbox.at[c, j],
            send_sem=sent.at[2], recv_sem=recv_z.at[c],
            device_id={"ctx": lax.rem(me + members, n)}, device_id_type=MESH,
        )

    def box_copy(c):
        return pltpu.make_async_remote_copy(
            src_ref=outbox.at[c], dst_ref=inbox.at[c],
            send_sem=sent.at[2], recv_sem=recv_z.at[c],
            device_id={"ctx": lax.rem(me + members, n)}, device_id_type=MESH,
        )

    def part_copy(c, j):
        return pltpu.make_async_remote_copy(
            src_ref=outbox.at[c, j], dst_ref=inbox.at[c, mine],
            send_sem=sent.at[2], recv_sem=recv_z.at[c],
            device_id={"ctx": lax.rem(base + members + j, n)}, device_id_type=MESH,
        )

    def half_box(c, i):
        both = pl.ds(2 * i, 2)
        return pltpu.make_async_remote_copy(
            src_ref=outbox.at[c, both], dst_ref=inbox.at[c, both],
            send_sem=sent.at[2], recv_sem=recv_z.at[c],
            device_id={"ctx": lax.rem(me + members, n)}, device_id_type=MESH,
        )

    def gate_chunk(c):
        def gate(k, carry):
            p = lax.rem(pair + 2 + k, members)
            value = (feature(k_ref, 0, c, p) * feature(v_ref, 1, c, p)).astype(bf16)
            gated[c, p] = value

            @pl.when(p != mine)
            def _():
                forward(c, p, mine).start()

            @pl.when(p == mine)
            def _():
                spans[c, mine] = value

            return carry

        lax.fori_loop(0, members, gate, 0)

    def relay_chunk(c, whole):
        if whole:
            raw_copy(c, mine).start()
        arrived(c, 1, 1).wait_recv()
        raw_copy(c, 2 * pair + 1 - mine).start()
        arrived(c, members - 2, 0).wait_recv()

        def relay(k, carry):
            raw_copy(c, lax.rem(pair + k, members)).start()
            return carry

        lax.fori_loop(2, members, relay, 0)

    def rows_copy(p, first, count):
        part = pl.ds(first, count)
        return pltpu.make_async_remote_copy(
            src_ref=gated.at[0, p, part], dst_ref=spans.at[0, mine, part],
            send_sem=sent.at[0], recv_sem=recv1.at[0, jnp.where(mine // 2 == p // 2, 1, 0)],
            device_id={"ctx": base + p}, device_id_type=MESH,
        )

    def first_body(k, carry):
        p = lax.rem(pair + 2 + k, members)

        @pl.when(p != mine)
        def _():
            gated[0, p] = (feature(k_ref, 0, 0, p) * feature(v_ref, 1, 0, p)).astype(bf16)
            rows_copy(p, 16, rows - 16).start()

        return carry

    def first_head(k, carry):
        p = lax.rem(pair + 2 + k, members)
        value = (feature(k_ref, 0, 0, p) * feature(v_ref, 1, 0, p)).astype(bf16)

        @pl.when(p != mine)
        def _():
            gated[0, p, 0:16, :] = value[:16]
            rows_copy(p, 0, 16).start()

        @pl.when(p == mine)
        def _():
            gated[0, mine] = value
            spans[0, mine] = value

        return carry

    lax.fori_loop(0, members, first_body, 0)

    @pl.when(me > 0)
    def _():
        rim_copy(me - 1, 0).wait_recv()
        spread(0, 4)

    lax.fori_loop(0, members, first_head, 0)

    @pl.when(quarter == 0)
    def _():
        pl.semaphore_wait(ready.at[0], 1)

    @pl.when(quarter == 0)
    def _():
        raw_copy(0, mine).start()

    gate_chunk(1)

    @pl.when(quarter == 0)
    def _():
        relay_chunk(0, False)

    def lead(c, carry):
        gate_chunk(c)
        return carry

    front = jnp.where(quarter == 0, 4, jnp.where(quarter == 1, 3, jnp.where(quarter == 2, 5, chunks)))
    front = jnp.minimum(front, chunks)

    @pl.when(quarter == 0)
    def _():
        lax.fori_loop(2, front, lead, 0)

    build_all()

    @pl.when(quarter > 0)
    def _():
        lax.fori_loop(2, front, lead, 0)

    @pl.when(linked)
    def _():
        pl.semaphore_wait(ready.at[0], 1)

    late_rim()
    loads[3].wait()
    loads[6].wait()
    loads[7].wait()
    border = border_of()
    early_all = border <= n // 2
    take_raw = early_all & (quarter == 1)
    is_raw = (quarter == 1) | (early_all & (quarter == 2))
    place = lax.broadcasted_iota(jnp.int32, (rows, width), 0).astype(f32)
    tile = 2 * rows

    def finish_chunk(c):
        all_backward(c).wait_recv()

        def finish(p, carry, last=False):
            cols = columns(c, p)
            total = landed[c, p].astype(f32) + skip_ref[:, cols] * gated[c, p].astype(f32)
            if last:
                total = total + inbox[c, p].astype(f32)
            out_ref[:, cols] = (qfeat[c, p] * total).astype(bf16)
            return carry

        late = (quarter == 3) & (c >= chunks - STRAIGHT)

        @pl.when(~late)
        def _():
            lax.fori_loop(0, members, finish, 0)

        @pl.when(late)
        def _():
            box_copy(c).wait_recv()
            lax.fori_loop(0, members, functools.partial(finish, last=True), 0)

    def at(index, size):
        return pl.ds(pl.multiple_of(index * size, size), size)

    lag = jnp.where(quarter == 0, chunks, jnp.where(quarter == 1, 4, jnp.where(quarter == 2, 3, 2)))

    skip = jnp.where(quarter == 3, STRAIGHT, 0)

    def step(u, carry):
        c = jnp.where(quarter == 3, lax.rem(u + chunks - STRAIGHT, chunks), u)
        straight = c >= chunks - STRAIGHT
        @pl.when((quarter == 0) & (c + 1 < chunks))
        def _():
            relay_chunk(c + 1, True)

        @pl.when(c + front < chunks)
        def _():
            gate_chunk(c + front)

        rate = decay_ref[:, columns(c, mine)]
        far = jnp.exp(-rate * long)

        def query(p, carry):
            qfeat[c, p] = feature(q_ref, 2, c, p)
            return carry

        lax.fori_loop(0, members, query, 0)

        @pl.when(quarter > 0)
        def _():
            arrived(c, 1, 1).wait_recv()
            arrived(c, members - 2, 0).wait_recv()

        def prepare(j, carry):
            spot = place + (j * rows).astype(f32)
            rise = jnp.exp(rate * spot)
            grow[j] = rise
            fade[j] = jnp.exp(-rate * spot)
            scaled[at(members + j, rows), :] = (spans[c, j].astype(f32) * rise).astype(bf16)
            return carry

        lax.fori_loop(0, members, prepare, 0)

        @pl.when(u - lag >= skip)
        def _():
            finish_chunk(u - lag - skip)

        def own_part(i):
            return jnp.dot(
                mix_here[at(i, tile), long:], scaled[long:, :], preferred_element_type=f32
            )

        @pl.when(linked)
        def _():
            def before(i, carry):
                acc = jnp.dot(
                    mix_next[at(i, tile), long:], scaled[long:, :], preferred_element_type=f32
                )
                for side in range(2):
                    ahead[2 * i + side] = acc[side * rows : (side + 1) * rows]
                return carry

            for i in range(members // 2):
                before(i, 0)
            box_copy(c).wait_recv()
            drop = jnp.where(is_raw, far, 1.0)

            def receive(j, carry):
                scaled[at(j, rows), :] = (
                    inbox[c, j].astype(f32) * (grow[j] * drop)
                ).astype(bf16)
                return carry

            lax.fori_loop(0, members, receive, 0)

        @pl.when(linked)
        def _():
            def send(i, carry):
                acc = jnp.dot(
                    mix_next[at(i, tile), :long], scaled[:long, :], preferred_element_type=f32
                )
                for side in range(2):
                    j = 2 * i + side
                    value = (ahead[j] + acc[side * rows : (side + 1) * rows]) * (fade[j] * far)
                    raw = spans[c, j].astype(f32)
                    outbox[c, j] = jnp.where(take_raw, raw, value).astype(bf16)

                @pl.when((quarter == 1) | ~straight)
                def _():
                    half_box(c, i).start()

                @pl.when((quarter == 2) & straight)
                def _():
                    for side in range(2):
                        part_copy(c, 2 * i + side).start()

                return carry

            for k in range(members // 2):
                send(lax.rem(mine // 2 + 1 + k, members // 2), 0)

        def publish(reader, value):
            value = value.astype(bf16)
            result[c, reader] = value

            @pl.when(reader != mine)
            def _():
                backward(c, reader, mine).start()

            @pl.when(reader == mine)
            def _():
                landed[c, mine] = value

        def publish_both(i, acc):
            for side in range(2):
                reader = 2 * i + side
                publish(reader, acc[side * rows : (side + 1) * rows] * fade[reader])

        @pl.when((quarter == 3) & ~straight)
        def _():
            for i in range(members // 2):
                acc = own_part(i)
                for side in range(2):
                    j = 2 * i + side
                    grow[j] = acc[side * rows : (side + 1) * rows] * fade[j]
            box_copy(c).wait_recv()

            def target(k, carry):
                reader = lax.rem(pair + 2 + k, members)
                publish(reader, grow[reader] + inbox[c, reader].astype(f32))
                return carry

            lax.fori_loop(0, members, target, 0)

        @pl.when((quarter == 0) | ((quarter == 3) & straight))
        def _():
            def target(i, carry):
                publish_both(i, own_part(i))
                return carry

            for k in range(members // 2):
                target(lax.rem(mine // 2 + 1 + k, members // 2), 0)

        @pl.when(linked)
        def _():
            def target(i, carry):
                publish_both(i, jnp.dot(
                    mix_here[at(i, tile), :], scaled[...], preferred_element_type=f32
                ))
                return carry

            for k in range(members // 2):
                target(lax.rem(mine // 2 + 1 + k, members // 2), 0)

        return carry

    lax.fori_loop(0, chunks, step, 0)

    def tail(c, carry):
        finish_chunk(c)
        return carry

    lax.fori_loop(chunks - lag - skip, chunks - skip, tail, 0)

    @pl.when(quarter == 3)
    def _():
        lax.fori_loop(chunks - STRAIGHT, chunks, tail, 0)

    def everything(src, dst, index, count):
        part = pl.ds(0, count)
        return pltpu.make_async_remote_copy(
            src_ref=src.at[:, part], dst_ref=dst.at[:, part],
            send_sem=sent.at[index], recv_sem=recv1.at[0, 0],
            device_id={"ctx": base + lax.rem(mine + 1, members)}, device_id_type=MESH,
        )

    everything(gated, spans, 0, members - 1).wait_send()
    everything(result, landed, 1, members - 1).wait_send()

    @pl.when(inner)
    def _():
        everything(spans, inbox, 2, members).wait_send()

    @pl.when(me < n - 1)
    def _():
        for part in range(2):
            rim_copy(me + 1, part).wait_send()


def hand_over(src_ref, dst_ref, sem):
    copy = pltpu.make_async_copy(src_ref, dst_ref, sem.at[0])
    copy.start()
    copy.wait()


def on_device(
    query_rows, key_rows, value_rows, conv_taps, decay_rate, lag_profile, skip_gain, pair_lists
):
    rows, channels = query_rows.shape
    n = lax.axis_size("ctx")
    members = n // 4
    share = channels // members
    width = WIDTH
    chunks = share // width
    long = members * rows
    pairs = pair_lists.transpose(1, 2, 0)
    hbm = pl.BlockSpec(memory_space=pltpu.HBM)
    bf16, f32 = jnp.bfloat16, jnp.float32
    piece = (chunks, members, rows, width)
    edges = 4 * members + max(16, 2 * members)
    dma = pltpu.SemaphoreType.DMA
    held = pl.pallas_call(
        functools.partial(kernel, n, rows, chunks, width),
        out_shape=pltpu.VMEM((rows, channels), bf16),
        in_specs=[hbm] * 8,
        out_specs=pl.BlockSpec(memory_space=pltpu.VMEM),
        scratch_shapes=[
            pltpu.VMEM((rows, channels), bf16),
            pltpu.VMEM((rows, channels), bf16),
            pltpu.VMEM((rows, channels), bf16),
            pltpu.VMEM(conv_taps.shape, f32),
            pltpu.VMEM((1, channels), f32),
            pltpu.VMEM((1, lag_profile.shape[0]), f32),
            pltpu.VMEM((1, channels), f32),
            pltpu.VMEM(pairs.shape, jnp.int32),
            pltpu.VMEM((3, 16, channels), bf16),
            pltpu.VMEM((edges, share), f32),
            pltpu.VMEM((edges, share), bf16),
            pltpu.VMEM((edges, share), bf16),
            pltpu.VMEM((8, channels), f32),
            pltpu.VMEM(piece, bf16),
            pltpu.VMEM(piece, f32),
            pltpu.VMEM(piece, bf16),
            pltpu.VMEM(piece, bf16),
            pltpu.VMEM(piece, bf16),
            pltpu.VMEM((3 * members, rows, rows), bf16),
            pltpu.VMEM((long, 2 * long), bf16),
            pltpu.VMEM((long, 2 * long), bf16),
            pltpu.VMEM((2 * long, width), bf16),
            pltpu.VMEM((members, rows, width), f32),
            pltpu.VMEM((members, rows, width), f32),
            pltpu.VMEM((members, rows, width), f32),
            pltpu.VMEM(piece, bf16),
            pltpu.VMEM(piece, bf16),
            dma((12,)),
            dma((4,)),
            dma((3,)),
            dma((chunks, 2)),
            dma((chunks,)),
            dma((chunks,)),
            pltpu.SemaphoreType.REGULAR((1,)),
        ],
        compiler_params=pltpu.CompilerParams(
            collective_id=0, has_side_effects=True, vmem_limit_bytes=62 * 1024 * 1024
        ),
    )(
        query_rows, key_rows, value_rows, conv_taps, decay_rate.reshape(1, -1),
        lag_profile.reshape(1, -1), skip_gain.reshape(1, -1), pairs,
    )
    return pl.pallas_call(
        hand_over,
        out_shape=jax.ShapeDtypeStruct((rows, channels), bf16),
        in_specs=[pl.BlockSpec(memory_space=pltpu.VMEM)],
        out_specs=hbm,
        scratch_shapes=[dma((1,))],
        compiler_params=pltpu.CompilerParams(vmem_limit_bytes=1024 * 1024),
    )(held)


def solution(mesh):
    rows = P(("group", "ctx"), None)
    return jax.shard_map(
        on_device,
        mesh=mesh,
        in_specs=(rows, rows, rows, P(), P(), P(), P(), P("group", None, None)),
        out_specs=rows,
        check_vma=False,
    )
```

```python
import functools

import jax
import jax.numpy as jnp
from jax import lax
from jax.experimental import pallas as pl
from jax.experimental.pallas import tpu as pltpu
from jax.sharding import PartitionSpec as P

MESH = pl.DeviceIdType.MESH
WIDTH = 128
STRAIGHT = 2
STRIPS = 8


def kernel(
    n, rows, chunks, width,
    q_hbm, k_hbm, v_hbm, taps_hbm, decay_hbm, lag_hbm, skip_hbm, pairs_hbm,
    out_ref, q_ref, k_ref, v_ref, taps_ref, decay_ref, lag_ref, skip_ref, pairs_ref,
    tail_ref, edge, rim_out, rim_in, rim, gated, qfeat, spans, inbox, outbox, toep, mix_here, mix_next,
    scaled, grow, fade, ahead, result, landed,
    load_sem, rim_sem, sent, recv1, recv_z, recv2, ready,
):
    me = lax.axis_index("ctx")
    members = n // 4
    quarter = me // members
    base = quarter * members
    mine = me - base
    pair = 2 * (mine // 2)
    long = members * rows
    share = chunks * width
    f32, bf16 = jnp.float32, jnp.bfloat16

    loads = [
        pltpu.make_async_copy(src, dst, load_sem.at[index])
        for index, (src, dst) in enumerate(
            (
                (k_hbm, k_ref), (v_hbm, v_ref), (taps_hbm, taps_ref), (q_hbm, q_ref),
                (lag_hbm, lag_ref), (pairs_hbm, pairs_ref), (decay_hbm, decay_ref),
                (skip_hbm, skip_ref),
            )
        )
    ]
    tails = [
        pltpu.make_async_copy(
            src.at[pl.ds(rows - 16, 16)], tail_ref.at[index], load_sem.at[9 + index]
        )
        for index, src in enumerate((k_hbm, v_hbm, q_hbm))
    ]
    for load in tails + loads:
        load.start()

    barrier = pltpu.get_barrier_semaphore()
    inner = quarter < 3
    linked = (quarter > 0) & (quarter < 3)
    first_of_later = (quarter > 0) & (mine == 0)
    last_of_earlier = (quarter < 3) & (mine == members - 1)

    def tell(sem, to):
        pl.semaphore_signal(sem, inc=1, device_id={"ctx": to}, device_id_type=MESH)

    def greet(k, c):
        tell(barrier, base + lax.rem(mine + k, members))
        return c

    lax.fori_loop(1, members, greet, 0)

    @pl.when(inner)
    def _():
        tell(barrier, me + members)

    @pl.when(first_of_later)
    def _():
        tell(barrier, me - 1)

    def build_toep(groups):
        wide = 4 * rows

        def build(g, c):
            upper = lag_ref[:, pl.ds(pl.multiple_of(g * wide, wide), wide)]
            below = jnp.maximum(4 * g - 1, 0)
            lower = lag_ref[:, pl.ds(pl.multiple_of(below * rows, rows), rows)]
            lower = jnp.where(g > 0, lower, 0.0)
            window = jnp.broadcast_to(
                jnp.concatenate([upper, lower], axis=1), (rows, wide + rows)
            )
            turned = pltpu.roll(window, 0, 1, stride=1, stride_axis=0)
            for e in range(4):
                toep[4 * g + e] = turned[:, e * rows : (e + 1) * rows].T.astype(bf16)
            return c

        lax.fori_loop(0, groups, build, 0)

    def border_of():
        listed = jnp.where(pairs_ref[:, 0, :] == 0, pairs_ref[:, 1, :], -1)
        return 1 + jnp.max(jnp.max(listed, axis=1, keepdims=True), axis=0, keepdims=True)

    def build_mix():
        border = border_of()
        early = jnp.where(border <= n // 2, 1.0, 0.0)
        raw = jnp.where(quarter == 1, 1.0, early)
        eye = jnp.where(
            lax.broadcasted_iota(jnp.int32, (rows, rows), 0)
            == lax.broadcasted_iota(jnp.int32, (rows, rows), 1),
            1.0, 0.0,
        ).astype(bf16)

        def live(source, target):
            a = jnp.where(border > source, 1.0, 0.0)
            b = jnp.where(border > target, 1.0, 0.0)
            return 1.0 - jnp.abs(a - b)

        def at(index):
            return pl.ds(pl.multiple_of(index * rows, rows), rows)

        def fill(i, carry):
            def one(j, carry):
                src, dst = base + j, base + i
                causal = jnp.where(j <= i, 1.0, 0.0)
                mix_here[at(i), at(members + j)] = (
                    toep[jnp.maximum(i - j, 0)] * (live(src, dst) * causal).astype(bf16)
                )

                @pl.when(linked)
                def _():
                    passed = (1.0 - raw) * jnp.where(i == j, 1.0, 0.0)
                    near = toep[members + i - j]
                    mix_here[at(i), at(j)] = (
                        near * (raw * live(src - members, dst)).astype(bf16)
                        + eye * passed.astype(bf16)
                    )
                    mix_next[at(i), at(members + j)] = (
                        near * live(src, dst + members).astype(bf16)
                    )
                    mix_next[at(i), at(j)] = (
                        toep[2 * members + i - j]
                        * (raw * live(src - members, dst + members)).astype(bf16)
                    )

                return carry

            return lax.fori_loop(0, members, one, carry)

        lax.fori_loop(0, members, fill, 0)

    def build_all():
        loads[4].wait()
        loads[5].wait()

        @pl.when(linked)
        def _():
            build_toep(3 * members // 4)

        @pl.when(~linked)
        def _():
            build_toep(members // 4)

        build_mix()

    def awaited():
        total = members - 1 + jnp.where(quarter > 0, 1, 0)
        return total + jnp.where(last_of_earlier, 1, 0)

    pl.semaphore_wait(barrier, awaited())

    @pl.when(quarter > 0)
    def _():
        tell(ready.at[0], me - members)

    def rim_copy(to, part):
        size = 4 * members if part == 0 else rim_out.shape[0] - 4 * members
        at = pl.ds(4 * members * part, size)
        return pltpu.make_async_remote_copy(
            src_ref=rim_out.at[at], dst_ref=rim_in.at[at], send_sem=rim_sem.at[part],
            recv_sem=rim_sem.at[2 + part], device_id={"ctx": to}, device_id_type=MESH,
        )

    def edges(index):
        tail = tail_ref[index].astype(f32)
        for p in range(members):
            for side in range(2):
                at = (2 * index + side) * members + p
                edge[at : at + 1, :] = tail[14 + side : 15 + side, p * share : (p + 1) * share]

    edge[4 * members :, :] = jnp.zeros((edge.shape[0] - 4 * members, share), f32)
    for index in range(2):
        tails[index].wait()
        edges(index)
    rim_out[: 4 * members, :] = edge[: 4 * members, :].astype(bf16)

    @pl.when(mine < members - 1)
    def _():
        rim_copy(me + 1, 0).start()

    tails[2].wait()
    edges(2)
    rim_out[4 * members :, :] = edge[4 * members :, :].astype(bf16)

    @pl.when(mine < members - 1)
    def _():
        rim_copy(me + 1, 1).start()

    @pl.when(last_of_earlier)
    def _():
        for part in range(2):
            rim_copy(me + 1, part).start()

    for index in range(3):
        loads[index].wait()

    def spread(first, last):
        size = max(16, (last - first) * members)
        held = rim_in[first * members : first * members + size, :].astype(f32)
        for at in range(first, last):
            for p in range(members):
                from_row = (at - first) * members + p
                rim[at : at + 1, p * share : (p + 1) * share] = held[from_row : from_row + 1, :]

    rim[...] = jnp.zeros_like(rim)

    def late_rim():
        @pl.when(me > 0)
        def _():
            rim_copy(me - 1, 1).wait_recv()
            spread(4, 6)

    row = lax.broadcasted_iota(jnp.int32, (rows, width), 0)

    def columns(c, p):
        return pl.ds(pl.multiple_of((p * chunks + c) * width, width), width)

    def feature(ref, index, c, p):
        cols = columns(c, p)
        tap = (index + 1) % 3
        x = ref[:, cols].astype(f32)
        two = rim[2 * index : 2 * index + 1, cols]
        one = rim[2 * index + 1 : 2 * index + 2, cols]
        x1 = jnp.where(row == 0, one, pltpu.roll(x, 1, 0))
        x2 = jnp.where(row == 0, two, jnp.where(row == 1, one, pltpu.roll(x, 2, 0)))
        return (
            taps_ref[tap, 0:1, cols] * x
            + taps_ref[tap, 1:2, cols] * x1
            + taps_ref[tap, 2:3, cols] * x2
        )

    def forward(c, p, sender):
        return pltpu.make_async_remote_copy(
            src_ref=gated.at[c, p], dst_ref=spans.at[c, sender],
            send_sem=sent.at[0], recv_sem=recv1.at[c, jnp.where(sender // 2 == p // 2, 1, 0)],
            device_id={"ctx": base + p}, device_id_type=MESH,
        )

    def backward(c, p, sender):
        return pltpu.make_async_remote_copy(
            src_ref=result.at[c, p], dst_ref=landed.at[c, sender],
            send_sem=sent.at[1], recv_sem=recv2.at[c],
            device_id={"ctx": base + p}, device_id_type=MESH,
        )

    others = pl.ds(0, members - 1)

    def arrived(c, count, mate):
        part = pl.ds(0, count)
        return pltpu.make_async_remote_copy(
            src_ref=gated.at[c, part], dst_ref=spans.at[c, part],
            send_sem=sent.at[0], recv_sem=recv1.at[c, mate],
            device_id={"ctx": base + lax.rem(mine + 1, members)}, device_id_type=MESH,
        )

    def all_backward(c):
        return pltpu.make_async_remote_copy(
            src_ref=result.at[c, others], dst_ref=landed.at[c, others],
            send_sem=sent.at[1], recv_sem=recv2.at[c],
            device_id={"ctx": base + lax.rem(mine + 1, members)}, device_id_type=MESH,
        )

    def raw_copy(c, j):
        return pltpu.make_async_remote_copy(
            src_ref=spans.at[c, j], dst_ref=inbox.at[c, j],
            send_sem=sent.at[2], recv_sem=recv_z.at[c],
            device_id={"ctx": lax.rem(me + members, n)}, device_id_type=MESH,
        )

    def box_copy(c):
        return pltpu.make_async_remote_copy(
            src_ref=outbox.at[c], dst_ref=inbox.at[c],
            send_sem=sent.at[2], recv_sem=recv_z.at[c],
            device_id={"ctx": lax.rem(me + members, n)}, device_id_type=MESH,
        )

    def part_copy(c, j):
        return pltpu.make_async_remote_copy(
            src_ref=outbox.at[c, j], dst_ref=inbox.at[c, mine],
            send_sem=sent.at[2], recv_sem=recv_z.at[c],
            device_id={"ctx": lax.rem(base + members + j, n)}, device_id_type=MESH,
        )

    def half_box(c, i):
        both = pl.ds(2 * i, 2)
        return pltpu.make_async_remote_copy(
            src_ref=outbox.at[c, both], dst_ref=inbox.at[c, both],
            send_sem=sent.at[2], recv_sem=recv_z.at[c],
            device_id={"ctx": lax.rem(me + members, n)}, device_id_type=MESH,
        )

    def gate_chunk(c):
        def gate(k, carry):
            p = lax.rem(pair + 2 + k, members)
            value = (feature(k_ref, 0, c, p) * feature(v_ref, 1, c, p)).astype(bf16)
            gated[c, p] = value

            @pl.when(p != mine)
            def _():
                forward(c, p, mine).start()

            @pl.when(p == mine)
            def _():
                spans[c, mine] = value

            return carry

        lax.fori_loop(0, members, gate, 0)

    def relay_chunk(c, whole):
        if whole:
            raw_copy(c, mine).start()
        arrived(c, 1, 1).wait_recv()
        raw_copy(c, 2 * pair + 1 - mine).start()
        arrived(c, members - 2, 0).wait_recv()

        def relay(k, carry):
            raw_copy(c, lax.rem(pair + k, members)).start()
            return carry

        lax.fori_loop(2, members, relay, 0)

    def rows_copy(p, first, count):
        part = pl.ds(first, count)
        return pltpu.make_async_remote_copy(
            src_ref=gated.at[0, p, part], dst_ref=spans.at[0, mine, part],
            send_sem=sent.at[0], recv_sem=recv1.at[0, jnp.where(mine // 2 == p // 2, 1, 0)],
            device_id={"ctx": base + p}, device_id_type=MESH,
        )

    def first_body(k, carry):
        p = lax.rem(pair + 2 + k, members)

        @pl.when(p != mine)
        def _():
            gated[0, p] = (feature(k_ref, 0, 0, p) * feature(v_ref, 1, 0, p)).astype(bf16)
            rows_copy(p, 16, rows - 16).start()

        return carry

    def first_head(k, carry):
        p = lax.rem(pair + 2 + k, members)
        value = (feature(k_ref, 0, 0, p) * feature(v_ref, 1, 0, p)).astype(bf16)

        @pl.when(p != mine)
        def _():
            gated[0, p, 0:16, :] = value[:16]
            rows_copy(p, 0, 16).start()

        @pl.when(p == mine)
        def _():
            gated[0, mine] = value
            spans[0, mine] = value

        return carry

    lax.fori_loop(0, members, first_body, 0)

    @pl.when(me > 0)
    def _():
        rim_copy(me - 1, 0).wait_recv()
        spread(0, 4)

    lax.fori_loop(0, members, first_head, 0)

    @pl.when(quarter == 0)
    def _():
        pl.semaphore_wait(ready.at[0], 1)

    @pl.when(quarter == 0)
    def _():
        raw_copy(0, mine).start()

    gate_chunk(1)

    @pl.when(quarter == 0)
    def _():
        relay_chunk(0, False)

    def lead(c, carry):
        gate_chunk(c)
        return carry

    front = jnp.where(quarter == 0, 4, jnp.where(quarter == 1, 3, jnp.where(quarter == 2, 5, chunks)))
    front = jnp.minimum(front, chunks)

    @pl.when(quarter == 0)
    def _():
        lax.fori_loop(2, front, lead, 0)

    build_all()

    @pl.when(quarter > 0)
    def _():
        lax.fori_loop(2, front, lead, 0)

    @pl.when(linked)
    def _():
        pl.semaphore_wait(ready.at[0], 1)

    late_rim()
    loads[3].wait()
    loads[6].wait()
    loads[7].wait()
    border = border_of()
    early_all = border <= n // 2
    take_raw = early_all & (quarter == 1)
    is_raw = (quarter == 1) | (early_all & (quarter == 2))
    place = lax.broadcasted_iota(jnp.int32, (rows, width), 0).astype(f32)
    tile = 2 * rows

    def finish_chunk(c):
        all_backward(c).wait_recv()

        def finish(p, carry, last=False):
            cols = columns(c, p)
            total = landed[c, p].astype(f32) + skip_ref[:, cols] * gated[c, p].astype(f32)
            if last:
                total = total + inbox[c, p].astype(f32)
            out_ref[:, cols] = (qfeat[c, p] * total).astype(bf16)
            return carry

        late = (quarter == 3) & (c >= chunks - STRAIGHT)

        @pl.when(~late)
        def _():
            lax.fori_loop(0, members, finish, 0)

        @pl.when(late)
        def _():
            box_copy(c).wait_recv()
            lax.fori_loop(0, members, functools.partial(finish, last=True), 0)

    def at(index, size):
        return pl.ds(pl.multiple_of(index * size, size), size)

    lag = jnp.where(quarter == 0, chunks, jnp.where(quarter == 1, 4, jnp.where(quarter == 2, 3, 2)))

    skip = jnp.where(quarter == 3, STRAIGHT, 0)

    def step(u, carry):
        c = jnp.where(quarter == 3, lax.rem(u + chunks - STRAIGHT, chunks), u)
        straight = c >= chunks - STRAIGHT
        @pl.when((quarter == 0) & (c + 1 < chunks))
        def _():
            relay_chunk(c + 1, True)

        @pl.when(c + front < chunks)
        def _():
            gate_chunk(c + front)

        rate = decay_ref[:, columns(c, mine)]
        far = jnp.exp(-rate * long)

        def query(p, carry):
            qfeat[c, p] = feature(q_ref, 2, c, p)
            return carry

        @pl.when(~linked)
        def _():
            lax.fori_loop(0, members, query, 0)

        @pl.when(quarter > 0)
        def _():
            arrived(c, 1, 1).wait_recv()
            arrived(c, members - 2, 0).wait_recv()

        def prepare(j, carry):
            spot = place + (j * rows).astype(f32)
            rise = jnp.exp(rate * spot)
            grow[j] = rise
            fade[j] = jnp.exp(-rate * spot)
            scaled[at(members + j, rows), :] = (spans[c, j].astype(f32) * rise).astype(bf16)
            return carry

        lax.fori_loop(0, members, prepare, 0)

        @pl.when(u - lag >= skip)
        def _():
            finish_chunk(u - lag - skip)

        def own_part(i):
            return jnp.dot(
                mix_here[at(i, tile), long:], scaled[long:, :], preferred_element_type=f32
            )

        @pl.when(linked)
        def _():
            def before(i, carry):
                acc = jnp.dot(
                    mix_next[at(i, tile), long:], scaled[long:, :], preferred_element_type=f32
                )
                for side in range(2):
                    ahead[2 * i + side] = acc[side * rows : (side + 1) * rows]
                return carry

            for i in range(members // 2):
                before(i, 0)
            box_copy(c).wait_recv()
            drop = jnp.where(is_raw, far, 1.0)

            def receive(j, carry):
                scaled[at(j, rows), :] = (
                    inbox[c, j].astype(f32) * (grow[j] * drop)
                ).astype(bf16)
                return carry

            lax.fori_loop(0, members, receive, 0)

        @pl.when(linked)
        def _():
            def send(i, carry):
                acc = jnp.dot(
                    mix_next[at(i, tile), :long], scaled[:long, :], preferred_element_type=f32
                )
                for side in range(2):
                    j = 2 * i + side
                    value = (ahead[j] + acc[side * rows : (side + 1) * rows]) * (fade[j] * far)
                    raw = spans[c, j].astype(f32)
                    outbox[c, j] = jnp.where(take_raw, raw, value).astype(bf16)

                @pl.when((quarter == 1) | ~straight)
                def _():
                    half_box(c, i).start()

                @pl.when((quarter == 2) & straight)
                def _():
                    for side in range(2):
                        part_copy(c, 2 * i + side).start()

                return carry

            for k in range(members // 2):
                send(lax.rem(mine // 2 + 1 + k, members // 2), 0)

        def publish(reader, value):
            value = value.astype(bf16)
            result[c, reader] = value

            @pl.when(reader != mine)
            def _():
                backward(c, reader, mine).start()

            @pl.when(reader == mine)
            def _():
                landed[c, mine] = value

        def publish_both(i, acc):
            for side in range(2):
                reader = 2 * i + side
                publish(reader, acc[side * rows : (side + 1) * rows] * fade[reader])

        @pl.when((quarter == 3) & ~straight)
        def _():
            for i in range(members // 2):
                acc = own_part(i)
                for side in range(2):
                    j = 2 * i + side
                    grow[j] = acc[side * rows : (side + 1) * rows] * fade[j]
            box_copy(c).wait_recv()

            def target(k, carry):
                reader = lax.rem(pair + 2 + k, members)
                publish(reader, grow[reader] + inbox[c, reader].astype(f32))
                return carry

            lax.fori_loop(0, members, target, 0)

        @pl.when((quarter == 0) | ((quarter == 3) & straight))
        def _():
            def target(i, carry):
                publish_both(i, own_part(i))
                return carry

            for k in range(members // 2):
                target(lax.rem(mine // 2 + 1 + k, members // 2), 0)

        @pl.when(linked)
        def _():
            def target(i, carry):
                publish_both(i, jnp.dot(
                    mix_here[at(i, tile), :], scaled[...], preferred_element_type=f32
                ))
                return carry

            for k in range(members // 2):
                target(lax.rem(mine // 2 + 1 + k, members // 2), 0)

        @pl.when(linked)
        def _():
            lax.fori_loop(0, members, query, 0)

        return carry

    lax.fori_loop(0, chunks, step, 0)

    def tail(c, carry):
        finish_chunk(c)
        return carry

    lax.fori_loop(chunks - lag - skip, chunks - skip, tail, 0)

    @pl.when(quarter == 3)
    def _():
        lax.fori_loop(chunks - STRAIGHT, chunks, tail, 0)

    def everything(src, dst, index, count):
        part = pl.ds(0, count)
        return pltpu.make_async_remote_copy(
            src_ref=src.at[:, part], dst_ref=dst.at[:, part],
            send_sem=sent.at[index], recv_sem=recv1.at[0, 0],
            device_id={"ctx": base + lax.rem(mine + 1, members)}, device_id_type=MESH,
        )

    everything(gated, spans, 0, members - 1).wait_send()
    everything(result, landed, 1, members - 1).wait_send()

    @pl.when(inner)
    def _():
        everything(spans, inbox, 2, members).wait_send()

    @pl.when(me < n - 1)
    def _():
        for part in range(2):
            rim_copy(me + 1, part).wait_send()


def on_device(
    query_rows, key_rows, value_rows, conv_taps, decay_rate, lag_profile, skip_gain, pair_lists
):
    rows, channels = query_rows.shape
    n = lax.axis_size("ctx")
    members = n // 4
    share = channels // members
    width = WIDTH
    chunks = share // width
    long = members * rows
    pairs = pair_lists.transpose(1, 2, 0)
    hbm = pl.BlockSpec(memory_space=pltpu.HBM)
    bf16, f32 = jnp.bfloat16, jnp.float32
    piece = (chunks, members, rows, width)
    edges = 4 * members + max(16, 2 * members)
    dma = pltpu.SemaphoreType.DMA
    held = pl.pallas_call(
        functools.partial(kernel, n, rows, chunks, width),
        out_shape=pltpu.VMEM((rows, channels), bf16),
        in_specs=[hbm] * 8,
        out_specs=pl.BlockSpec(memory_space=pltpu.VMEM),
        scratch_shapes=[
            pltpu.VMEM((rows, channels), bf16),
            pltpu.VMEM((rows, channels), bf16),
            pltpu.VMEM((rows, channels), bf16),
            pltpu.VMEM(conv_taps.shape, f32),
            pltpu.VMEM((1, channels), f32),
            pltpu.VMEM((1, lag_profile.shape[0]), f32),
            pltpu.VMEM((1, channels), f32),
            pltpu.VMEM(pairs.shape, jnp.int32),
            pltpu.VMEM((3, 16, channels), bf16),
            pltpu.VMEM((edges, share), f32),
            pltpu.VMEM((edges, share), bf16),
            pltpu.VMEM((edges, share), bf16),
            pltpu.VMEM((8, channels), f32),
            pltpu.VMEM(piece, bf16),
            pltpu.VMEM(piece, f32),
            pltpu.VMEM(piece, bf16),
            pltpu.VMEM(piece, bf16),
            pltpu.VMEM(piece, bf16),
            pltpu.VMEM((3 * members, rows, rows), bf16),
            pltpu.VMEM((long, 2 * long), bf16),
            pltpu.VMEM((long, 2 * long), bf16),
            pltpu.VMEM((2 * long, width), bf16),
            pltpu.VMEM((members, rows, width), f32),
            pltpu.VMEM((members, rows, width), f32),
            pltpu.VMEM((members, rows, width), f32),
            pltpu.VMEM(piece, bf16),
            pltpu.VMEM(piece, bf16),
            dma((12,)),
            dma((4,)),
            dma((3,)),
            dma((chunks, 2)),
            dma((chunks,)),
            dma((chunks,)),
            pltpu.SemaphoreType.REGULAR((1,)),
        ],
        compiler_params=pltpu.CompilerParams(
            collective_id=0, has_side_effects=True, vmem_limit_bytes=62 * 1024 * 1024
        ),
    )(
        query_rows, key_rows, value_rows, conv_taps, decay_rate.reshape(1, -1),
        lag_profile.reshape(1, -1), skip_gain.reshape(1, -1), pairs,
    )
    return held


def solution(mesh):
    rows = P(("group", "ctx"), None)
    return jax.shard_map(
        on_device,
        mesh=mesh,
        in_specs=(rows, rows, rows, P(), P(), P(), P(), P("group", None, None)),
        out_specs=rows,
        check_vma=False,
    )
```

```python
import functools

import jax
import jax.numpy as jnp
from jax import lax
from jax.experimental import pallas as pl
from jax.experimental.pallas import tpu as pltpu
from jax.sharding import PartitionSpec as P

MESH = pl.DeviceIdType.MESH
WIDTH = 128
STRAIGHT = 2
STRIPS = 8


def kernel(
    n, rows, chunks, width,
    q_hbm, k_hbm, v_hbm, taps_hbm, decay_hbm, lag_hbm, skip_hbm, pairs_hbm,
    out_ref, q_ref, k_ref, v_ref, taps_ref, decay_ref, lag_ref, skip_ref, pairs_ref,
    tail_ref, edge, rim_out, rim_in, rim, gated, qfeat, spans, inbox, outbox, toep, mix_here, mix_next,
    scaled, grow, fade, ahead, result, landed,
    load_sem, rim_sem, sent, recv1, recv_z, recv2, ready,
):
    me = lax.axis_index("ctx")
    members = n // 4
    quarter = me // members
    base = quarter * members
    mine = me - base
    pair = 2 * (mine // 2)
    long = members * rows
    share = chunks * width
    f32, bf16 = jnp.float32, jnp.bfloat16

    loads = [
        pltpu.make_async_copy(src, dst, load_sem.at[index])
        for index, (src, dst) in enumerate(
            (
                (k_hbm, k_ref), (v_hbm, v_ref), (taps_hbm, taps_ref), (q_hbm, q_ref),
                (lag_hbm, lag_ref), (pairs_hbm, pairs_ref), (decay_hbm, decay_ref),
                (skip_hbm, skip_ref),
            )
        )
    ]
    tails = [
        pltpu.make_async_copy(
            src.at[pl.ds(rows - 16, 16)], tail_ref.at[index], load_sem.at[9 + index]
        )
        for index, src in enumerate((k_hbm, v_hbm, q_hbm))
    ]
    for load in tails + loads:
        load.start()

    barrier = pltpu.get_barrier_semaphore()
    inner = quarter < 3
    linked = (quarter > 0) & (quarter < 3)
    first_of_later = (quarter > 0) & (mine == 0)
    last_of_earlier = (quarter < 3) & (mine == members - 1)

    def tell(sem, to):
        pl.semaphore_signal(sem, inc=1, device_id={"ctx": to}, device_id_type=MESH)

    def greet(k, c):
        tell(barrier, base + lax.rem(mine + k, members))
        return c

    lax.fori_loop(1, members, greet, 0)

    @pl.when(inner)
    def _():
        tell(barrier, me + members)

    @pl.when(first_of_later)
    def _():
        tell(barrier, me - 1)

    def build_toep(groups):
        wide = 4 * rows

        def build(g, c):
            upper = lag_ref[:, pl.ds(pl.multiple_of(g * wide, wide), wide)]
            below = jnp.maximum(4 * g - 1, 0)
            lower = lag_ref[:, pl.ds(pl.multiple_of(below * rows, rows), rows)]
            lower = jnp.where(g > 0, lower, 0.0)
            window = jnp.broadcast_to(
                jnp.concatenate([upper, lower], axis=1), (rows, wide + rows)
            )
            turned = pltpu.roll(window, 0, 1, stride=1, stride_axis=0)
            for e in range(4):
                toep[4 * g + e] = turned[:, e * rows : (e + 1) * rows].T.astype(bf16)
            return c

        lax.fori_loop(0, groups, build, 0)

    def border_of():
        listed = jnp.where(pairs_ref[:, 0, :] == 0, pairs_ref[:, 1, :], -1)
        return 1 + jnp.max(jnp.max(listed, axis=1, keepdims=True), axis=0, keepdims=True)

    def build_mix():
        border = border_of()
        early = jnp.where(border <= n // 2, 1.0, 0.0)
        raw = jnp.where(quarter == 1, 1.0, early)
        eye = jnp.where(
            lax.broadcasted_iota(jnp.int32, (rows, rows), 0)
            == lax.broadcasted_iota(jnp.int32, (rows, rows), 1),
            1.0, 0.0,
        ).astype(bf16)

        def live(source, target):
            a = jnp.where(border > source, 1.0, 0.0)
            b = jnp.where(border > target, 1.0, 0.0)
            return 1.0 - jnp.abs(a - b)

        def at(index):
            return pl.ds(pl.multiple_of(index * rows, rows), rows)

        def fill(i, carry):
            def one(j, carry):
                src, dst = base + j, base + i
                causal = jnp.where(j <= i, 1.0, 0.0)
                mix_here[at(i), at(members + j)] = (
                    toep[jnp.maximum(i - j, 0)] * (live(src, dst) * causal).astype(bf16)
                )

                @pl.when(linked)
                def _():
                    passed = (1.0 - raw) * jnp.where(i == j, 1.0, 0.0)
                    near = toep[members + i - j]
                    mix_here[at(i), at(j)] = (
                        near * (raw * live(src - members, dst)).astype(bf16)
                        + eye * passed.astype(bf16)
                    )
                    mix_next[at(i), at(members + j)] = (
                        near * live(src, dst + members).astype(bf16)
                    )
                    mix_next[at(i), at(j)] = (
                        toep[2 * members + i - j]
                        * (raw * live(src - members, dst + members)).astype(bf16)
                    )

                return carry

            return lax.fori_loop(0, members, one, carry)

        lax.fori_loop(0, members, fill, 0)

    def build_all():
        loads[4].wait()
        loads[5].wait()

        @pl.when(linked)
        def _():
            build_toep(3 * members // 4)

        @pl.when(~linked)
        def _():
            build_toep(members // 4)

        build_mix()

    def awaited():
        total = members - 1 + jnp.where(quarter > 0, 1, 0)
        return total + jnp.where(last_of_earlier, 1, 0)

    pl.semaphore_wait(barrier, awaited())

    @pl.when(quarter > 0)
    def _():
        tell(ready.at[0], me - members)

    def rim_copy(to, part):
        size = 4 * members if part == 0 else rim_out.shape[0] - 4 * members
        at = pl.ds(4 * members * part, size)
        return pltpu.make_async_remote_copy(
            src_ref=rim_out.at[at], dst_ref=rim_in.at[at], send_sem=rim_sem.at[part],
            recv_sem=rim_sem.at[2 + part], device_id={"ctx": to}, device_id_type=MESH,
        )

    def edges(index):
        tail = tail_ref[index].astype(f32)
        for p in range(members):
            for side in range(2):
                at = (2 * index + side) * members + p
                edge[at : at + 1, :] = tail[14 + side : 15 + side, p * share : (p + 1) * share]

    edge[4 * members :, :] = jnp.zeros((edge.shape[0] - 4 * members, share), f32)
    for index in range(2):
        tails[index].wait()
        edges(index)
    rim_out[: 4 * members, :] = edge[: 4 * members, :].astype(bf16)

    @pl.when(mine < members - 1)
    def _():
        rim_copy(me + 1, 0).start()

    tails[2].wait()
    edges(2)
    rim_out[4 * members :, :] = edge[4 * members :, :].astype(bf16)

    @pl.when(mine < members - 1)
    def _():
        rim_copy(me + 1, 1).start()

    @pl.when(last_of_earlier)
    def _():
        for part in range(2):
            rim_copy(me + 1, part).start()

    for index in range(3):
        loads[index].wait()

    def spread(first, last):
        size = max(16, (last - first) * members)
        held = rim_in[first * members : first * members + size, :].astype(f32)
        for at in range(first, last):
            for p in range(members):
                from_row = (at - first) * members + p
                rim[at : at + 1, p * share : (p + 1) * share] = held[from_row : from_row + 1, :]

    rim[...] = jnp.zeros_like(rim)

    def late_rim():
        @pl.when(me > 0)
        def _():
            rim_copy(me - 1, 1).wait_recv()
            spread(4, 6)

    row = lax.broadcasted_iota(jnp.int32, (rows, width), 0)

    def columns(c, p):
        return pl.ds(pl.multiple_of((p * chunks + c) * width, width), width)

    def feature(ref, index, c, p):
        cols = columns(c, p)
        tap = (index + 1) % 3
        x = ref[:, cols].astype(f32)
        two = rim[2 * index : 2 * index + 1, cols]
        one = rim[2 * index + 1 : 2 * index + 2, cols]
        x1 = jnp.where(row == 0, one, pltpu.roll(x, 1, 0))
        x2 = jnp.where(row == 0, two, jnp.where(row == 1, one, pltpu.roll(x, 2, 0)))
        return (
            taps_ref[tap, 0:1, cols] * x
            + taps_ref[tap, 1:2, cols] * x1
            + taps_ref[tap, 2:3, cols] * x2
        )

    def forward(c, p, sender):
        return pltpu.make_async_remote_copy(
            src_ref=gated.at[c, p], dst_ref=spans.at[c, sender],
            send_sem=sent.at[0], recv_sem=recv1.at[c, jnp.where(sender // 2 == p // 2, 1, 0)],
            device_id={"ctx": base + p}, device_id_type=MESH,
        )

    def backward(c, p, sender):
        return pltpu.make_async_remote_copy(
            src_ref=result.at[c, p], dst_ref=landed.at[c, sender],
            send_sem=sent.at[1], recv_sem=recv2.at[c],
            device_id={"ctx": base + p}, device_id_type=MESH,
        )

    others = pl.ds(0, members - 1)

    def arrived(c, count, mate):
        part = pl.ds(0, count)
        return pltpu.make_async_remote_copy(
            src_ref=gated.at[c, part], dst_ref=spans.at[c, part],
            send_sem=sent.at[0], recv_sem=recv1.at[c, mate],
            device_id={"ctx": base + lax.rem(mine + 1, members)}, device_id_type=MESH,
        )

    def all_backward(c):
        return pltpu.make_async_remote_copy(
            src_ref=result.at[c, others], dst_ref=landed.at[c, others],
            send_sem=sent.at[1], recv_sem=recv2.at[c],
            device_id={"ctx": base + lax.rem(mine + 1, members)}, device_id_type=MESH,
        )

    def raw_copy(c, j):
        return pltpu.make_async_remote_copy(
            src_ref=spans.at[c, j], dst_ref=inbox.at[c, j],
            send_sem=sent.at[2], recv_sem=recv_z.at[c],
            device_id={"ctx": lax.rem(me + members, n)}, device_id_type=MESH,
        )

    def box_copy(c):
        return pltpu.make_async_remote_copy(
            src_ref=outbox.at[c], dst_ref=inbox.at[c],
            send_sem=sent.at[2], recv_sem=recv_z.at[c],
            device_id={"ctx": lax.rem(me + members, n)}, device_id_type=MESH,
        )

    def part_copy(c, j):
        return pltpu.make_async_remote_copy(
            src_ref=outbox.at[c, j], dst_ref=inbox.at[c, mine],
            send_sem=sent.at[2], recv_sem=recv_z.at[c],
            device_id={"ctx": lax.rem(base + members + j, n)}, device_id_type=MESH,
        )

    def half_box(c, i):
        both = pl.ds(2 * i, 2)
        return pltpu.make_async_remote_copy(
            src_ref=outbox.at[c, both], dst_ref=inbox.at[c, both],
            send_sem=sent.at[2], recv_sem=recv_z.at[c],
            device_id={"ctx": lax.rem(me + members, n)}, device_id_type=MESH,
        )

    def gate_chunk(c):
        def gate(k, carry):
            p = lax.rem(pair + 2 + k, members)
            value = (feature(k_ref, 0, c, p) * feature(v_ref, 1, c, p)).astype(bf16)
            gated[c, p] = value

            @pl.when(p != mine)
            def _():
                forward(c, p, mine).start()

            @pl.when(p == mine)
            def _():
                spans[c, mine] = value

            return carry

        lax.fori_loop(0, members, gate, 0)

    def relay_chunk(c, whole):
        if whole:
            raw_copy(c, mine).start()
        arrived(c, 1, 1).wait_recv()
        raw_copy(c, 2 * pair + 1 - mine).start()
        arrived(c, members - 2, 0).wait_recv()

        def relay(k, carry):
            raw_copy(c, lax.rem(pair + k, members)).start()
            return carry

        lax.fori_loop(2, members, relay, 0)

    def rows_copy(p, first, count):
        part = pl.ds(first, count)
        return pltpu.make_async_remote_copy(
            src_ref=gated.at[0, p, part], dst_ref=spans.at[0, mine, part],
            send_sem=sent.at[0], recv_sem=recv1.at[0, jnp.where(mine // 2 == p // 2, 1, 0)],
            device_id={"ctx": base + p}, device_id_type=MESH,
        )

    def first_body(k, carry):
        p = lax.rem(pair + 2 + k, members)

        @pl.when(p != mine)
        def _():
            gated[0, p] = (feature(k_ref, 0, 0, p) * feature(v_ref, 1, 0, p)).astype(bf16)
            rows_copy(p, 16, rows - 16).start()

        return carry

    def first_head(k, carry):
        p = lax.rem(pair + 2 + k, members)
        value = (feature(k_ref, 0, 0, p) * feature(v_ref, 1, 0, p)).astype(bf16)

        @pl.when(p != mine)
        def _():
            gated[0, p, 0:16, :] = value[:16]
            rows_copy(p, 0, 16).start()

        @pl.when(p == mine)
        def _():
            gated[0, mine] = value
            spans[0, mine] = value

        return carry

    lax.fori_loop(0, members, first_body, 0)

    @pl.when(me > 0)
    def _():
        rim_copy(me - 1, 0).wait_recv()
        spread(0, 4)

    lax.fori_loop(0, members, first_head, 0)

    @pl.when(quarter == 0)
    def _():
        pl.semaphore_wait(ready.at[0], 1)

    @pl.when(quarter == 0)
    def _():
        raw_copy(0, mine).start()

    gate_chunk(1)

    @pl.when(quarter == 0)
    def _():
        relay_chunk(0, False)

    def lead(c, carry):
        gate_chunk(c)
        return carry

    front = jnp.where(quarter == 0, 4, jnp.where(quarter == 1, 2, jnp.where(quarter == 2, 4, chunks)))
    front = jnp.minimum(front, chunks)

    @pl.when(quarter == 0)
    def _():
        lax.fori_loop(2, front, lead, 0)

    build_all()

    @pl.when(quarter > 0)
    def _():
        lax.fori_loop(2, front, lead, 0)

    @pl.when(linked)
    def _():
        pl.semaphore_wait(ready.at[0], 1)

    late_rim()
    loads[3].wait()
    loads[6].wait()
    loads[7].wait()
    border = border_of()
    early_all = border <= n // 2
    take_raw = early_all & (quarter == 1)
    is_raw = (quarter == 1) | (early_all & (quarter == 2))
    place = lax.broadcasted_iota(jnp.int32, (rows, width), 0).astype(f32)
    tile = 2 * rows

    def finish_chunk(c):
        all_backward(c).wait_recv()

        def finish(p, carry, last=False):
            cols = columns(c, p)
            total = landed[c, p].astype(f32) + skip_ref[:, cols] * gated[c, p].astype(f32)
            if last:
                total = total + inbox[c, p].astype(f32)
            out_ref[:, cols] = (qfeat[c, p] * total).astype(bf16)
            return carry

        late = (quarter == 3) & (c >= chunks - STRAIGHT)

        @pl.when(~late)
        def _():
            lax.fori_loop(0, members, finish, 0)

        @pl.when(late)
        def _():
            box_copy(c).wait_recv()
            lax.fori_loop(0, members, functools.partial(finish, last=True), 0)

    def at(index, size):
        return pl.ds(pl.multiple_of(index * size, size), size)

    lag = jnp.where(quarter == 0, chunks, jnp.where(quarter == 1, 4, jnp.where(quarter == 2, 3, 2)))

    skip = jnp.where(quarter == 3, STRAIGHT, 0)

    def step(u, carry):
        c = jnp.where(quarter == 3, lax.rem(u + chunks - STRAIGHT, chunks), u)
        straight = c >= chunks - STRAIGHT
        @pl.when((quarter == 0) & (c + 1 < chunks))
        def _():
            relay_chunk(c + 1, True)

        @pl.when(c + front < chunks)
        def _():
            gate_chunk(c + front)

        rate = decay_ref[:, columns(c, mine)]
        far = jnp.exp(-rate * long)

        def query(p, carry):
            qfeat[c, p] = feature(q_ref, 2, c, p)
            return carry

        lax.fori_loop(0, members, query, 0)

        @pl.when(quarter > 0)
        def _():
            arrived(c, 1, 1).wait_recv()
            arrived(c, members - 2, 0).wait_recv()

        def prepare(j, carry):
            spot = place + (j * rows).astype(f32)
            rise = jnp.exp(rate * spot)
            grow[j] = rise
            fade[j] = jnp.exp(-rate * spot)
            scaled[at(members + j, rows), :] = (spans[c, j].astype(f32) * rise).astype(bf16)
            return carry

        lax.fori_loop(0, members, prepare, 0)

        @pl.when(u - lag >= skip)
        def _():
            finish_chunk(u - lag - skip)

        def own_part(i):
            return jnp.dot(
                mix_here[at(i, tile), long:], scaled[long:, :], preferred_element_type=f32
            )

        @pl.when(linked)
        def _():
            def before(i, carry):
                acc = jnp.dot(
                    mix_next[at(i, tile), long:], scaled[long:, :], preferred_element_type=f32
                )
                for side in range(2):
                    ahead[2 * i + side] = acc[side * rows : (side + 1) * rows]
                return carry

            for i in range(members // 2):
                before(i, 0)
            box_copy(c).wait_recv()
            drop = jnp.where(is_raw, far, 1.0)

            def receive(j, carry):
                scaled[at(j, rows), :] = (
                    inbox[c, j].astype(f32) * (grow[j] * drop)
                ).astype(bf16)
                return carry

            lax.fori_loop(0, members, receive, 0)

        @pl.when(linked)
        def _():
            def send(i, carry):
                acc = jnp.dot(
                    mix_next[at(i, tile), :long], scaled[:long, :], preferred_element_type=f32
                )
                for side in range(2):
                    j = 2 * i + side
                    value = (ahead[j] + acc[side * rows : (side + 1) * rows]) * (fade[j] * far)
                    raw = spans[c, j].astype(f32)
                    outbox[c, j] = jnp.where(take_raw, raw, value).astype(bf16)

                @pl.when((quarter == 1) | ~straight)
                def _():
                    half_box(c, i).start()

                @pl.when((quarter == 2) & straight)
                def _():
                    for side in range(2):
                        part_copy(c, 2 * i + side).start()

                return carry

            for k in range(members // 2):
                send(lax.rem(mine // 2 + 1 + k, members // 2), 0)

        def publish(reader, value):
            value = value.astype(bf16)
            result[c, reader] = value

            @pl.when(reader != mine)
            def _():
                backward(c, reader, mine).start()

            @pl.when(reader == mine)
            def _():
                landed[c, mine] = value

        def publish_both(i, acc):
            for side in range(2):
                reader = 2 * i + side
                publish(reader, acc[side * rows : (side + 1) * rows] * fade[reader])

        @pl.when((quarter == 3) & ~straight)
        def _():
            for i in range(members // 2):
                acc = own_part(i)
                for side in range(2):
                    j = 2 * i + side
                    grow[j] = acc[side * rows : (side + 1) * rows] * fade[j]
            box_copy(c).wait_recv()

            def target(k, carry):
                reader = lax.rem(pair + 2 + k, members)
                publish(reader, grow[reader] + inbox[c, reader].astype(f32))
                return carry

            lax.fori_loop(0, members, target, 0)

        @pl.when((quarter == 0) | ((quarter == 3) & straight))
        def _():
            def target(i, carry):
                publish_both(i, own_part(i))
                return carry

            for k in range(members // 2):
                target(lax.rem(mine // 2 + 1 + k, members // 2), 0)

        @pl.when(linked)
        def _():
            def target(i, carry):
                publish_both(i, jnp.dot(
                    mix_here[at(i, tile), :], scaled[...], preferred_element_type=f32
                ))
                return carry

            for k in range(members // 2):
                target(lax.rem(mine // 2 + 1 + k, members // 2), 0)

        return carry

    lax.fori_loop(0, chunks, step, 0)

    def tail(c, carry):
        finish_chunk(c)
        return carry

    lax.fori_loop(chunks - lag - skip, chunks - skip, tail, 0)

    @pl.when(quarter == 3)
    def _():
        lax.fori_loop(chunks - STRAIGHT, chunks, tail, 0)

    def everything(src, dst, index, count):
        part = pl.ds(0, count)
        return pltpu.make_async_remote_copy(
            src_ref=src.at[:, part], dst_ref=dst.at[:, part],
            send_sem=sent.at[index], recv_sem=recv1.at[0, 0],
            device_id={"ctx": base + lax.rem(mine + 1, members)}, device_id_type=MESH,
        )

    everything(gated, spans, 0, members - 1).wait_send()
    everything(result, landed, 1, members - 1).wait_send()

    @pl.when(inner)
    def _():
        everything(spans, inbox, 2, members).wait_send()

    @pl.when(me < n - 1)
    def _():
        for part in range(2):
            rim_copy(me + 1, part).wait_send()


def hand_over(src_ref, dst_ref, sem):
    copy = pltpu.make_async_copy(src_ref, dst_ref, sem.at[0])
    copy.start()
    copy.wait()


def on_device(
    query_rows, key_rows, value_rows, conv_taps, decay_rate, lag_profile, skip_gain, pair_lists
):
    rows, channels = query_rows.shape
    n = lax.axis_size("ctx")
    members = n // 4
    share = channels // members
    width = WIDTH
    chunks = share // width
    long = members * rows
    pairs = pair_lists.transpose(1, 2, 0)
    hbm = pl.BlockSpec(memory_space=pltpu.HBM)
    bf16, f32 = jnp.bfloat16, jnp.float32
    piece = (chunks, members, rows, width)
    edges = 4 * members + max(16, 2 * members)
    dma = pltpu.SemaphoreType.DMA
    held = pl.pallas_call(
        functools.partial(kernel, n, rows, chunks, width),
        out_shape=pltpu.VMEM((rows, channels), bf16),
        in_specs=[hbm] * 8,
        out_specs=pl.BlockSpec(memory_space=pltpu.VMEM),
        scratch_shapes=[
            pltpu.VMEM((rows, channels), bf16),
            pltpu.VMEM((rows, channels), bf16),
            pltpu.VMEM((rows, channels), bf16),
            pltpu.VMEM(conv_taps.shape, f32),
            pltpu.VMEM((1, channels), f32),
            pltpu.VMEM((1, lag_profile.shape[0]), f32),
            pltpu.VMEM((1, channels), f32),
            pltpu.VMEM(pairs.shape, jnp.int32),
            pltpu.VMEM((3, 16, channels), bf16),
            pltpu.VMEM((edges, share), f32),
            pltpu.VMEM((edges, share), bf16),
            pltpu.VMEM((edges, share), bf16),
            pltpu.VMEM((8, channels), f32),
            pltpu.VMEM(piece, bf16),
            pltpu.VMEM(piece, f32),
            pltpu.VMEM(piece, bf16),
            pltpu.VMEM(piece, bf16),
            pltpu.VMEM(piece, bf16),
            pltpu.VMEM((3 * members, rows, rows), bf16),
            pltpu.VMEM((long, 2 * long), bf16),
            pltpu.VMEM((long, 2 * long), bf16),
            pltpu.VMEM((2 * long, width), bf16),
            pltpu.VMEM((members, rows, width), f32),
            pltpu.VMEM((members, rows, width), f32),
            pltpu.VMEM((members, rows, width), f32),
            pltpu.VMEM(piece, bf16),
            pltpu.VMEM(piece, bf16),
            dma((12,)),
            dma((4,)),
            dma((3,)),
            dma((chunks, 2)),
            dma((chunks,)),
            dma((chunks,)),
            pltpu.SemaphoreType.REGULAR((1,)),
        ],
        compiler_params=pltpu.CompilerParams(
            collective_id=0, has_side_effects=True, vmem_limit_bytes=62 * 1024 * 1024
        ),
    )(
        query_rows, key_rows, value_rows, conv_taps, decay_rate.reshape(1, -1),
        lag_profile.reshape(1, -1), skip_gain.reshape(1, -1), pairs,
    )
    return pl.pallas_call(
        hand_over,
        out_shape=jax.ShapeDtypeStruct((rows, channels), bf16),
        in_specs=[pl.BlockSpec(memory_space=pltpu.VMEM)],
        out_specs=hbm,
        scratch_shapes=[dma((1,))],
        compiler_params=pltpu.CompilerParams(vmem_limit_bytes=1024 * 1024),
    )(held)


def solution(mesh):
    rows = P(("group", "ctx"), None)
    return jax.shard_map(
        on_device,
        mesh=mesh,
        in_specs=(rows, rows, rows, P(), P(), P(), P(), P("group", None, None)),
        out_specs=rows,
        check_vma=False,
    )
```
